32 devices in a mesh: groups: 2 (over y), atoms: 8 (over z, x), samples: 2 (over core).
Axes of the slice: x: 2, y: 2, z: 4, core: 2. Of those that a mesh axis runs over, the one named last changes fastest.
Arguments:
- act: bfloat16 [16, 10240, 128], P('samples', ('groups', 'atoms')), parts along dimension 1, may hold values from -6 to 6
- grad_out: bfloat16 [16, 10240, 128], P('samples', ('groups', 'atoms')), parts along dimension 1, may hold values from -6 to 6
- pair: bfloat16 [320, 32, 16, 128], P(('groups', 'atoms')), parts along dimension 0, may hold values from -500 to 500
- w_query: bfloat16 [128, 128], replicated, may hold values from -0.5 to 0.5
- w_key: bfloat16 [128, 128], replicated, may hold values from -0.5 to 0.5
- w_value: bfloat16 [128, 128], replicated, may hold values from -0.5 to 0.5
- w_gate: bfloat16 [128, 128], replicated, may hold values from -0.5 to 0.5
- w_out: bfloat16 [128, 128], replicated, may hold values from -0.5 to 0.5
- w_pair: bfloat16 [16, 4], replicated, may hold values from -1.5 to 1.5
- w_token: float32 [4], replicated, may hold values from -2 to 2
- offsets: int32 [320], P(('groups', 'atoms')), parts along dimension 0, may hold values from -128 to 32, as said below
- atom_token: int32 [10240], P(('groups', 'atoms')), parts along dimension 0, may hold values from 0 to 639, never falling along the last dimension, each value on 1 to 24 neighbouring positions
- padding: int32 [16], P(('groups', 'atoms')), parts along dimension 0, may hold values from 0 to 64, as said below
Outputs:
- grad_act: bfloat16 [16, 10240, 128], P('samples', ('groups', 'atoms')), parts along dimension 1
- grad_pair: bfloat16 [320, 32, 16, 128], P(('groups', 'atoms'), 'samples'), parts along dimension 0
- grad_weights: float32 [10, 128, 128], P('groups'), parts along dimension 0
- grad_pair_weight: float32 [32, 4], P('groups'), parts along dimension 0
- grad_token_weight: float32 [8], P('groups'), parts along dimension 0
The draws below stay inside these ranges and needn't reach their ends.
There are 2 independent parts, one for each index of `groups`. The reference program is written for one: setup_inputs(seed, part) draws one part's arguments, and reference() takes and returns one part's arrays. A program takes and returns all parts, laid end to end along the dimension named above; an argument that names none is the same for every part. Nothing has to cross between parts.
Inputs may be any that keep to these rules, and one draw needn't show every extreme that they name: Window w reads the 128 atoms that begin at 32 * w + offsets[w], moved into the complex. padding[r] atoms at the end of atom range r are padding. `atom_token`: the atoms of one token are contiguous, at most 24 of them.
All inputs are finite; a program needn't handle non-finite values.
Results may differ from the reference program's by a relative error of at most 0.025.
Values may be sent and summed in bfloat16 or wider, within the bound.
A program may use at most 128 MiB of HBM per device.

```python
import math
import jax
import jax.numpy as jnp
import numpy as np
from jax import lax

C = 128
HEADS = 4
CP = 16
WQ = 32
WK = 128
ATOM_DEV = 640
NATOMS = 5120
SAMPLES = 16
NWIN = 160
NTOK = 640
RANGES = 8
PAD_MOST = 64


def draw_pair(key, part):
    full_shape = (NWIN, WQ, CP, WK)
    key_one = jax.random.fold_in(key, 0)
    return jnp.clip(jax.random.normal(key_one, full_shape, jnp.float32), -6.0, 6.0).astype(jnp.bfloat16)


def draw_offsets(key, part):
    values = jax.random.randint(key, (NWIN,), -WK, WQ + 1, dtype=jnp.int32)
    middle = NWIN // 2
    return values.at[middle].set(-WK).at[middle + 1].set(WQ)


def draw_padding(key, part):
    values = jax.random.randint(key, (RANGES,), 0, PAD_MOST + 1, dtype=jnp.int32)
    return values.at[0].set(PAD_MOST).at[RANGES - 1].set(0)


def level_of(key, shape, shards, low, high):
    def one(axis_at, shards_of):
        heights = jax.random.uniform(jax.random.fold_in(jax.random.fold_in(key, 6), axis_at), (shards_of,), jnp.float32, low / len(shards), high / len(shards))
        return jnp.repeat(jnp.exp(heights), shape[axis_at] // shards_of).reshape((-1,) + (1,) * (len(shape) - axis_at - 1))

    level = one(*shards[0])
    for cut in shards[1:]:
        level = level * one(*cut)
    return level


def profile(number_of, total, limit, slope):
    portions = [(1 << 20) // math.isqrt(rank ** slope) + 1 for rank in range(2, number_of + 1)]
    surplus, counts = total - limit - (number_of - 1), [1] * (number_of - 1)
    while surplus > 0:
        movable = [i for i in range(number_of - 1) if counts[i] < limit]
        whole, remaining = sum([portions[i] for i in movable]), surplus
        for i in movable:
            addition = min(limit - counts[i], max(1, remaining * portions[i] // whole), surplus)
            counts[i] = counts[i] + addition
            surplus = surplus - addition
    return np.array([limit] + counts)


def uneven(key, number_of, total, most, skew):
    if number_of == 2:
        one = jax.random.randint(key, (), max(1, total - most), min(most, total - 1) + 1)
        return jnp.stack([one, total - one])
    tallies = jnp.asarray(profile(number_of, total, most, skew), jnp.int32)
    pairs = (number_of - 1) // 2
    donor, receiver = tallies[1:1 + 2 * pairs:2], tallies[2:2 + 2 * pairs:2]
    slack = jnp.minimum(donor - 1, most - receiver)
    passed = jax.random.randint(jax.random.fold_in(key, 1), (pairs,), 0, 1 << 20) % (slack + 1)
    tallies = tallies.at[1:1 + 2 * pairs:2].set(donor - passed).at[2:2 + 2 * pairs:2].set(receiver + passed)
    return tallies[jax.random.permutation(jax.random.fold_in(key, 2), number_of)]


def normal_values(key, extent, scale, limit, cuts=(), kind=jnp.bfloat16):
    result = jax.random.normal(key, extent, jnp.float32) * scale
    if len(cuts) > 0:
        result = level_of(key, extent, cuts, -0.22, 0.18) * result
    return jnp.clip(result, min=-limit, max=limit).astype(kind)


def setup_inputs(seed: int = 0, part: int = 0) -> dict:
    arg_keys = jax.random.split(jax.random.key(seed), 14)
    part_keys = jax.random.split(jax.random.fold_in(arg_keys[13], part), 14)
    act = normal_values(part_keys[0], (SAMPLES, NATOMS, C), 1.0, 6.0, ((0, 2), (1, 8)))
    grad_out = normal_values(part_keys[1], (SAMPLES, NATOMS, C), 1.0, 6.0, ((0, 2), (1, 8)))
    pair = draw_pair(jax.random.fold_in(jax.random.fold_in(arg_keys[13], part), 71), part)
    w_query = normal_values(arg_keys[3], (C, C), C ** -0.5, 0.5)
    w_key = normal_values(arg_keys[4], (C, C), C ** -0.5, 0.5)
    w_value = normal_values(arg_keys[5], (C, C), C ** -0.5, 0.5)
    w_gate = normal_values(arg_keys[6], (C, C), C ** -0.5, 0.5)
    w_out = normal_values(arg_keys[7], (C, C), C ** -0.5, 0.5)
    w_pair = normal_values(arg_keys[8], (CP, HEADS), CP ** -0.5, 1.5)
    w_token = jnp.clip(jax.random.uniform(arg_keys[9], (HEADS,), jnp.float32, -2.0, 2.0), -2.0, 2.0)
    offsets = draw_offsets(jax.random.fold_in(jax.random.fold_in(arg_keys[13], part), 71), part)
    atom_token = jnp.searchsorted(jnp.cumsum(uneven(part_keys[11], NTOK, NATOMS, 24, 2)), jnp.arange(NATOMS), side="right").astype(jnp.int32)
    padding = draw_padding(jax.random.fold_in(jax.random.fold_in(arg_keys[13], part), 71), part)
    return {"act": act, "grad_out": grad_out, "pair": pair, "w_query": w_query, "w_key": w_key, "w_value": w_value, "w_gate": w_gate, "w_out": w_out, "w_pair": w_pair, "w_token": w_token, "offsets": offsets, "atom_token": atom_token, "padding": padding}


MASKED = -1000000000.0

def float_einsum(pattern, left_op, right_op):
    return jnp.einsum(pattern, left_op.astype(jnp.float32), right_op.astype(jnp.float32), precision=lax.Precision.HIGHEST)

def window_layout(offsets, atom_token, padding):
    position = jnp.arange(NATOMS, dtype=jnp.int32)
    ranges = (position // ATOM_DEV).astype(jnp.int32)
    is_live = position % ATOM_DEV < ATOM_DEV - padding[ranges]
    starts = jnp.clip(WQ * jnp.arange(NWIN, dtype=jnp.int32) + offsets, 0, NATOMS - WK).astype(jnp.int32)
    key_rows = (starts[:, None] + jnp.arange(WK, dtype=jnp.int32)[None, :]).astype(jnp.int32)
    key_live = is_live[key_rows]
    same_token = atom_token.reshape(NWIN, WQ)[:, :, None] == atom_token[key_rows][:, None, :]
    return (key_rows, key_live, same_token)

def attend(query, keys, values, gate_logit, grad_y, pair_bias, key_live):
    windows = keys.shape[0]
    head_count = pair_bias.shape[1]
    channels = query.shape[-1]
    head_dim = channels // head_count
    score_scale = 1.0 / math.sqrt(head_dim)
    query_heads = query.reshape(windows, -1, head_count, head_dim)
    key_heads = keys.reshape(windows, -1, head_count, head_dim)
    value_heads = values.reshape(windows, -1, head_count, head_dim)
    scores = float_einsum('wihd,wjhd->whij', query_heads, key_heads) * score_scale + pair_bias
    scores = jnp.where(key_live[:, None, None, :], scores, MASKED)
    row_max = lax.optimization_barrier(jnp.max(scores, axis=-1, keepdims=True))
    exponent = jnp.exp(scores - row_max)
    attn_probs = exponent / lax.optimization_barrier(jnp.sum(exponent, axis=-1, keepdims=True))
    probs_b = attn_probs.astype(jnp.bfloat16)
    attended = float_einsum('whij,wjhd->wihd', probs_b, value_heads).reshape(query.shape)
    gate_value = jax.nn.sigmoid(gate_logit)
    gated = (gate_value * attended).astype(jnp.bfloat16)
    d_attended = (grad_y * gate_value).astype(jnp.bfloat16)
    d_gate = (grad_y * attended * gate_value * (1.0 - gate_value)).astype(jnp.bfloat16)
    attended_heads = d_attended.reshape(windows, -1, head_count, head_dim)
    d_probs = float_einsum('wihd,wjhd->whij', attended_heads, value_heads)
    d_scores = attn_probs * (d_probs - lax.optimization_barrier(jnp.sum(attn_probs * d_probs, axis=-1, keepdims=True)))
    ds_b = d_scores.astype(jnp.bfloat16)
    d_query = (float_einsum('whij,wjhd->wihd', ds_b, key_heads) * score_scale).astype(jnp.bfloat16).reshape(query.shape)
    d_keys = float_einsum('whij,wihd->wjhd', ds_b, query_heads) * score_scale
    d_values = float_einsum('whij,wihd->wjhd', probs_b, attended_heads)
    return (gated, d_query, d_gate, d_keys, d_values, d_scores)

def reference(act, grad_out, pair, w_query, w_key, w_value, w_gate, w_out, w_pair, w_token, offsets, atom_token, padding):
    key_rows, key_live, same_token = window_layout(offsets, atom_token, padding)
    same_float = same_token.astype(jnp.float32)
    pair_bias = float_einsum('wicj,ch->whij', pair, w_pair) + w_token[None, :, None, None] * same_float[:, None, :, :]
    projection = jnp.concatenate([w_query, w_key, w_value, w_gate], axis=1)

    def one_sample(running, inputs):
        bias_sum, weight_sum, out_sum = running
        sample_act, sample_grad = inputs
        mixed = jnp.dot(sample_act, projection, preferred_element_type=jnp.float32)
        query = mixed[:, :C].astype(jnp.bfloat16)
        keys = mixed[:, C:2 * C].astype(jnp.bfloat16)
        values = mixed[:, 2 * C:3 * C].astype(jnp.bfloat16)
        gate_logit = mixed[:, 3 * C:]
        grad_y = jnp.dot(sample_grad, w_out.T, preferred_element_type=jnp.float32)
        gated, d_query, d_gate, d_keys, d_values, d_scores = attend(query, keys[key_rows], values[key_rows], gate_logit, grad_y, pair_bias, key_live)
        key_grad = jnp.zeros((NATOMS, C), jnp.float32).at[key_rows].add(d_keys.reshape(NWIN, WK, C))
        value_grad = jnp.zeros((NATOMS, C), jnp.float32).at[key_rows].add(d_values.reshape(NWIN, WK, C))
        stacked = jnp.concatenate([d_query, key_grad.astype(jnp.bfloat16), value_grad.astype(jnp.bfloat16), d_gate], axis=1)
        grad_act = jnp.dot(stacked, projection.T, preferred_element_type=jnp.float32).astype(jnp.bfloat16)
        weight_sum = weight_sum + jnp.dot(sample_act.T, stacked, preferred_element_type=jnp.float32)
        out_sum = out_sum + jnp.dot(gated.T, sample_grad, preferred_element_type=jnp.float32)
        return ((bias_sum + d_scores, weight_sum, out_sum), grad_act)
    start_state = (jnp.zeros((NWIN, HEADS, WQ, WK), jnp.float32), jnp.zeros((C, 4 * C), jnp.float32), jnp.zeros((C, C), jnp.float32))
    (bias_total, weight_sum, out_sum), grad_act = lax.scan(one_sample, start_state, (act, grad_out))
    grad_pair = float_einsum('whij,ch->wicj', bias_total, w_pair).astype(jnp.bfloat16)
    grad_weights = jnp.concatenate([weight_sum.reshape(C, 4, C).transpose(1, 0, 2), out_sum[None]], axis=0)
    grad_pair_weight = float_einsum('wicj,whij->ch', pair, bias_total)
    grad_token_weight = lax.optimization_barrier(jnp.sum(bias_total * same_float[:, None, :, :], axis=(0, 2, 3)))
    return (grad_act, grad_pair, grad_weights, grad_pair_weight, grad_token_weight)
```

```python
import math

import jax
import jax.numpy as jnp
from jax import lax
from jax.experimental import pallas as pl
from jax.experimental.pallas import tpu as pltpu
from jax.sharding import PartitionSpec as P

MASKED = -1000000000.0
BF16 = jnp.bfloat16
F32 = jnp.float32
LOG2E = math.log2(math.e)
TOGETHER = 4
PAD = 32


def nn(a, b):
    return lax.dot_general(a, b, (((1,), (0,)), ((), ())), preferred_element_type=F32)


def nt(a, b):
    return lax.dot_general(a, b, (((1,), (1,)), ((), ())), preferred_element_type=F32)


def tn(a, b):
    return lax.dot_general(a, b, (((0,), (0,)), ((), ())), preferred_element_type=F32)


def greet(barrier, devices):
    for device in devices:
        pl.semaphore_signal(
            barrier, inc=1, device_id=device, device_id_type=pl.DeviceIdType.MESH
        )


def remote(src, dst, sems, slot, device):
    return pltpu.make_async_remote_copy(
        src_ref=src,
        dst_ref=dst,
        send_sem=sems.at[0, slot],
        recv_sem=sems.at[1, slot],
        device_id=device,
        device_id_type=pl.DeviceIdType.MESH,
    )


def fused_kernel(
    ranges,
    offsets_ref,
    wtoken_ref,
    padding_ref,
    act_hbm,
    grad_hbm,
    pair_hbm,
    token_ref,
    wq_ref,
    wk_ref,
    wv_ref,
    wg_ref,
    wo_ref,
    wpair_ref,
    ga_hbm,
    pair_out_hbm,
    total_ref,
    act_ref,
    grad_ref,
    pair_ref,
    before_ref,
    after_ref,
    code_scr,
    code_before,
    code_after,
    k_scr,
    v_scr,
    q_scr,
    da_scr,
    gate_scr,
    gyg_scr,
    dqg_scr,
    gated_scr,
    dk_scr,
    dv_scr,
    pw_scr,
    tok_scr,
    wpair_scr,
    key_code_scr,
    query_code_scr,
    mine_ref,
    theirs_ref,
    got,
    to_lower_ref,
    to_upper_ref,
    from_lower,
    from_upper,
    sums_ref,
    got_half,
    part,
    slots,
    starts_ref,
    load_sems,
    store_sems,
    halo_sems,
    edge_sems,
    core_sems,
    scatter_sems,
    gather_sems,
):
    me = lax.axis_index("atoms")
    core = lax.axis_index("samples")
    other = 1 - core
    samples, atoms, channels = act_ref.shape
    windows = pair_ref.shape[0]
    rows = atoms // windows
    span = before_ref.shape[1]
    wide = atoms + 2 * span
    pair_channels = wpair_ref.shape[1]
    heads = wpair_ref.shape[0]
    head_dim = channels // heads
    scale = 1.0 / math.sqrt(head_dim)
    stack = heads * rows
    half_rows = rows // 2
    chunk = part.shape[1]
    half = ranges * chunk
    has_lower, has_upper = me > 0, me < ranges - 1
    lower, upper, peer = {"atoms": me - 1}, {"atoms": me + 1}, {"samples": other}
    everyone = [{"atoms": lax.rem(me + d, ranges)} for d in range(1, ranges)]

    barrier = pltpu.get_barrier_semaphore()
    greet(barrier, [peer] + everyone)
    load_act = pltpu.make_async_copy(act_hbm, act_ref, load_sems.at[0])
    load_grad = pltpu.make_async_copy(grad_hbm, grad_ref, load_sems.at[1])
    load_pair = pltpu.make_async_copy(pair_hbm, pair_ref, load_sems.at[2])
    load_act.start()
    load_grad.start()
    load_pair.start()

    code_rows = atoms // span
    live_end = atoms - padding_ref[0]
    lane_at = lax.broadcasted_iota(jnp.int32, (1, span), 1)
    for r in range(code_rows):
        code_scr[r] = jnp.where(lane_at + r * span < live_end, token_ref[r : r + 1, :] + 1, 0)

    pl.semaphore_wait(barrier, ranges)
    halo_up = [
        remote(act_hbm.at[:, pl.ds(atoms - span, span)], before_ref, halo_sems, 0, upper),
        remote(code_scr.at[code_rows - 1], code_before, halo_sems, 1, upper),
    ]
    halo_down = [
        remote(act_hbm.at[:, pl.ds(0, span)], after_ref, halo_sems, 2, lower),
        remote(code_scr.at[0], code_after, halo_sems, 3, lower),
    ]

    @pl.when(has_upper)
    def _():
        for copy in halo_up:
            copy.start()

    @pl.when(has_lower)
    def _():
        for copy in halo_down:
            copy.start()

    @pl.when(jnp.logical_not(has_lower))
    def _():
        before_ref[...] = jnp.zeros_like(before_ref)
        code_before[...] = jnp.zeros_like(code_before)

    @pl.when(jnp.logical_not(has_upper))
    def _():
        after_ref[...] = jnp.zeros_like(after_ref)
        code_after[...] = jnp.zeros_like(code_after)

    def code_column(first, row):
        column = jnp.broadcast_to(row.astype(F32), (stack, span)).T
        key_code_scr[first : first + span, :] = column

    lane_row = lax.broadcasted_iota(jnp.int32, (pair_channels, stack), 1) % rows
    lane_head = lax.broadcasted_iota(jnp.int32, (pair_channels, stack), 1) // rows
    wpair_values = wpair_ref[...].astype(F32).T
    wpair_rows = jnp.zeros((pair_channels, stack), F32)
    wtoken_row = jnp.zeros((1, stack), F32)
    for h in range(heads):
        wpair_rows = jnp.where(lane_head == h, wpair_values[:, h : h + 1], wpair_rows)
        wtoken_row = jnp.where(lane_head[0:1] == h, wtoken_ref[h], wtoken_row)
    for i in range(rows):
        wpair_scr[i * pair_channels : (i + 1) * pair_channels, :] = jnp.where(
            lane_row == i, wpair_rows, 0.0
        ).astype(BF16)
    for r in range(code_rows):
        code_column(span + r * span, code_scr[r])
        tokens = (token_ref[r : r + 1, :] + 1).astype(F32)
        for u in range(span // rows):
            piece = tokens[:, u * rows : (u + 1) * rows]
            query_code_scr[r * (span // rows) + u] = jnp.concatenate([piece] * heads, axis=1)
    pw_scr[...] = jnp.zeros_like(pw_scr)
    tok_scr[...] = jnp.zeros_like(tok_scr)
    sums_ref[...] = jnp.zeros_like(sums_ref)
    anchor = me * atoms
    last_start = ranges * atoms - span
    for w in range(windows):
        starts_ref[w] = (
            jnp.clip(anchor + w * rows + offsets_ref[w], 0, last_start) - anchor + span
        )

    load_act.wait()
    load_grad.wait()
    slot = span + PAD

    def project(s, carry):
        own = act_ref[s]
        q_scr[s] = (nn(own, wq_ref[...]) * (scale * LOG2E)).astype(BF16)
        gate = jax.nn.sigmoid(nn(own, wg_ref[...]))
        gated_gy = nt(grad_ref[s], wo_ref[...]) * gate
        gate_scr[s] = gate
        da_scr[s] = gated_gy.astype(BF16)
        gyg_scr[s] = gated_gy * (1.0 - gate)
        k_scr[s, span : span + atoms, :] = nn(own, wk_ref[...]).astype(BF16).astype(F32)
        v_scr[s, span : span + atoms, :] = nn(own, wv_ref[...]).astype(BF16).astype(F32)
        blank = jnp.zeros((PAD, channels), F32)
        for w in range(windows + 1):
            dk_scr[s, w * slot : w * slot + PAD, :] = blank
            dv_scr[s, w * slot : w * slot + PAD, :] = blank
        return carry

    lax.fori_loop(0, samples, project, 0)
    load_pair.wait()

    row_head = lax.broadcasted_iota(jnp.int32, (stack, channels), 0) // rows
    column_head = lax.broadcasted_iota(jnp.int32, (stack, channels), 1) // head_dim
    head_mask = jnp.where(row_head == column_head, 1.0, 0.0).astype(BF16)
    lane = lax.broadcasted_iota(jnp.int32, (rows, channels), 1) // head_dim
    head_is = [lane == h for h in range(heads)]
    first_mine = core == 0

    def spread(x):
        return jnp.concatenate([x] * heads, axis=0) * head_mask

    def collect(x):
        out = x[0:rows]
        for h in range(1, heads):
            out = jnp.where(head_is[h], x[h * rows : (h + 1) * rows], out)
        return out

    def attend(block):
        ws = [block * TOGETHER + u for u in range(TOGETHER)]
        mine_rows = [pl.ds(pl.multiple_of(w * rows, rows), rows) for w in ws]
        key_rows = [pl.ds(starts_ref[w], span) for w in ws]
        slot_rows = [pl.ds(pl.multiple_of(w * slot + PAD, 8), span) for w in ws]
        sames, biases = [], []
        for u, w in enumerate(ws):
            key_code = key_code_scr[key_rows[u], :]
            same = key_code == query_code_scr[w]
            bias = (tn(pair_ref[w], wpair_scr[...]) + jnp.where(same, wtoken_row, 0.0)) * LOG2E
            biases.append(jnp.where(key_code > 0.0, bias, MASKED))
            sames.append(same)
        units = [(u, s) for u in range(TOGETHER) for s in range(samples)]
        keys = [k_scr[s, key_rows[u], :].astype(BF16) for u, s in units]
        values = [v_scr[s, key_rows[u], :].astype(BF16) for u, s in units]
        qm = [spread(q_scr[s, mine_rows[u], :]) for u, s in units]
        dam = [spread(da_scr[s, mine_rows[u], :]) for u, s in units]
        scores = [nt(k, q) + biases[u] for k, q, (u, s) in zip(keys, qm, units)]
        dprobs = [nt(v, d) for v, d in zip(values, dam)]
        tops = [jnp.max(x, axis=0, keepdims=True) for x in scores]
        exps = [jnp.exp2(x - t) for x, t in zip(scores, tops)]
        probs = [e * (1.0 / jnp.sum(e, axis=0, keepdims=True)) for e in exps]
        probs_b = [p.astype(BF16) for p in probs]
        for (u, s), p, d in zip(units, probs_b, dam):
            dv_scr[s, slot_rows[u], :] = nn(p, d)
        ds = [p * (d - jnp.sum(p * d, axis=0, keepdims=True)) for p, d in zip(probs, dprobs)]
        ds_b = [d.astype(BF16) for d in ds]
        for (u, s), d, q in zip(units, ds_b, qm):
            dk_scr[s, slot_rows[u], :] = nn(d, q)
        for (u, s), p, v in zip(units, probs_b, values):
            a = collect(tn(p, v))
            gated_scr[s, mine_rows[u], :] = (gate_scr[s, mine_rows[u], :] * a).astype(BF16)
            dqg_scr[s, mine_rows[u], channels:] = (gyg_scr[s, mine_rows[u], :] * a).astype(BF16)
        for (u, s), d, k in zip(units, ds_b, keys):
            dqg_scr[s, mine_rows[u], 0:channels] = (collect(tn(d, k)) * scale).astype(BF16)
        for u, w in enumerate(ws):
            of_window = [d for d, unit in zip(ds, units) if unit[0] == u]
            total = of_window[0]
            for d in of_window[1:]:
                total = total + d
            tok_scr[...] += jnp.where(sames[u], total, 0.0)
            pw_scr[...] += nn(pair_ref[w], total.astype(BF16))
            turned = total.T
            for h in range(heads):
                low = turned[h * rows : h * rows + half_rows]
                high = turned[h * rows + half_rows : (h + 1) * rows]
                at = slice(h * half_rows, (h + 1) * half_rows)
                mine_ref[w, at, :] = jnp.where(first_mine, low, high)
                theirs_ref[w, at, :] = jnp.where(first_mine, high, low).astype(BF16)

    def gather_rows(s, b):
        dk, dv = None, None
        for w in range(max(0, b - 2 * span // rows), min(b, windows - 1) + 1):
            shift = jnp.clip(b * rows - starts_ref[w], -PAD, span)
            at = pl.ds(w * slot + PAD + shift, rows)
            k, v = dk_scr[s, at, :], dv_scr[s, at, :]
            dk, dv = (k, v) if dk is None else (dk + k, dv + v)
        return dk * (1.0 / LOG2E), dv

    halo_blocks = span // rows
    own_blocks = atoms // rows

    def project_halo(s, carry):
        for ref, first in ((before_ref, 0), (after_ref, span + atoms)):
            k_scr[s, first : first + span, :] = nn(ref[s], wk_ref[...]).astype(BF16).astype(F32)
            v_scr[s, first : first + span, :] = nn(ref[s], wv_ref[...]).astype(BF16).astype(F32)
        return carry

    edge_up = remote(to_upper_ref, from_lower, edge_sems, 0, upper)
    edge_down = remote(to_lower_ref, from_upper, edge_sems, 1, lower)

    def halo_gradient(s, carry):
        for first, out_ref in ((0, to_lower_ref), (halo_blocks + own_blocks, to_upper_ref)):
            for b in range(first, first + halo_blocks):
                dk, dv = gather_rows(s, b)
                k_scr[s, b * rows : (b + 1) * rows, :] = dk
                v_scr[s, b * rows : (b + 1) * rows, :] = dv
            at = slice(first * rows, first * rows + span)
            dkv = jnp.concatenate([k_scr[s, at, :].astype(BF16), v_scr[s, at, :].astype(BF16)], axis=1)
            weights = jnp.concatenate([wk_ref[...], wv_ref[...]], axis=1)
            out_ref[s] = nt(dkv, weights).astype(BF16)
        return carry

    blocks = windows // TOGETHER
    early = max(1, (blocks - 2) // 2 + (blocks - 2) % 2)

    def step(it, carry):
        @pl.when(it == early)
        def _():
            @pl.when(has_upper)
            def _():
                for copy in halo_down:
                    copy.wait_recv()

            @pl.when(has_lower)
            def _():
                for copy in halo_up:
                    copy.wait_recv()

            code_column(0, code_before[...])
            code_column(span + atoms, code_after[...])
            lax.fori_loop(0, samples, project_halo, 0)

        @pl.when(it == early + 2)
        def _():
            lax.fori_loop(0, samples, halo_gradient, 0)

            @pl.when(has_upper)
            def _():
                edge_up.start()

            @pl.when(has_lower)
            def _():
                edge_down.start()

        block = jnp.where(
            it < early,
            it + 1,
            jnp.where(it == early, 0, jnp.where(it == early + 1, blocks - 1, it - 1)),
        )
        attend(block)
        return carry

    lax.fori_loop(0, blocks, step, 0)
    pair_copy = remote(theirs_ref, got, core_sems, 1, peer)
    pair_copy.start()

    def weight_gradients(s, carry):
        for b in range(halo_blocks, halo_blocks + own_blocks):
            dk, dv = gather_rows(s, b)
            k_scr[s, b * rows : (b + 1) * rows, :] = dk
            v_scr[s, b * rows : (b + 1) * rows, :] = dv
        full = jnp.concatenate([before_ref[s], act_ref[s], after_ref[s]], axis=0)
        c = channels
        dkv = jnp.concatenate([k_scr[s].astype(BF16), v_scr[s].astype(BF16)], axis=1)
        from_kv = tn(full, dkv)
        from_qg = tn(act_ref[s], dqg_scr[s])
        sums_ref[0:c, :] += from_qg[:, 0:c]
        sums_ref[c : 2 * c, :] += from_kv[:, 0:c]
        sums_ref[2 * c : 3 * c, :] += from_kv[:, c:]
        sums_ref[3 * c : 4 * c, :] += from_qg[:, c:]
        sums_ref[4 * c : 5 * c, :] += tn(gated_scr[s], grad_ref[s])
        return carry

    lax.fori_loop(0, samples, weight_gradients, 0)
    shape = pw_scr.shape
    at_row = lax.broadcasted_iota(jnp.int32, shape, 0) // pair_channels
    at_col = lax.broadcasted_iota(jnp.int32, shape, 1) % rows
    diagonal = jnp.where(at_row == at_col, pw_scr[...], 0.0)
    base = 5 * channels
    sums_ref[base : base + pair_channels, :] = jnp.sum(
        diagonal.reshape(rows, pair_channels, stack), axis=0
    )
    sums_ref[base + pair_channels : base + pair_channels + 1, :] = jnp.sum(
        tok_scr[...], axis=0, keepdims=True
    )

    half_copy = remote(
        sums_ref.at[pl.ds(pl.multiple_of(other * half, 8), half)], got_half, core_sems, 0, peer
    )
    half_copy.start()

    inner = slice(span, atoms - span)

    def own_gradient(s, carry):
        own = slice(span, span + atoms)
        dq = dqg_scr[s, :, 0:channels]
        dg = dqg_scr[s, :, channels:]
        grads = jnp.concatenate(
            [dq, k_scr[s, own, :].astype(BF16), v_scr[s, own, :].astype(BF16), dg], axis=1
        )
        weights = jnp.concatenate([wq_ref[...], wk_ref[...], wv_ref[...], wg_ref[...]], axis=1)
        ga = nt(grads, weights)
        dk_scr[s, 0:span, :] = ga[0:span]
        dk_scr[s, span : 2 * span, :] = ga[atoms - span :]
        q_scr[s, inner, :] = ga[inner].astype(BF16)
        return carry

    lax.fori_loop(0, 2, own_gradient, 0)
    half_copy.wait_recv()
    own_half = pl.ds(pl.multiple_of(core * half, 8), half)
    part[...] = (sums_ref[own_half, :] + got_half[...]).reshape(part.shape)
    scatter = []
    for d in range(1, ranges):
        target = lax.rem(me + d, ranges)
        copy = remote(part.at[target], slots.at[d - 1], scatter_sems, d - 1, everyone[d - 1])
        copy.start()
        scatter.append(copy)
    lax.fori_loop(2, samples, own_gradient, 0)

    lane_out = lax.broadcasted_iota(jnp.int32, (pair_channels, heads * half_rows), 1)
    spread_rows = jnp.zeros((pair_channels, heads * half_rows), F32)
    for h in range(heads):
        spread_rows = jnp.where(lane_out // half_rows == h, wpair_values[:, h : h + 1], spread_rows)
    weight = jnp.concatenate(
        [
            jnp.where(lane_out % half_rows == i, spread_rows, 0.0).astype(BF16)
            for i in range(half_rows)
        ],
        axis=0,
    )
    for copy in scatter:
        copy.wait_recv()
    chunk_total = part[me]
    for d in range(1, ranges):
        chunk_total = chunk_total + slots[d - 1]
    place = pl.ds(pl.multiple_of(core * half + me * chunk, 8), chunk)
    total_ref[place, :] = chunk_total
    gather = []
    for d in range(1, ranges):
        copy = remote(
            total_ref.at[place], total_ref.at[place], gather_sems, d - 1, everyone[d - 1]
        )
        copy.start()
        gather.append(copy)

    pair_copy.wait_recv()
    out_rows = half_rows * pair_channels

    def pair_gradient(w, carry):
        both = mine_ref[w] + got[w].astype(F32)
        high = both.astype(BF16)
        low = (both - high.astype(F32)).astype(BF16)
        pair_ref[w, 0:out_rows, :] = (nn(weight, high) + nn(weight, low)).astype(BF16)
        return carry

    lax.fori_loop(0, windows, pair_gradient, 0)
    store_pair = pltpu.make_async_copy(
        pair_ref.at[:, pl.ds(0, out_rows)], pair_out_hbm, store_sems.at[0]
    )
    store_pair.start()

    for copy in gather:
        copy.wait_recv()
    last_copy = remote(
        total_ref.at[own_half], total_ref.at[own_half], core_sems, 2, peer
    )
    last_copy.start()

    @pl.when(has_lower)
    def _():
        edge_down.wait_send()
        edge_up.wait_recv()

    @pl.when(has_upper)
    def _():
        edge_up.wait_send()
        edge_down.wait_recv()

    @pl.when(jnp.logical_not(has_lower))
    def _():
        from_lower[...] = jnp.zeros_like(from_lower)

    @pl.when(jnp.logical_not(has_upper))
    def _():
        from_upper[...] = jnp.zeros_like(from_upper)

    def add_edges(s, carry):
        q_scr[s, 0:span, :] = (dk_scr[s, 0:span, :] + from_lower[s].astype(F32)).astype(BF16)
        q_scr[s, atoms - span : atoms, :] = (
            dk_scr[s, span : 2 * span, :] + from_upper[s].astype(F32)
        ).astype(BF16)
        return carry

    lax.fori_loop(0, samples, add_edges, 0)
    store_act = pltpu.make_async_copy(q_scr, ga_hbm, store_sems.at[1])
    store_act.start()

    @pl.when(has_upper)
    def _():
        for copy in halo_up:
            copy.wait_send()

    @pl.when(has_lower)
    def _():
        for copy in halo_down:
            copy.wait_send()

    half_copy.wait_send()
    pair_copy.wait_send()
    for copy in scatter + gather:
        copy.wait_send()
    last_copy.wait()
    store_pair.wait()
    store_act.wait()


def finish_kernel(heads, ga_ref, pair_ref, total_ref, ga_out, pair_out, small_out, sems):
    copies = [
        pltpu.make_async_copy(ga_ref, ga_out, sems.at[0]),
        pltpu.make_async_copy(pair_ref, pair_out, sems.at[1]),
    ]
    for copy in copies:
        copy.start()
    small_out[...] = total_ref[...]
    for copy in copies:
        copy.wait()


def per_device(
    act,
    grad_out,
    pair,
    w_query,
    w_key,
    w_value,
    w_gate,
    w_out,
    w_pair,
    w_token,
    offsets,
    atom_token,
    padding,
):
    samples, atoms, channels = act.shape
    windows = offsets.shape[0]
    rows = atoms // windows
    pair_channels, heads = w_pair.shape
    span = pair.shape[-1]
    stack = heads * rows
    half = rows // 2
    ranges = lax.axis_size("atoms")
    wide = atoms + 2 * span
    vmem = pl.BlockSpec(memory_space=pltpu.VMEM)
    smem = pl.BlockSpec(memory_space=pltpu.SMEM)
    anywhere = pl.BlockSpec(memory_space=pl.ANY)
    chunk = 8 * pl.cdiv(5 * channels + pair_channels + 1, 16 * ranges)
    sum_rows = 2 * ranges * chunk

    def kernel(*refs):
        fused_kernel(ranges, *refs)

    edge = pltpu.VMEM((samples, span, channels), BF16)
    slot_rows = windows * (span + PAD) + PAD
    grad_act, grad_pair, total = pl.pallas_call(
        kernel,
        out_shape=(
            jax.ShapeDtypeStruct((samples, atoms, channels), BF16),
            jax.ShapeDtypeStruct((windows, half * pair_channels, span), BF16),
            jax.ShapeDtypeStruct((sum_rows, channels), F32),
        ),
        in_specs=[smem] * 3 + [anywhere] * 3 + [vmem] * 7,
        out_specs=(anywhere, anywhere, vmem),
        scratch_shapes=[
            pltpu.VMEM((samples, atoms, channels), BF16),
            pltpu.VMEM((samples, atoms, channels), BF16),
            pltpu.VMEM((windows, rows * pair_channels, span), BF16),
            edge,
            edge,
            pltpu.VMEM((atoms // span, 1, span), jnp.int32),
            pltpu.VMEM((1, span), jnp.int32),
            pltpu.VMEM((1, span), jnp.int32),
            pltpu.VMEM((samples, wide, channels), F32),
            pltpu.VMEM((samples, wide, channels), F32),
            pltpu.VMEM((samples, atoms, channels), BF16),
            pltpu.VMEM((samples, atoms, channels), BF16),
            pltpu.VMEM((samples, atoms, channels), F32),
            pltpu.VMEM((samples, atoms, channels), F32),
            pltpu.VMEM((samples, atoms, 2 * channels), BF16),
            pltpu.VMEM((samples, atoms, channels), BF16),
            pltpu.VMEM((samples, slot_rows, channels), F32),
            pltpu.VMEM((samples, slot_rows, channels), F32),
            pltpu.VMEM((rows * pair_channels, stack), F32),
            pltpu.VMEM((span, stack), F32),
            pltpu.VMEM((rows * pair_channels, stack), BF16),
            pltpu.VMEM((wide, stack), F32),
            pltpu.VMEM((windows, 1, stack), F32),
            pltpu.VMEM((windows, heads * half, span), F32),
            pltpu.VMEM((windows, heads * half, span), BF16),
            pltpu.VMEM((windows, heads * half, span), BF16),
            edge,
            edge,
            edge,
            edge,
            pltpu.VMEM((sum_rows, channels), F32),
            pltpu.VMEM((ranges * chunk, channels), F32),
            pltpu.VMEM((ranges, chunk, channels), F32),
            pltpu.VMEM((ranges - 1, chunk, channels), F32),
            pltpu.SMEM((windows,), jnp.int32),
            pltpu.SemaphoreType.DMA((3,)),
            pltpu.SemaphoreType.DMA((2,)),
            pltpu.SemaphoreType.DMA((2, 4)),
            pltpu.SemaphoreType.DMA((2, 2)),
            pltpu.SemaphoreType.DMA((2, 3)),
            pltpu.SemaphoreType.DMA((2, ranges - 1)),
            pltpu.SemaphoreType.DMA((2, ranges - 1)),
        ],
        compiler_params=pltpu.CompilerParams(
            collective_id=0, has_side_effects=True, vmem_limit_bytes=63 * 1024 * 1024
        ),
        name="fused",
    )(
        offsets,
        w_token,
        padding,
        act,
        grad_out,
        pair.reshape(windows, rows * pair_channels, span),
        atom_token.reshape(atoms // span, span),
        w_query,
        w_key,
        w_value,
        w_gate,
        w_out,
        w_pair.T,
    )

    def last_kernel(*refs):
        finish_kernel(heads, *refs)

    grad_act, grad_pair, total = pl.pallas_call(
        last_kernel,
        out_shape=(
            jax.ShapeDtypeStruct(grad_act.shape, BF16),
            jax.ShapeDtypeStruct(grad_pair.shape, BF16),
            jax.ShapeDtypeStruct(total.shape, F32),
        ),
        in_specs=[anywhere, anywhere, vmem],
        out_specs=(anywhere, anywhere, vmem),
        scratch_shapes=[pltpu.SemaphoreType.DMA((2,))],
        name="finish",
    )(grad_act, grad_pair, total)

    base = 5 * channels
    grad_weights = total[:base].reshape(5, channels, channels)
    grad_pair_weight = jnp.sum(
        total[base : base + pair_channels].reshape(pair_channels, heads, rows), axis=-1
    )
    grad_token_weight = jnp.sum(total[base + pair_channels].reshape(heads, rows), axis=-1)
    grad_pair = grad_pair.reshape(windows, half, pair_channels, span)
    return (grad_act, grad_pair, grad_weights, grad_pair_weight, grad_token_weight)


def solution(mesh):
    in_specs = (
        P("samples", ("groups", "atoms"), None),
        P("samples", ("groups", "atoms"), None),
        P(("groups", "atoms"), None, None, None),
        P(),
        P(),
        P(),
        P(),
        P(),
        P(),
        P(),
        P(("groups", "atoms")),
        P(("groups", "atoms")),
        P(("groups", "atoms")),
    )
    out_specs = (
        P("samples", ("groups", "atoms"), None),
        P(("groups", "atoms"), "samples", None, None),
        P("groups", None, None),
        P("groups", None),
        P("groups"),
    )
    return jax.shard_map(
        per_device, mesh=mesh, in_specs=in_specs, out_specs=out_specs, check_vma=False
    )
```

```python
import math

import jax
import jax.numpy as jnp
from jax import lax
from jax.experimental import pallas as pl
from jax.experimental.pallas import tpu as pltpu
from jax.sharding import PartitionSpec as P

MASKED = -1000000000.0
BF16 = jnp.bfloat16
F32 = jnp.float32
LOG2E = math.log2(math.e)
TOGETHER = 4
PAD = 32


def nn(a, b):
    return lax.dot_general(a, b, (((1,), (0,)), ((), ())), preferred_element_type=F32)


def nt(a, b):
    return lax.dot_general(a, b, (((1,), (1,)), ((), ())), preferred_element_type=F32)


def tn(a, b):
    return lax.dot_general(a, b, (((0,), (0,)), ((), ())), preferred_element_type=F32)


def greet(barrier, devices):
    for device in devices:
        pl.semaphore_signal(
            barrier, inc=1, device_id=device, device_id_type=pl.DeviceIdType.MESH
        )


def remote(src, dst, sems, slot, device):
    return pltpu.make_async_remote_copy(
        src_ref=src,
        dst_ref=dst,
        send_sem=sems.at[0, slot],
        recv_sem=sems.at[1, slot],
        device_id=device,
        device_id_type=pl.DeviceIdType.MESH,
    )


def fused_kernel(
    ranges,
    offsets_ref,
    wtoken_ref,
    padding_ref,
    act_hbm,
    grad_hbm,
    pair_hbm,
    token_ref,
    wq_ref,
    wk_ref,
    wv_ref,
    wg_ref,
    wo_ref,
    wpair_ref,
    ga_hbm,
    pair_out_hbm,
    total_ref,
    act_ref,
    grad_ref,
    pair_ref,
    before_ref,
    after_ref,
    code_scr,
    code_before,
    code_after,
    k_scr,
    v_scr,
    q_scr,
    da_scr,
    gate_scr,
    gyg_scr,
    dqg_scr,
    gated_scr,
    dk_scr,
    dv_scr,
    pw_scr,
    tok_scr,
    wpair_scr,
    key_code_scr,
    query_code_scr,
    mine_ref,
    theirs_ref,
    got,
    to_lower_ref,
    to_upper_ref,
    from_lower,
    from_upper,
    sums_ref,
    got_half,
    part,
    slots,
    starts_ref,
    load_sems,
    store_sems,
    halo_sems,
    edge_sems,
    core_sems,
    scatter_sems,
    gather_sems,
):
    me = lax.axis_index("atoms")
    core = lax.axis_index("samples")
    other = 1 - core
    samples, atoms, channels = act_ref.shape
    windows = pair_ref.shape[0]
    rows = atoms // windows
    span = before_ref.shape[1]
    wide = atoms + 2 * span
    pair_channels = wpair_ref.shape[1]
    heads = wpair_ref.shape[0]
    head_dim = channels // heads
    scale = 1.0 / math.sqrt(head_dim)
    stack = heads * rows
    half_rows = rows // 2
    chunk = part.shape[1]
    half = ranges * chunk
    has_lower, has_upper = me > 0, me < ranges - 1
    lower, upper, peer = {"atoms": me - 1}, {"atoms": me + 1}, {"samples": other}
    everyone = [{"atoms": lax.rem(me + d, ranges)} for d in range(1, ranges)]

    barrier = pltpu.get_barrier_semaphore()
    greet(barrier, [peer] + everyone)
    load_act = pltpu.make_async_copy(act_hbm, act_ref, load_sems.at[0])
    load_grad = pltpu.make_async_copy(grad_hbm, grad_ref, load_sems.at[1])
    load_pair = pltpu.make_async_copy(pair_hbm, pair_ref, load_sems.at[2])
    load_act.start()
    load_grad.start()
    load_pair.start()

    code_rows = atoms // span
    live_end = atoms - padding_ref[0]
    lane_at = lax.broadcasted_iota(jnp.int32, (1, span), 1)
    for r in range(code_rows):
        code_scr[r] = jnp.where(lane_at + r * span < live_end, token_ref[r : r + 1, :] + 1, 0)

    pl.semaphore_wait(barrier, ranges)
    halo_up = [
        remote(act_hbm.at[:, pl.ds(atoms - span, span)], before_ref, halo_sems, 0, upper),
        remote(code_scr.at[code_rows - 1], code_before, halo_sems, 1, upper),
    ]
    halo_down = [
        remote(act_hbm.at[:, pl.ds(0, span)], after_ref, halo_sems, 2, lower),
        remote(code_scr.at[0], code_after, halo_sems, 3, lower),
    ]

    @pl.when(has_upper)
    def _():
        for copy in halo_up:
            copy.start()

    @pl.when(has_lower)
    def _():
        for copy in halo_down:
            copy.start()

    @pl.when(jnp.logical_not(has_lower))
    def _():
        before_ref[...] = jnp.zeros_like(before_ref)
        code_before[...] = jnp.zeros_like(code_before)

    @pl.when(jnp.logical_not(has_upper))
    def _():
        after_ref[...] = jnp.zeros_like(after_ref)
        code_after[...] = jnp.zeros_like(code_after)

    def code_column(first, row):
        column = jnp.broadcast_to(row.astype(F32), (stack, span)).T
        key_code_scr[first : first + span, :] = column

    lane_row = lax.broadcasted_iota(jnp.int32, (pair_channels, stack), 1) % rows
    lane_head = lax.broadcasted_iota(jnp.int32, (pair_channels, stack), 1) // rows
    wpair_values = wpair_ref[...].astype(F32).T
    wpair_rows = jnp.zeros((pair_channels, stack), F32)
    wtoken_row = jnp.zeros((1, stack), F32)
    for h in range(heads):
        wpair_rows = jnp.where(lane_head == h, wpair_values[:, h : h + 1], wpair_rows)
        wtoken_row = jnp.where(lane_head[0:1] == h, wtoken_ref[h], wtoken_row)
    for i in range(rows):
        wpair_scr[i * pair_channels : (i + 1) * pair_channels, :] = jnp.where(
            lane_row == i, wpair_rows, 0.0
        ).astype(BF16)
    for r in range(code_rows):
        code_column(span + r * span, code_scr[r])
        tokens = (token_ref[r : r + 1, :] + 1).astype(F32)
        for u in range(span // rows):
            piece = tokens[:, u * rows : (u + 1) * rows]
            query_code_scr[r * (span // rows) + u] = jnp.concatenate([piece] * heads, axis=1)
    pw_scr[...] = jnp.zeros_like(pw_scr)
    tok_scr[...] = jnp.zeros_like(tok_scr)
    sums_ref[...] = jnp.zeros_like(sums_ref)
    anchor = me * atoms
    last_start = ranges * atoms - span
    for w in range(windows):
        starts_ref[w] = (
            jnp.clip(anchor + w * rows + offsets_ref[w], 0, last_start) - anchor + span
        )

    load_act.wait()
    load_grad.wait()
    slot = span + PAD

    def project(s, carry):
        own = act_ref[s]
        q_scr[s] = (nn(own, wq_ref[...]) * (scale * LOG2E)).astype(BF16)
        gate = jax.nn.sigmoid(nn(own, wg_ref[...]))
        gated_gy = nt(grad_ref[s], wo_ref[...]) * gate
        gate_scr[s] = gate
        da_scr[s] = gated_gy.astype(BF16)
        gyg_scr[s] = gated_gy * (1.0 - gate)
        k_scr[s, span : span + atoms, :] = nn(own, wk_ref[...]).astype(BF16).astype(F32)
        v_scr[s, span : span + atoms, :] = nn(own, wv_ref[...]).astype(BF16).astype(F32)
        blank = jnp.zeros((PAD, channels), F32)
        for w in range(windows + 1):
            dk_scr[s, w * slot : w * slot + PAD, :] = blank
            dv_scr[s, w * slot : w * slot + PAD, :] = blank
        return carry

    lax.fori_loop(0, samples, project, 0)
    load_pair.wait()

    row_head = lax.broadcasted_iota(jnp.int32, (stack, channels), 0) // rows
    column_head = lax.broadcasted_iota(jnp.int32, (stack, channels), 1) // head_dim
    head_mask = jnp.where(row_head == column_head, 1.0, 0.0).astype(BF16)
    lane = lax.broadcasted_iota(jnp.int32, (rows, channels), 1) // head_dim
    head_is = [lane == h for h in range(heads)]
    first_mine = core == 0

    def spread(x):
        return jnp.concatenate([x] * heads, axis=0) * head_mask

    def collect(x):
        out = x[0:rows]
        for h in range(1, heads):
            out = jnp.where(head_is[h], x[h * rows : (h + 1) * rows], out)
        return out

    def attend(block):
        ws = [block * TOGETHER + u for u in range(TOGETHER)]
        mine_rows = [pl.ds(pl.multiple_of(w * rows, rows), rows) for w in ws]
        key_rows = [pl.ds(starts_ref[w], span) for w in ws]
        slot_rows = [pl.ds(pl.multiple_of(w * slot + PAD, 8), span) for w in ws]
        sames, biases = [], []
        for u, w in enumerate(ws):
            key_code = key_code_scr[key_rows[u], :]
            same = key_code == query_code_scr[w]
            bias = (tn(pair_ref[w], wpair_scr[...]) + jnp.where(same, wtoken_row, 0.0)) * LOG2E
            biases.append(jnp.where(key_code > 0.0, bias, MASKED))
            sames.append(same)
        units = [(u, s) for u in range(TOGETHER) for s in range(samples)]
        keys = [k_scr[s, key_rows[u], :].astype(BF16) for u, s in units]
        values = [v_scr[s, key_rows[u], :].astype(BF16) for u, s in units]
        qm = [spread(q_scr[s, mine_rows[u], :]) for u, s in units]
        dam = [spread(da_scr[s, mine_rows[u], :]) for u, s in units]
        scores = [nt(k, q) + biases[u] for k, q, (u, s) in zip(keys, qm, units)]
        dprobs = [nt(v, d) for v, d in zip(values, dam)]
        tops = [jnp.max(x, axis=0, keepdims=True) for x in scores]
        exps = [jnp.exp2(x - t) for x, t in zip(scores, tops)]
        probs = [e * (1.0 / jnp.sum(e, axis=0, keepdims=True)) for e in exps]
        probs_b = [p.astype(BF16) for p in probs]
        for (u, s), p, d in zip(units, probs_b, dam):
            dv_scr[s, slot_rows[u], :] = nn(p, d)
        ds = [p * (d - jnp.sum(p * d, axis=0, keepdims=True)) for p, d in zip(probs, dprobs)]
        ds_b = [d.astype(BF16) for d in ds]
        for (u, s), d, q in zip(units, ds_b, qm):
            dk_scr[s, slot_rows[u], :] = nn(d, q)
        for (u, s), p, v in zip(units, probs_b, values):
            a = collect(tn(p, v))
            gated_scr[s, mine_rows[u], :] = (gate_scr[s, mine_rows[u], :] * a).astype(BF16)
            dqg_scr[s, mine_rows[u], channels:] = (gyg_scr[s, mine_rows[u], :] * a).astype(BF16)
        for (u, s), d, k in zip(units, ds_b, keys):
            dqg_scr[s, mine_rows[u], 0:channels] = (collect(tn(d, k)) * scale).astype(BF16)
        for u, w in enumerate(ws):
            of_window = [d for d, unit in zip(ds, units) if unit[0] == u]
            total = of_window[0]
            for d in of_window[1:]:
                total = total + d
            tok_scr[...] += jnp.where(sames[u], total, 0.0)
            pw_scr[...] += nn(pair_ref[w], total.astype(BF16))
            turned = total.T
            for h in range(heads):
                low = turned[h * rows : h * rows + half_rows]
                high = turned[h * rows + half_rows : (h + 1) * rows]
                at = slice(h * half_rows, (h + 1) * half_rows)
                mine_ref[w, at, :] = jnp.where(first_mine, low, high)
                theirs_ref[w, at, :] = jnp.where(first_mine, high, low).astype(BF16)

    def gather_rows(s, b):
        dk, dv = None, None
        for w in range(max(0, b - 2 * span // rows), min(b, windows - 1) + 1):
            shift = jnp.clip(b * rows - starts_ref[w], -PAD, span)
            at = pl.ds(w * slot + PAD + shift, rows)
            k, v = dk_scr[s, at, :], dv_scr[s, at, :]
            dk, dv = (k, v) if dk is None else (dk + k, dv + v)
        return dk * (1.0 / LOG2E), dv

    halo_blocks = span // rows
    own_blocks = atoms // rows

    def project_halo(s, carry):
        for ref, first in ((before_ref, 0), (after_ref, span + atoms)):
            k_scr[s, first : first + span, :] = nn(ref[s], wk_ref[...]).astype(BF16).astype(F32)
            v_scr[s, first : first + span, :] = nn(ref[s], wv_ref[...]).astype(BF16).astype(F32)
        return carry

    edge_up = remote(to_upper_ref, from_lower, edge_sems, 0, upper)
    edge_down = remote(to_lower_ref, from_upper, edge_sems, 1, lower)

    def halo_gradient(s, carry):
        for first, out_ref in ((0, to_lower_ref), (halo_blocks + own_blocks, to_upper_ref)):
            for b in range(first, first + halo_blocks):
                dk, dv = gather_rows(s, b)
                k_scr[s, b * rows : (b + 1) * rows, :] = dk
                v_scr[s, b * rows : (b + 1) * rows, :] = dv
            at = slice(first * rows, first * rows + span)
            dkv = jnp.concatenate([k_scr[s, at, :].astype(BF16), v_scr[s, at, :].astype(BF16)], axis=1)
            weights = jnp.concatenate([wk_ref[...], wv_ref[...]], axis=1)
            out_ref[s] = nt(dkv, weights).astype(BF16)
        return carry

    blocks = windows // TOGETHER
    early = max(1, (blocks - 2) // 2 + (blocks - 2) % 2)

    def step(it, carry):
        @pl.when(it == early)
        def _():
            @pl.when(has_upper)
            def _():
                for copy in halo_down:
                    copy.wait_recv()

            @pl.when(has_lower)
            def _():
                for copy in halo_up:
                    copy.wait_recv()

            code_column(0, code_before[...])
            code_column(span + atoms, code_after[...])
            lax.fori_loop(0, samples, project_halo, 0)

        @pl.when(it == early + 2)
        def _():
            lax.fori_loop(0, samples, halo_gradient, 0)

            @pl.when(has_upper)
            def _():
                edge_up.start()

            @pl.when(has_lower)
            def _():
                edge_down.start()

        block = jnp.where(
            it < early,
            it + 1,
            jnp.where(it == early, 0, jnp.where(it == early + 1, blocks - 1, it - 1)),
        )
        attend(block)
        return carry

    lax.fori_loop(0, blocks, step, 0)
    pair_copy = remote(theirs_ref, got, core_sems, 1, peer)
    pair_copy.start()

    def weight_gradients(s, carry):
        for b in range(halo_blocks, halo_blocks + own_blocks):
            dk, dv = gather_rows(s, b)
            k_scr[s, b * rows : (b + 1) * rows, :] = dk
            v_scr[s, b * rows : (b + 1) * rows, :] = dv
        full = jnp.concatenate([before_ref[s], act_ref[s], after_ref[s]], axis=0)
        c = channels
        dkv = jnp.concatenate([k_scr[s].astype(BF16), v_scr[s].astype(BF16)], axis=1)
        from_kv = tn(full, dkv)
        from_qg = tn(act_ref[s], dqg_scr[s])
        sums_ref[0:c, :] += from_qg[:, 0:c]
        sums_ref[c : 2 * c, :] += from_kv[:, 0:c]
        sums_ref[2 * c : 3 * c, :] += from_kv[:, c:]
        sums_ref[3 * c : 4 * c, :] += from_qg[:, c:]
        sums_ref[4 * c : 5 * c, :] += tn(gated_scr[s], grad_ref[s])
        return carry

    lax.fori_loop(0, samples, weight_gradients, 0)
    shape = pw_scr.shape
    at_row = lax.broadcasted_iota(jnp.int32, shape, 0) // pair_channels
    at_col = lax.broadcasted_iota(jnp.int32, shape, 1) % rows
    diagonal = jnp.where(at_row == at_col, pw_scr[...], 0.0)
    base = 5 * channels
    sums_ref[base : base + pair_channels, :] = jnp.sum(
        diagonal.reshape(rows, pair_channels, stack), axis=0
    )
    sums_ref[base + pair_channels : base + pair_channels + 1, :] = jnp.sum(
        tok_scr[...], axis=0, keepdims=True
    )

    half_copy = remote(
        sums_ref.at[pl.ds(pl.multiple_of(other * half, 8), half)], got_half, core_sems, 0, peer
    )
    half_copy.start()

    inner = slice(span, atoms - span)

    def own_gradient(s, carry):
        own = slice(span, span + atoms)
        dq = dqg_scr[s, :, 0:channels]
        dg = dqg_scr[s, :, channels:]
        grads = jnp.concatenate(
            [dq, k_scr[s, own, :].astype(BF16), v_scr[s, own, :].astype(BF16), dg], axis=1
        )
        weights = jnp.concatenate([wq_ref[...], wk_ref[...], wv_ref[...], wg_ref[...]], axis=1)
        ga = nt(grads, weights)
        dk_scr[s, 0:span, :] = ga[0:span]
        dk_scr[s, span : 2 * span, :] = ga[atoms - span :]
        q_scr[s, inner, :] = ga[inner].astype(BF16)
        return carry

    lax.fori_loop(0, 2, own_gradient, 0)
    half_copy.wait_recv()
    own_half = pl.ds(pl.multiple_of(core * half, 8), half)
    part[...] = (sums_ref[own_half, :] + got_half[...]).reshape(part.shape)
    scatter = []
    for d in range(1, ranges):
        target = lax.rem(me + d, ranges)
        copy = remote(part.at[target], slots.at[d - 1], scatter_sems, d - 1, everyone[d - 1])
        copy.start()
        scatter.append(copy)
    lax.fori_loop(2, samples, own_gradient, 0)

    lane_out = lax.broadcasted_iota(jnp.int32, (pair_channels, heads * half_rows), 1)
    spread_rows = jnp.zeros((pair_channels, heads * half_rows), F32)
    for h in range(heads):
        spread_rows = jnp.where(lane_out // half_rows == h, wpair_values[:, h : h + 1], spread_rows)
    weight = jnp.concatenate(
        [
            jnp.where(lane_out % half_rows == i, spread_rows, 0.0).astype(BF16)
            for i in range(half_rows)
        ],
        axis=0,
    )
    for copy in scatter:
        copy.wait_recv()
    chunk_total = part[me]
    for d in range(1, ranges):
        chunk_total = chunk_total + slots[d - 1]
    place = pl.ds(pl.multiple_of(core * half + me * chunk, 8), chunk)
    total_ref[place, :] = chunk_total
    gather = []
    for d in range(1, ranges):
        copy = remote(
            total_ref.at[place], total_ref.at[place], gather_sems, d - 1, everyone[d - 1]
        )
        copy.start()
        gather.append(copy)

    pair_copy.wait_recv()
    out_rows = half_rows * pair_channels

    def pair_gradient(w, carry):
        both = mine_ref[w] + got[w].astype(F32)
        high = both.astype(BF16)
        low = (both - high.astype(F32)).astype(BF16)
        pair_ref[w, 0:out_rows, :] = (nn(weight, high) + nn(weight, low)).astype(BF16)
        return carry

    lax.fori_loop(0, windows, pair_gradient, 0)
    store_pair = pltpu.make_async_copy(
        pair_ref.at[:, pl.ds(0, out_rows)], pair_out_hbm, store_sems.at[0]
    )
    store_pair.start()

    for copy in gather:
        copy.wait_recv()
    last_copy = remote(
        total_ref.at[own_half], total_ref.at[own_half], core_sems, 2, peer
    )
    last_copy.start()

    @pl.when(has_lower)
    def _():
        edge_down.wait_send()
        edge_up.wait_recv()

    @pl.when(has_upper)
    def _():
        edge_up.wait_send()
        edge_down.wait_recv()

    @pl.when(jnp.logical_not(has_lower))
    def _():
        from_lower[...] = jnp.zeros_like(from_lower)

    @pl.when(jnp.logical_not(has_upper))
    def _():
        from_upper[...] = jnp.zeros_like(from_upper)

    def add_edges(s, carry):
        q_scr[s, 0:span, :] = (dk_scr[s, 0:span, :] + from_lower[s].astype(F32)).astype(BF16)
        q_scr[s, atoms - span : atoms, :] = (
            dk_scr[s, span : 2 * span, :] + from_upper[s].astype(F32)
        ).astype(BF16)
        return carry

    lax.fori_loop(0, samples, add_edges, 0)
    store_act = pltpu.make_async_copy(q_scr, ga_hbm, store_sems.at[1])
    store_act.start()

    @pl.when(has_upper)
    def _():
        for copy in halo_up:
            copy.wait_send()

    @pl.when(has_lower)
    def _():
        for copy in halo_down:
            copy.wait_send()

    half_copy.wait_send()
    pair_copy.wait_send()
    for copy in scatter + gather:
        copy.wait_send()
    last_copy.wait()
    store_pair.wait()
    store_act.wait()


def finish_kernel(
    shapes,
    ga_ref,
    gp_ref,
    total_ref,
    ga_out,
    gp_out,
    weights_out,
    pair_weight_out,
    token_weight_out,
    ga_scr,
    gp_scr,
    load_sems,
    store_sems,
):
    pair_channels, heads, pieces = shapes
    moves = []
    for n, (src, held, dst) in enumerate(((ga_ref, ga_scr, ga_out), (gp_ref, gp_scr, gp_out))):
        size = src.shape[0] // pieces
        for p in range(pieces):
            at = pl.ds(p * size, size)
            load = pltpu.make_async_copy(src.at[at], held.at[at], load_sems.at[n, p])
            store = pltpu.make_async_copy(held.at[at], dst.at[at], store_sems.at[n, p])
            moves.append((load, store))
    for load, _ in moves:
        load.start()
    base = weights_out.shape[0]
    channels = weights_out.shape[1]
    weights_out[...] = total_ref[0:base, :]
    turned = total_ref[base : base + channels, :].T
    by_head = jnp.sum(turned.reshape(heads, channels // heads, channels), axis=1)
    pair_weight_out[...] = by_head[:, 0:pair_channels]
    for h in range(heads):
        token_weight_out[h] = by_head[h, pair_channels]
    for load, store in moves:
        load.wait()
        store.start()
    for _, store in moves:
        store.wait()


def per_device(
    act,
    grad_out,
    pair,
    w_query,
    w_key,
    w_value,
    w_gate,
    w_out,
    w_pair,
    w_token,
    offsets,
    atom_token,
    padding,
):
    samples, atoms, channels = act.shape
    windows = offsets.shape[0]
    rows = atoms // windows
    pair_channels, heads = w_pair.shape
    span = pair.shape[-1]
    stack = heads * rows
    half = rows // 2
    ranges = lax.axis_size("atoms")
    wide = atoms + 2 * span
    vmem = pl.BlockSpec(memory_space=pltpu.VMEM)
    smem = pl.BlockSpec(memory_space=pltpu.SMEM)
    anywhere = pl.BlockSpec(memory_space=pl.ANY)
    chunk = 8 * pl.cdiv(5 * channels + pair_channels + 1, 16 * ranges)
    sum_rows = 2 * ranges * chunk

    def kernel(*refs):
        fused_kernel(ranges, *refs)

    edge = pltpu.VMEM((samples, span, channels), BF16)
    slot_rows = windows * (span + PAD) + PAD
    grad_act, grad_pair, total = pl.pallas_call(
        kernel,
        out_shape=(
            jax.ShapeDtypeStruct((samples, atoms, channels), BF16),
            jax.ShapeDtypeStruct((windows, half * pair_channels, span), BF16),
            jax.ShapeDtypeStruct((sum_rows, channels), F32),
        ),
        in_specs=[smem] * 3 + [anywhere] * 3 + [vmem] * 7,
        out_specs=(anywhere, anywhere, vmem),
        scratch_shapes=[
            pltpu.VMEM((samples, atoms, channels), BF16),
            pltpu.VMEM((samples, atoms, channels), BF16),
            pltpu.VMEM((windows, rows * pair_channels, span), BF16),
            edge,
            edge,
            pltpu.VMEM((atoms // span, 1, span), jnp.int32),
            pltpu.VMEM((1, span), jnp.int32),
            pltpu.VMEM((1, span), jnp.int32),
            pltpu.VMEM((samples, wide, channels), F32),
            pltpu.VMEM((samples, wide, channels), F32),
            pltpu.VMEM((samples, atoms, channels), BF16),
            pltpu.VMEM((samples, atoms, channels), BF16),
            pltpu.VMEM((samples, atoms, channels), F32),
            pltpu.VMEM((samples, atoms, channels), F32),
            pltpu.VMEM((samples, atoms, 2 * channels), BF16),
            pltpu.VMEM((samples, atoms, channels), BF16),
            pltpu.VMEM((samples, slot_rows, channels), F32),
            pltpu.VMEM((samples, slot_rows, channels), F32),
            pltpu.VMEM((rows * pair_channels, stack), F32),
            pltpu.VMEM((span, stack), F32),
            pltpu.VMEM((rows * pair_channels, stack), BF16),
            pltpu.VMEM((wide, stack), F32),
            pltpu.VMEM((windows, 1, stack), F32),
            pltpu.VMEM((windows, heads * half, span), F32),
            pltpu.VMEM((windows, heads * half, span), BF16),
            pltpu.VMEM((windows, heads * half, span), BF16),
            edge,
            edge,
            edge,
            edge,
            pltpu.VMEM((sum_rows, channels), F32),
            pltpu.VMEM((ranges * chunk, channels), F32),
            pltpu.VMEM((ranges, chunk, channels), F32),
            pltpu.VMEM((ranges - 1, chunk, channels), F32),
            pltpu.SMEM((windows,), jnp.int32),
            pltpu.SemaphoreType.DMA((3,)),
            pltpu.SemaphoreType.DMA((2,)),
            pltpu.SemaphoreType.DMA((2, 4)),
            pltpu.SemaphoreType.DMA((2, 2)),
            pltpu.SemaphoreType.DMA((2, 3)),
            pltpu.SemaphoreType.DMA((2, ranges - 1)),
            pltpu.SemaphoreType.DMA((2, ranges - 1)),
        ],
        compiler_params=pltpu.CompilerParams(
            collective_id=0, has_side_effects=True, vmem_limit_bytes=63 * 1024 * 1024
        ),
        name="fused",
    )(
        offsets,
        w_token,
        padding,
        act,
        grad_out,
        pair.reshape(windows, rows * pair_channels, span),
        atom_token.reshape(atoms // span, span),
        w_query,
        w_key,
        w_value,
        w_gate,
        w_out,
        w_pair.T,
    )

    pieces = math.gcd(4, math.gcd(samples, windows))
    base = 5 * channels

    def last_kernel(*refs):
        finish_kernel((pair_channels, heads, pieces), *refs)

    grad_act, grad_pair, weights, pair_weight, grad_token_weight = pl.pallas_call(
        last_kernel,
        out_shape=(
            jax.ShapeDtypeStruct(grad_act.shape, BF16),
            jax.ShapeDtypeStruct(grad_pair.shape, BF16),
            jax.ShapeDtypeStruct((base, channels), F32),
            jax.ShapeDtypeStruct((heads, pair_channels), F32),
            jax.ShapeDtypeStruct((heads,), F32),
        ),
        in_specs=[anywhere, anywhere, vmem],
        out_specs=(anywhere, anywhere, vmem, vmem, smem),
        scratch_shapes=[
            pltpu.VMEM(grad_act.shape, BF16),
            pltpu.VMEM(grad_pair.shape, BF16),
            pltpu.SemaphoreType.DMA((2, pieces)),
            pltpu.SemaphoreType.DMA((2, pieces)),
        ],
        name="finish",
    )(grad_act, grad_pair, total)

    grad_weights = weights.reshape(5, channels, channels)
    grad_pair_weight = pair_weight.T
    grad_pair = grad_pair.reshape(windows, half, pair_channels, span)
    return (grad_act, grad_pair, grad_weights, grad_pair_weight, grad_token_weight)


def solution(mesh):
    in_specs = (
        P("samples", ("groups", "atoms"), None),
        P("samples", ("groups", "atoms"), None),
        P(("groups", "atoms"), None, None, None),
        P(),
        P(),
        P(),
        P(),
        P(),
        P(),
        P(),
        P(("groups", "atoms")),
        P(("groups", "atoms")),
        P(("groups", "atoms")),
    )
    out_specs = (
        P("samples", ("groups", "atoms"), None),
        P(("groups", "atoms"), "samples", None, None),
        P("groups", None, None),
        P("groups", None),
        P("groups"),
    )
    return jax.shard_map(
        per_device, mesh=mesh, in_specs=in_specs, out_specs=out_specs, check_vma=False
    )
```

```python
import math

import jax
import jax.numpy as jnp
from jax import lax
from jax.experimental import pallas as pl
from jax.experimental.pallas import tpu as pltpu
from jax.sharding import PartitionSpec as P

MASKED = -1000000000.0
BF16 = jnp.bfloat16
F32 = jnp.float32
LOG2E = math.log2(math.e)
TOGETHER = 4
PAD = 32


def nn(a, b):
    return lax.dot_general(a, b, (((1,), (0,)), ((), ())), preferred_element_type=F32)


def nt(a, b):
    return lax.dot_general(a, b, (((1,), (1,)), ((), ())), preferred_element_type=F32)


def tn(a, b):
    return lax.dot_general(a, b, (((0,), (0,)), ((), ())), preferred_element_type=F32)


def greet(barrier, devices):
    for device in devices:
        pl.semaphore_signal(
            barrier, inc=1, device_id=device, device_id_type=pl.DeviceIdType.MESH
        )


def remote(src, dst, sems, slot, device):
    return pltpu.make_async_remote_copy(
        src_ref=src,
        dst_ref=dst,
        send_sem=sems.at[0, slot],
        recv_sem=sems.at[1, slot],
        device_id=device,
        device_id_type=pl.DeviceIdType.MESH,
    )


def fused_kernel(
    ranges,
    offsets_ref,
    wtoken_ref,
    padding_ref,
    act_hbm,
    grad_hbm,
    pair_hbm,
    token_ref,
    wq_ref,
    wk_ref,
    wv_ref,
    wg_ref,
    wo_ref,
    wpair_ref,
    ga_hbm,
    pair_out_hbm,
    total_ref,
    act_ref,
    grad_ref,
    pair_ref,
    before_ref,
    after_ref,
    code_scr,
    code_before,
    code_after,
    k_scr,
    v_scr,
    q_scr,
    da_scr,
    gate_scr,
    gyg_scr,
    dqg_scr,
    gated_scr,
    dk_scr,
    dv_scr,
    pw_scr,
    tok_scr,
    wpair_scr,
    key_code_scr,
    query_code_scr,
    mine_ref,
    theirs_ref,
    got,
    from_lower,
    from_upper,
    sums_ref,
    got_half,
    part_b,
    slots,
    starts_ref,
    load_sems,
    store_sems,
    halo_sems,
    edge_sems,
    core_sems,
    scatter_sems,
    gather_sems,
):
    me = lax.axis_index("atoms")
    core = lax.axis_index("samples")
    other = 1 - core
    samples, atoms, channels = act_ref.shape
    windows = pair_ref.shape[0]
    rows = atoms // windows
    span = before_ref.shape[1]
    wide = atoms + 2 * span
    pair_channels = wpair_ref.shape[1]
    heads = wpair_ref.shape[0]
    head_dim = channels // heads
    scale = 1.0 / math.sqrt(head_dim)
    stack = heads * rows
    half_rows = rows // 2
    chunk = part_b.shape[1]
    half = ranges * chunk
    has_lower, has_upper = me > 0, me < ranges - 1
    lower, upper, peer = {"atoms": me - 1}, {"atoms": me + 1}, {"samples": other}
    everyone = [{"atoms": lax.rem(me + d, ranges)} for d in range(1, ranges)]

    barrier = pltpu.get_barrier_semaphore()
    greet(barrier, [peer] + everyone)
    load_act = pltpu.make_async_copy(act_hbm, act_ref, load_sems.at[0])
    load_grad = pltpu.make_async_copy(grad_hbm, grad_ref, load_sems.at[1])
    load_pair = pltpu.make_async_copy(pair_hbm, pair_ref, load_sems.at[2])
    load_act.start()
    load_grad.start()
    load_pair.start()

    code_rows = atoms // span
    live_end = atoms - padding_ref[0]
    lane_at = lax.broadcasted_iota(jnp.int32, (1, span), 1)
    for r in range(code_rows):
        code_scr[r] = jnp.where(lane_at + r * span < live_end, token_ref[r : r + 1, :] + 1, 0)

    pl.semaphore_wait(barrier, ranges)
    halo_up = [
        remote(act_hbm.at[:, pl.ds(atoms - span, span)], before_ref, halo_sems, 0, upper),
        remote(code_scr.at[code_rows - 1], code_before, halo_sems, 1, upper),
    ]
    halo_down = [
        remote(act_hbm.at[:, pl.ds(0, span)], after_ref, halo_sems, 2, lower),
        remote(code_scr.at[0], code_after, halo_sems, 3, lower),
    ]

    @pl.when(has_upper)
    def _():
        for copy in halo_up:
            copy.start()

    @pl.when(has_lower)
    def _():
        for copy in halo_down:
            copy.start()

    @pl.when(jnp.logical_not(has_lower))
    def _():
        before_ref[...] = jnp.zeros_like(before_ref)
        code_before[...] = jnp.zeros_like(code_before)

    @pl.when(jnp.logical_not(has_upper))
    def _():
        after_ref[...] = jnp.zeros_like(after_ref)
        code_after[...] = jnp.zeros_like(code_after)

    def code_column(first, row):
        column = jnp.broadcast_to(row.astype(F32), (stack, span)).T
        key_code_scr[first : first + span, :] = column

    lane_row = lax.broadcasted_iota(jnp.int32, (pair_channels, stack), 1) % rows
    lane_head = lax.broadcasted_iota(jnp.int32, (pair_channels, stack), 1) // rows
    wpair_values = wpair_ref[...].astype(F32).T
    wpair_rows = jnp.zeros((pair_channels, stack), F32)
    wtoken_row = jnp.zeros((1, stack), F32)
    for h in range(heads):
        wpair_rows = jnp.where(lane_head == h, wpair_values[:, h : h + 1], wpair_rows)
        wtoken_row = jnp.where(lane_head[0:1] == h, wtoken_ref[h], wtoken_row)
    for i in range(rows):
        wpair_scr[i * pair_channels : (i + 1) * pair_channels, :] = jnp.where(
            lane_row == i, wpair_rows, 0.0
        ).astype(BF16)
    for r in range(code_rows):
        code_column(span + r * span, code_scr[r])
        tokens = (token_ref[r : r + 1, :] + 1).astype(F32)
        for u in range(span // rows):
            piece = tokens[:, u * rows : (u + 1) * rows]
            query_code_scr[r * (span // rows) + u] = jnp.concatenate([piece] * heads, axis=1)
    pw_scr[...] = jnp.zeros_like(pw_scr)
    tok_scr[...] = jnp.zeros_like(tok_scr)
    sums_ref[...] = jnp.zeros_like(sums_ref)
    anchor = me * atoms
    last_start = ranges * atoms - span
    for w in range(windows):
        starts_ref[w] = (
            jnp.clip(anchor + w * rows + offsets_ref[w], 0, last_start) - anchor + span
        )

    load_act.wait()
    load_grad.wait()
    slot = span + PAD

    def project(s, carry):
        own = act_ref[s]
        q_scr[s] = (nn(own, wq_ref[...]) * (scale * LOG2E)).astype(BF16)
        gate = jax.nn.sigmoid(nn(own, wg_ref[...]))
        gated_gy = nt(grad_ref[s], wo_ref[...]) * gate
        gate_scr[s] = gate
        da_scr[s] = gated_gy.astype(BF16)
        gyg_scr[s] = gated_gy * (1.0 - gate)
        k_scr[s, span : span + atoms, :] = nn(own, wk_ref[...]).astype(BF16).astype(F32)
        v_scr[s, span : span + atoms, :] = nn(own, wv_ref[...]).astype(BF16).astype(F32)
        blank = jnp.zeros((PAD, channels), F32)
        for w in range(windows + 1):
            dk_scr[s, w * slot : w * slot + PAD, :] = blank
            dv_scr[s, w * slot : w * slot + PAD, :] = blank
        return carry

    lax.fori_loop(0, samples, project, 0)
    load_pair.wait()

    row_head = lax.broadcasted_iota(jnp.int32, (stack, channels), 0) // rows
    column_head = lax.broadcasted_iota(jnp.int32, (stack, channels), 1) // head_dim
    head_mask = jnp.where(row_head == column_head, 1.0, 0.0).astype(BF16)
    lane = lax.broadcasted_iota(jnp.int32, (rows, channels), 1) // head_dim
    head_is = [lane == h for h in range(heads)]
    first_mine = core == 0

    def spread(x):
        return jnp.concatenate([x] * heads, axis=0) * head_mask

    def collect(x):
        out = x[0:rows]
        for h in range(1, heads):
            out = jnp.where(head_is[h], x[h * rows : (h + 1) * rows], out)
        return out

    def attend(block):
        ws = [block * TOGETHER + u for u in range(TOGETHER)]
        mine_rows = [pl.ds(pl.multiple_of(w * rows, rows), rows) for w in ws]
        key_rows = [pl.ds(starts_ref[w], span) for w in ws]
        slot_rows = [pl.ds(pl.multiple_of(w * slot + PAD, 8), span) for w in ws]
        sames, biases = [], []
        for u, w in enumerate(ws):
            key_code = key_code_scr[key_rows[u], :]
            same = key_code == query_code_scr[w]
            bias = (tn(pair_ref[w], wpair_scr[...]) + jnp.where(same, wtoken_row, 0.0)) * LOG2E
            biases.append(jnp.where(key_code > 0.0, bias, MASKED))
            sames.append(same)
        units = [(u, s) for u in range(TOGETHER) for s in range(samples)]
        keys = [k_scr[s, key_rows[u], :].astype(BF16) for u, s in units]
        values = [v_scr[s, key_rows[u], :].astype(BF16) for u, s in units]
        qm = [spread(q_scr[s, mine_rows[u], :]) for u, s in units]
        dam = [spread(da_scr[s, mine_rows[u], :]) for u, s in units]
        scores = [nt(k, q) + biases[u] for k, q, (u, s) in zip(keys, qm, units)]
        dprobs = [nt(v, d) for v, d in zip(values, dam)]
        tops = [jnp.max(x, axis=0, keepdims=True) for x in scores]
        exps = [jnp.exp2(x - t) for x, t in zip(scores, tops)]
        probs = [e * (1.0 / jnp.sum(e, axis=0, keepdims=True)) for e in exps]
        probs_b = [p.astype(BF16) for p in probs]
        for (u, s), p, d in zip(units, probs_b, dam):
            dv_scr[s, slot_rows[u], :] = nn(p, d)
        ds = [p * (d - jnp.sum(p * d, axis=0, keepdims=True)) for p, d in zip(probs, dprobs)]
        ds_b = [d.astype(BF16) for d in ds]
        for (u, s), d, q in zip(units, ds_b, qm):
            dk_scr[s, slot_rows[u], :] = nn(d, q)
        for (u, s), p, v in zip(units, probs_b, values):
            a = collect(tn(p, v))
            gated_scr[s, mine_rows[u], :] = (gate_scr[s, mine_rows[u], :] * a).astype(BF16)
            dqg_scr[s, mine_rows[u], channels:] = (gyg_scr[s, mine_rows[u], :] * a).astype(BF16)
        for (u, s), d, k in zip(units, ds_b, keys):
            dqg_scr[s, mine_rows[u], 0:channels] = (collect(tn(d, k)) * scale).astype(BF16)
        for u, w in enumerate(ws):
            of_window = [d for d, unit in zip(ds, units) if unit[0] == u]
            total = of_window[0]
            for d in of_window[1:]:
                total = total + d
            tok_scr[...] += jnp.where(sames[u], total, 0.0)
            pw_scr[...] += nn(pair_ref[w], total.astype(BF16))
            turned = total.T
            for h in range(heads):
                low = turned[h * rows : h * rows + half_rows]
                high = turned[h * rows + half_rows : (h + 1) * rows]
                at = slice(h * half_rows, (h + 1) * half_rows)
                mine_ref[w, at, :] = jnp.where(first_mine, low, high)
                theirs_ref[w, at, :] = jnp.where(first_mine, high, low).astype(BF16)

    def gather_rows(s, b):
        dk, dv = None, None
        for w in range(max(0, b - 2 * span // rows), min(b, windows - 1) + 1):
            shift = jnp.clip(b * rows - starts_ref[w], -PAD, span)
            at = pl.ds(w * slot + PAD + shift, rows)
            k, v = dk_scr[s, at, :], dv_scr[s, at, :]
            dk, dv = (k, v) if dk is None else (dk + k, dv + v)
        return dk * (1.0 / LOG2E), dv

    halo_blocks = span // rows
    own_blocks = atoms // rows

    def project_halo(s, carry):
        for ref, first in ((before_ref, 0), (after_ref, span + atoms)):
            k_scr[s, first : first + span, :] = nn(ref[s], wk_ref[...]).astype(BF16).astype(F32)
            v_scr[s, first : first + span, :] = nn(ref[s], wv_ref[...]).astype(BF16).astype(F32)
        return carry

    edge_up = remote(after_ref, from_lower, edge_sems, 0, upper)
    edge_down = remote(before_ref, from_upper, edge_sems, 1, lower)

    def halo_gradient(s, carry):
        c = channels
        for first, ref in ((0, before_ref), (halo_blocks + own_blocks, after_ref)):
            parts = [gather_rows(s, b) for b in range(first, first + halo_blocks)]
            dkv = jnp.concatenate(
                [jnp.concatenate([p[i] for p in parts], axis=0).astype(BF16) for i in (0, 1)],
                axis=1,
            )
            weights = jnp.concatenate([wk_ref[...], wv_ref[...]], axis=1)
            from_kv = tn(ref[s], dkv)
            sums_ref[c : 2 * c, :] += from_kv[:, 0:c]
            sums_ref[2 * c : 3 * c, :] += from_kv[:, c:]
            ref[s] = nt(dkv, weights).astype(BF16)
        return carry

    blocks = windows // TOGETHER
    early = blocks - 2

    def step(it, carry):
        @pl.when(it == early)
        def _():
            @pl.when(has_upper)
            def _():
                for copy in halo_down:
                    copy.wait_recv()

            @pl.when(has_lower)
            def _():
                for copy in halo_up:
                    copy.wait_recv()

            code_column(0, code_before[...])
            code_column(span + atoms, code_after[...])
            lax.fori_loop(0, samples, project_halo, 0)

        block = jnp.where(
            it < early,
            it + 1,
            jnp.where(it == early, 0, blocks - 1),
        )
        attend(block)
        return carry

    lax.fori_loop(0, blocks, step, 0)
    pair_copy = remote(theirs_ref, got, core_sems, 1, peer)
    pair_copy.start()
    lax.fori_loop(0, samples, halo_gradient, 0)

    @pl.when(has_upper)
    def _():
        edge_up.start()

    @pl.when(has_lower)
    def _():
        edge_down.start()

    def weight_gradients(s, carry):
        for b in range(halo_blocks, halo_blocks + own_blocks):
            dk, dv = gather_rows(s, b)
            k_scr[s, b * rows : (b + 1) * rows, :] = dk
            v_scr[s, b * rows : (b + 1) * rows, :] = dv
        c = channels
        own = slice(span, span + atoms)
        grads = jnp.concatenate(
            [
                dqg_scr[s, :, 0:c],
                k_scr[s, own, :].astype(BF16),
                v_scr[s, own, :].astype(BF16),
                dqg_scr[s, :, c:],
            ],
            axis=1,
        )
        sums = tn(act_ref[s], grads)
        for n in range(4):
            sums_ref[n * c : (n + 1) * c, :] += sums[:, n * c : (n + 1) * c]
        sums_ref[4 * c : 5 * c, :] += tn(gated_scr[s], grad_ref[s])
        return carry

    lax.fori_loop(0, samples, weight_gradients, 0)
    shape = pw_scr.shape
    at_row = lax.broadcasted_iota(jnp.int32, shape, 0) // pair_channels
    at_col = lax.broadcasted_iota(jnp.int32, shape, 1) % rows
    diagonal = jnp.where(at_row == at_col, pw_scr[...], 0.0)
    base = 5 * channels
    small_rows = 8 * pl.cdiv(pair_channels + 1, 8)
    sums_ref[base : base + pair_channels, :] = jnp.sum(
        diagonal.reshape(rows, pair_channels, stack), axis=0
    )
    sums_ref[base + pair_channels : base + pair_channels + 1, :] = jnp.sum(
        tok_scr[...], axis=0, keepdims=True
    )

    half_copy = remote(
        sums_ref.at[pl.ds(pl.multiple_of(other * half, 8), half)], got_half, core_sems, 0, peer
    )
    half_copy.start()

    inner = slice(span, atoms - span)

    def own_gradient(s, carry):
        own = slice(span, span + atoms)
        dq = dqg_scr[s, :, 0:channels]
        dg = dqg_scr[s, :, channels:]
        grads = jnp.concatenate(
            [dq, k_scr[s, own, :].astype(BF16), v_scr[s, own, :].astype(BF16), dg], axis=1
        )
        weights = jnp.concatenate([wq_ref[...], wk_ref[...], wv_ref[...], wg_ref[...]], axis=1)
        ga = nt(grads, weights)
        dk_scr[s, 0:span, :] = ga[0:span]
        dk_scr[s, span : 2 * span, :] = ga[atoms - span :]
        q_scr[s, inner, :] = ga[inner].astype(BF16)
        return carry

    lax.fori_loop(0, 2, own_gradient, 0)
    half_copy.wait_recv()
    own_half = pl.ds(pl.multiple_of(core * half, 16), half)
    small = base % half
    got_half[...] += sums_ref[own_half, :]
    rest = got_half[small : small + small_rows, :]
    rest = rest - rest.astype(BF16).astype(F32)
    low_rows = slice(small + small_rows, small + 2 * small_rows)
    got_half[low_rows, :] = jnp.where(core == base // half, rest, got_half[low_rows, :])
    part_b[...] = got_half[...].reshape(part_b.shape).astype(BF16)
    scatter = []
    for d in range(1, ranges):
        target = lax.rem(me + d, ranges)
        copy = remote(part_b.at[target], slots.at[d - 1], scatter_sems, d - 1, everyone[d - 1])
        copy.start()
        scatter.append(copy)
    lax.fori_loop(2, samples, own_gradient, 0)

    lane_out = lax.broadcasted_iota(jnp.int32, (pair_channels, heads * half_rows), 1)
    spread_rows = jnp.zeros((pair_channels, heads * half_rows), F32)
    for h in range(heads):
        spread_rows = jnp.where(lane_out // half_rows == h, wpair_values[:, h : h + 1], spread_rows)
    weight = jnp.concatenate(
        [
            jnp.where(lane_out % half_rows == i, spread_rows, 0.0).astype(BF16)
            for i in range(half_rows)
        ],
        axis=0,
    )
    for copy in scatter:
        copy.wait_recv()
    chunk_total = got_half[pl.ds(pl.multiple_of(me * chunk, 8), chunk), :]
    for d in range(1, ranges):
        chunk_total = chunk_total + slots[d - 1].astype(F32)
    place = pl.ds(pl.multiple_of(core * half + me * chunk, 16), chunk)
    total_ref[place, :] = chunk_total.astype(BF16)
    gather = []
    for d in range(1, ranges):
        copy = remote(
            total_ref.at[place], total_ref.at[place], gather_sems, d - 1, everyone[d - 1]
        )
        copy.start()
        gather.append(copy)

    pair_copy.wait_recv()
    out_rows = half_rows * pair_channels

    def pair_gradient(w, carry):
        both = mine_ref[w] + got[w].astype(F32)
        high = both.astype(BF16)
        low = (both - high.astype(F32)).astype(BF16)
        pair_ref[w, 0:out_rows, :] = (nn(weight, high) + nn(weight, low)).astype(BF16)
        return carry

    lax.fori_loop(0, windows, pair_gradient, 0, unroll=math.gcd(5, windows))
    store_pair = pltpu.make_async_copy(
        pair_ref.at[:, pl.ds(0, out_rows)], pair_out_hbm, store_sems.at[0]
    )
    store_pair.start()

    for copy in gather:
        copy.wait_recv()
    last_copy = remote(
        total_ref.at[own_half], total_ref.at[own_half], core_sems, 2, peer
    )
    last_copy.start()

    @pl.when(has_lower)
    def _():
        edge_down.wait_send()
        edge_up.wait_recv()

    @pl.when(has_upper)
    def _():
        edge_up.wait_send()
        edge_down.wait_recv()

    @pl.when(jnp.logical_not(has_lower))
    def _():
        from_lower[...] = jnp.zeros_like(from_lower)

    @pl.when(jnp.logical_not(has_upper))
    def _():
        from_upper[...] = jnp.zeros_like(from_upper)

    def add_edges(s, carry):
        q_scr[s, 0:span, :] = (dk_scr[s, 0:span, :] + from_lower[s].astype(F32)).astype(BF16)
        q_scr[s, atoms - span : atoms, :] = (
            dk_scr[s, span : 2 * span, :] + from_upper[s].astype(F32)
        ).astype(BF16)
        return carry

    lax.fori_loop(0, samples, add_edges, 0)
    store_act = pltpu.make_async_copy(q_scr, ga_hbm, store_sems.at[1])
    store_act.start()

    @pl.when(has_upper)
    def _():
        for copy in halo_up:
            copy.wait_send()

    @pl.when(has_lower)
    def _():
        for copy in halo_down:
            copy.wait_send()

    half_copy.wait_send()
    pair_copy.wait_send()
    for copy in scatter + gather:
        copy.wait_send()
    last_copy.wait()
    store_pair.wait()
    store_act.wait()


def finish_kernel(
    shapes,
    ga_ref,
    gp_ref,
    total_ref,
    ga_out,
    gp_out,
    weights_out,
    pair_weight_out,
    token_weight_out,
    ga_scr,
    gp_scr,
    total_scr,
    weights_scr,
    load_sems,
    store_sems,
    small_sems,
):
    pair_channels, heads, small_rows, pieces = shapes
    load_total = pltpu.make_async_copy(total_ref, total_scr, small_sems.at[0])
    load_total.start()
    moves = []
    for n, (src, held, dst) in enumerate(((ga_ref, ga_scr, ga_out), (gp_ref, gp_scr, gp_out))):
        size = src.shape[0] // pieces
        for p in range(pieces):
            at = pl.ds(p * size, size)
            load = pltpu.make_async_copy(src.at[at], held.at[at], load_sems.at[n, p])
            store = pltpu.make_async_copy(held.at[at], dst.at[at], store_sems.at[n, p])
            moves.append((load, store))
    for load, _ in moves:
        load.start()
    base = weights_out.shape[0]
    channels = weights_out.shape[1]
    load_total.wait()
    weights_scr[...] = total_scr[0:base, :].astype(F32)
    store_weights = pltpu.make_async_copy(weights_scr, weights_out, small_sems.at[1])
    store_weights.start()
    for load, store in moves:
        load.wait()
        store.start()
    tail = total_scr[base : base + 2 * small_rows, :].astype(F32)
    turned = (tail[0:small_rows] + tail[small_rows:]).T
    by_head = jnp.sum(turned.reshape(heads, channels // heads, small_rows), axis=1)
    pair_weight_out[...] = by_head[:, 0:pair_channels]
    for h in range(heads):
        token_weight_out[h] = by_head[h, pair_channels]
    store_weights.wait()
    for _, store in moves:
        store.wait()


def per_device(
    act,
    grad_out,
    pair,
    w_query,
    w_key,
    w_value,
    w_gate,
    w_out,
    w_pair,
    w_token,
    offsets,
    atom_token,
    padding,
):
    samples, atoms, channels = act.shape
    windows = offsets.shape[0]
    rows = atoms // windows
    pair_channels, heads = w_pair.shape
    span = pair.shape[-1]
    stack = heads * rows
    half = rows // 2
    ranges = lax.axis_size("atoms")
    wide = atoms + 2 * span
    vmem = pl.BlockSpec(memory_space=pltpu.VMEM)
    smem = pl.BlockSpec(memory_space=pltpu.SMEM)
    anywhere = pl.BlockSpec(memory_space=pl.ANY)
    small_rows = 8 * pl.cdiv(pair_channels + 1, 8)
    chunk = 16 * pl.cdiv(5 * channels + 2 * small_rows, 32 * ranges)
    sum_rows = 2 * ranges * chunk

    def kernel(*refs):
        fused_kernel(ranges, *refs)

    edge = pltpu.VMEM((samples, span, channels), BF16)
    slot_rows = windows * (span + PAD) + PAD
    grad_act, grad_pair, total = pl.pallas_call(
        kernel,
        out_shape=(
            jax.ShapeDtypeStruct((samples, atoms, channels), BF16),
            jax.ShapeDtypeStruct((windows, half * pair_channels, span), BF16),
            jax.ShapeDtypeStruct((sum_rows, channels), BF16),
        ),
        in_specs=[smem] * 3 + [anywhere] * 3 + [vmem] * 7,
        out_specs=(anywhere, anywhere, vmem),
        scratch_shapes=[
            pltpu.VMEM((samples, atoms, channels), BF16),
            pltpu.VMEM((samples, atoms, channels), BF16),
            pltpu.VMEM((windows, rows * pair_channels, span), BF16),
            edge,
            edge,
            pltpu.VMEM((atoms // span, 1, span), jnp.int32),
            pltpu.VMEM((1, span), jnp.int32),
            pltpu.VMEM((1, span), jnp.int32),
            pltpu.VMEM((samples, wide, channels), F32),
            pltpu.VMEM((samples, wide, channels), F32),
            pltpu.VMEM((samples, atoms, channels), BF16),
            pltpu.VMEM((samples, atoms, channels), BF16),
            pltpu.VMEM((samples, atoms, channels), F32),
            pltpu.VMEM((samples, atoms, channels), F32),
            pltpu.VMEM((samples, atoms, 2 * channels), BF16),
            pltpu.VMEM((samples, atoms, channels), BF16),
            pltpu.VMEM((samples, slot_rows, channels), F32),
            pltpu.VMEM((samples, slot_rows, channels), F32),
            pltpu.VMEM((rows * pair_channels, stack), F32),
            pltpu.VMEM((span, stack), F32),
            pltpu.VMEM((rows * pair_channels, stack), BF16),
            pltpu.VMEM((wide, stack), F32),
            pltpu.VMEM((windows, 1, stack), F32),
            pltpu.VMEM((windows, heads * half, span), F32),
            pltpu.VMEM((windows, heads * half, span), BF16),
            pltpu.VMEM((windows, heads * half, span), BF16),
            edge,
            edge,
            pltpu.VMEM((sum_rows, channels), F32),
            pltpu.VMEM((ranges * chunk, channels), F32),
            pltpu.VMEM((ranges, chunk, channels), BF16),
            pltpu.VMEM((ranges - 1, chunk, channels), BF16),
            pltpu.SMEM((windows,), jnp.int32),
            pltpu.SemaphoreType.DMA((3,)),
            pltpu.SemaphoreType.DMA((2,)),
            pltpu.SemaphoreType.DMA((2, 4)),
            pltpu.SemaphoreType.DMA((2, 2)),
            pltpu.SemaphoreType.DMA((2, 3)),
            pltpu.SemaphoreType.DMA((2, ranges - 1)),
            pltpu.SemaphoreType.DMA((2, ranges - 1)),
        ],
        compiler_params=pltpu.CompilerParams(
            collective_id=0, has_side_effects=True, vmem_limit_bytes=63 * 1024 * 1024
        ),
        name="fused",
    )(
        offsets,
        w_token,
        padding,
        act,
        grad_out,
        pair.reshape(windows, rows * pair_channels, span),
        atom_token.reshape(atoms // span, span),
        w_query,
        w_key,
        w_value,
        w_gate,
        w_out,
        w_pair.T,
    )

    pieces = math.gcd(4, math.gcd(samples, windows))
    base = 5 * channels

    def last_kernel(*refs):
        finish_kernel((pair_channels, heads, small_rows, pieces), *refs)

    grad_act, grad_pair, weights, pair_weight, grad_token_weight = pl.pallas_call(
        last_kernel,
        out_shape=(
            jax.ShapeDtypeStruct(grad_act.shape, BF16),
            jax.ShapeDtypeStruct(grad_pair.shape, BF16),
            jax.ShapeDtypeStruct((base, channels), F32),
            jax.ShapeDtypeStruct((heads, pair_channels), F32),
            jax.ShapeDtypeStruct((heads,), F32),
        ),
        in_specs=[anywhere] * 3,
        out_specs=(anywhere, anywhere, anywhere, vmem, smem),
        scratch_shapes=[
            pltpu.VMEM(grad_act.shape, BF16),
            pltpu.VMEM(grad_pair.shape, BF16),
            pltpu.VMEM(total.shape, BF16),
            pltpu.VMEM((base, channels), F32),
            pltpu.SemaphoreType.DMA((2, pieces)),
            pltpu.SemaphoreType.DMA((2, pieces)),
            pltpu.SemaphoreType.DMA((2,)),
        ],
        name="finish",
    )(grad_act, grad_pair, total)

    grad_weights = weights.reshape(5, channels, channels)
    grad_pair_weight = pair_weight.T
    grad_pair = grad_pair.reshape(windows, half, pair_channels, span)
    return (grad_act, grad_pair, grad_weights, grad_pair_weight, grad_token_weight)


def solution(mesh):
    in_specs = (
        P("samples", ("groups", "atoms"), None),
        P("samples", ("groups", "atoms"), None),
        P(("groups", "atoms"), None, None, None),
        P(),
        P(),
        P(),
        P(),
        P(),
        P(),
        P(),
        P(("groups", "atoms")),
        P(("groups", "atoms")),
        P(("groups", "atoms")),
    )
    out_specs = (
        P("samples", ("groups", "atoms"), None),
        P(("groups", "atoms"), "samples", None, None),
        P("groups", None, None),
        P("groups", None),
        P("groups"),
    )
    return jax.shard_map(
        per_device, mesh=mesh, in_specs=in_specs, out_specs=out_specs, check_vma=False
    )
```

```python
import math

import jax
import jax.numpy as jnp
from jax import lax
from jax.experimental import pallas as pl
from jax.experimental.pallas import tpu as pltpu
from jax.sharding import PartitionSpec as P

MASKED = -1000000000.0
BF16 = jnp.bfloat16
F32 = jnp.float32
LOG2E = math.log2(math.e)
TOGETHER = 4
PAD = 32


def nn(a, b):
    return lax.dot_general(a, b, (((1,), (0,)), ((), ())), preferred_element_type=F32)


def nt(a, b):
    return lax.dot_general(a, b, (((1,), (1,)), ((), ())), preferred_element_type=F32)


def tn(a, b):
    return lax.dot_general(a, b, (((0,), (0,)), ((), ())), preferred_element_type=F32)


def greet(barrier, devices):
    for device in devices:
        pl.semaphore_signal(
            barrier, inc=1, device_id=device, device_id_type=pl.DeviceIdType.MESH
        )


def remote(src, dst, sems, slot, device):
    return pltpu.make_async_remote_copy(
        src_ref=src,
        dst_ref=dst,
        send_sem=sems.at[0, slot],
        recv_sem=sems.at[1, slot],
        device_id=device,
        device_id_type=pl.DeviceIdType.MESH,
    )


def fused_kernel(
    ranges,
    offsets_ref,
    wtoken_ref,
    padding_ref,
    act_hbm,
    grad_hbm,
    pair_hbm,
    token_ref,
    wq_ref,
    wk_ref,
    wv_ref,
    wg_ref,
    wo_ref,
    wpair_ref,
    ga_hbm,
    pair_out_hbm,
    total_ref,
    act_ref,
    grad_ref,
    pair_ref,
    before_ref,
    after_ref,
    code_scr,
    code_before,
    code_after,
    k_scr,
    v_scr,
    q_scr,
    da_scr,
    gate_scr,
    gyg_scr,
    dqg_scr,
    gated_scr,
    dk_scr,
    dv_scr,
    pw_scr,
    tok_scr,
    wpair_scr,
    key_code_scr,
    query_code_scr,
    mine_ref,
    theirs_ref,
    got,
    from_lower,
    from_upper,
    sums_ref,
    got_half,
    part_b,
    slots,
    starts_ref,
    load_sems,
    store_sems,
    halo_sems,
    edge_sems,
    core_sems,
    scatter_sems,
    gather_sems,
):
    me = lax.axis_index("atoms")
    core = lax.axis_index("samples")
    other = 1 - core
    samples, atoms, channels = act_ref.shape
    windows = pair_ref.shape[0]
    rows = atoms // windows
    span = before_ref.shape[1]
    wide = atoms + 2 * span
    pair_channels = wpair_ref.shape[1]
    heads = wpair_ref.shape[0]
    head_dim = channels // heads
    scale = 1.0 / math.sqrt(head_dim)
    stack = heads * rows
    half_rows = rows // 2
    chunk = part_b.shape[1]
    half = ranges * chunk
    unroll = math.gcd(4, samples)
    has_lower, has_upper = me > 0, me < ranges - 1
    lower, upper, peer = {"atoms": me - 1}, {"atoms": me + 1}, {"samples": other}
    everyone = [{"atoms": lax.rem(me + d, ranges)} for d in range(1, ranges)]

    barrier = pltpu.get_barrier_semaphore()
    greet(barrier, [peer] + everyone)
    load_act = pltpu.make_async_copy(act_hbm, act_ref, load_sems.at[0])
    load_grad = pltpu.make_async_copy(grad_hbm, grad_ref, load_sems.at[1])
    load_pair = pltpu.make_async_copy(pair_hbm, pair_ref, load_sems.at[2])
    load_act.start()
    load_grad.start()
    load_pair.start()

    code_rows = atoms // span
    live_end = atoms - padding_ref[0]
    lane_at = lax.broadcasted_iota(jnp.int32, (1, span), 1)
    for r in range(code_rows):
        code_scr[r] = jnp.where(lane_at + r * span < live_end, token_ref[r : r + 1, :] + 1, 0)

    pl.semaphore_wait(barrier, ranges)
    halo_up = [
        remote(act_hbm.at[:, pl.ds(atoms - span, span)], before_ref, halo_sems, 0, upper),
        remote(code_scr.at[code_rows - 1], code_before, halo_sems, 1, upper),
    ]
    halo_down = [
        remote(act_hbm.at[:, pl.ds(0, span)], after_ref, halo_sems, 2, lower),
        remote(code_scr.at[0], code_after, halo_sems, 3, lower),
    ]

    @pl.when(has_upper)
    def _():
        for copy in halo_up:
            copy.start()

    @pl.when(has_lower)
    def _():
        for copy in halo_down:
            copy.start()

    @pl.when(jnp.logical_not(has_lower))
    def _():
        before_ref[...] = jnp.zeros_like(before_ref)
        code_before[...] = jnp.zeros_like(code_before)

    @pl.when(jnp.logical_not(has_upper))
    def _():
        after_ref[...] = jnp.zeros_like(after_ref)
        code_after[...] = jnp.zeros_like(code_after)

    def code_column(first, row):
        column = jnp.broadcast_to(row.astype(F32), (stack, span)).T
        key_code_scr[first : first + span, :] = column

    lane_row = lax.broadcasted_iota(jnp.int32, (pair_channels, stack), 1) % rows
    lane_head = lax.broadcasted_iota(jnp.int32, (pair_channels, stack), 1) // rows
    wpair_values = wpair_ref[...].astype(F32).T
    wpair_rows = jnp.zeros((pair_channels, stack), F32)
    wtoken_row = jnp.zeros((1, stack), F32)
    for h in range(heads):
        wpair_rows = jnp.where(lane_head == h, wpair_values[:, h : h + 1], wpair_rows)
        wtoken_row = jnp.where(lane_head[0:1] == h, wtoken_ref[h], wtoken_row)
    for i in range(rows):
        wpair_scr[i * pair_channels : (i + 1) * pair_channels, :] = jnp.where(
            lane_row == i, wpair_rows, 0.0
        ).astype(BF16)
    for r in range(code_rows):
        code_column(span + r * span, code_scr[r])
        tokens = (token_ref[r : r + 1, :] + 1).astype(F32)
        for u in range(span // rows):
            piece = tokens[:, u * rows : (u + 1) * rows]
            query_code_scr[r * (span // rows) + u] = jnp.concatenate([piece] * heads, axis=1)
    pw_scr[...] = jnp.zeros_like(pw_scr)
    tok_scr[...] = jnp.zeros_like(tok_scr)
    sums_ref[...] = jnp.zeros_like(sums_ref)
    anchor = me * atoms
    last_start = ranges * atoms - span
    for w in range(windows):
        starts_ref[w] = (
            jnp.clip(anchor + w * rows + offsets_ref[w], 0, last_start) - anchor + span
        )

    load_act.wait()
    load_grad.wait()
    slot = span + PAD

    def project(s, carry):
        own = act_ref[s]
        q_scr[s] = (nn(own, wq_ref[...]) * (scale * LOG2E)).astype(BF16)
        gate = jax.nn.sigmoid(nn(own, wg_ref[...]))
        gated_gy = nt(grad_ref[s], wo_ref[...]) * gate
        gate_scr[s] = gate
        da_scr[s] = gated_gy.astype(BF16)
        gyg_scr[s] = gated_gy * (1.0 - gate)
        k_scr[s, span : span + atoms, :] = nn(own, wk_ref[...]).astype(BF16).astype(F32)
        v_scr[s, span : span + atoms, :] = nn(own, wv_ref[...]).astype(BF16).astype(F32)
        blank = jnp.zeros((PAD, channels), F32)
        for w in range(windows + 1):
            dk_scr[s, w * slot : w * slot + PAD, :] = blank
            dv_scr[s, w * slot : w * slot + PAD, :] = blank
        return carry

    lax.fori_loop(0, samples, project, 0, unroll=unroll)
    load_pair.wait()

    row_head = lax.broadcasted_iota(jnp.int32, (stack, channels), 0) // rows
    column_head = lax.broadcasted_iota(jnp.int32, (stack, channels), 1) // head_dim
    head_mask = jnp.where(row_head == column_head, 1.0, 0.0).astype(BF16)
    lane = lax.broadcasted_iota(jnp.int32, (rows, channels), 1) // head_dim
    head_is = [lane == h for h in range(heads)]
    first_mine = core == 0

    def spread(x):
        return jnp.concatenate([x] * heads, axis=0) * head_mask

    def collect(x):
        out = x[0:rows]
        for h in range(1, heads):
            out = jnp.where(head_is[h], x[h * rows : (h + 1) * rows], out)
        return out

    def attend(block):
        ws = [block * TOGETHER + u for u in range(TOGETHER)]
        mine_rows = [pl.ds(pl.multiple_of(w * rows, rows), rows) for w in ws]
        key_rows = [pl.ds(starts_ref[w], span) for w in ws]
        slot_rows = [pl.ds(pl.multiple_of(w * slot + PAD, 8), span) for w in ws]
        sames, biases = [], []
        for u, w in enumerate(ws):
            key_code = key_code_scr[key_rows[u], :]
            same = key_code == query_code_scr[w]
            bias = (tn(pair_ref[w], wpair_scr[...]) + jnp.where(same, wtoken_row, 0.0)) * LOG2E
            biases.append(jnp.where(key_code > 0.0, bias, MASKED))
            sames.append(same)
        units = [(u, s) for u in range(TOGETHER) for s in range(samples)]
        keys = [k_scr[s, key_rows[u], :].astype(BF16) for u, s in units]
        values = [v_scr[s, key_rows[u], :].astype(BF16) for u, s in units]
        qm = [spread(q_scr[s, mine_rows[u], :]) for u, s in units]
        dam = [spread(da_scr[s, mine_rows[u], :]) for u, s in units]
        scores = [nt(k, q) + biases[u] for k, q, (u, s) in zip(keys, qm, units)]
        dprobs = [nt(v, d) for v, d in zip(values, dam)]
        tops = [jnp.max(x, axis=0, keepdims=True) for x in scores]
        exps = [jnp.exp2(x - t) for x, t in zip(scores, tops)]
        probs = [e * (1.0 / jnp.sum(e, axis=0, keepdims=True)) for e in exps]
        probs_b = [p.astype(BF16) for p in probs]
        for (u, s), p, d in zip(units, probs_b, dam):
            dv_scr[s, slot_rows[u], :] = nn(p, d)
        ds = [p * (d - jnp.sum(p * d, axis=0, keepdims=True)) for p, d in zip(probs, dprobs)]
        ds_b = [d.astype(BF16) for d in ds]
        for (u, s), d, q in zip(units, ds_b, qm):
            dk_scr[s, slot_rows[u], :] = nn(d, q)
        for (u, s), p, v in zip(units, probs_b, values):
            a = collect(tn(p, v))
            gated_scr[s, mine_rows[u], :] = (gate_scr[s, mine_rows[u], :] * a).astype(BF16)
            dqg_scr[s, mine_rows[u], channels:] = (gyg_scr[s, mine_rows[u], :] * a).astype(BF16)
        for (u, s), d, k in zip(units, ds_b, keys):
            dqg_scr[s, mine_rows[u], 0:channels] = (collect(tn(d, k)) * scale).astype(BF16)
        for u, w in enumerate(ws):
            of_window = [d for d, unit in zip(ds, units) if unit[0] == u]
            total = of_window[0]
            for d in of_window[1:]:
                total = total + d
            of_token = jnp.where(sames[u], total, 0.0)
            token_sum = of_token if u == 0 else token_sum + of_token
            pw_scr[...] += nn(pair_ref[w], total.astype(BF16))
            turned = total.T
            for h in range(heads):
                low = turned[h * rows : h * rows + half_rows]
                high = turned[h * rows + half_rows : (h + 1) * rows]
                at = slice(h * half_rows, (h + 1) * half_rows)
                mine_ref[w, at, :] = jnp.where(first_mine, low, high)
                theirs_ref[w, at, :] = jnp.where(first_mine, high, low).astype(BF16)
        tok_scr[...] += token_sum

    def gather_rows(s, b):
        dk, dv = None, None
        for w in range(max(0, b - 2 * span // rows), min(b, windows - 1) + 1):
            shift = jnp.clip(b * rows - starts_ref[w], -PAD, span)
            at = pl.ds(w * slot + PAD + shift, rows)
            k, v = dk_scr[s, at, :], dv_scr[s, at, :]
            dk, dv = (k, v) if dk is None else (dk + k, dv + v)
        return dk * (1.0 / LOG2E), dv

    halo_blocks = span // rows
    own_blocks = atoms // rows

    def project_halo(s, carry):
        for ref, first in ((before_ref, 0), (after_ref, span + atoms)):
            k_scr[s, first : first + span, :] = nn(ref[s], wk_ref[...]).astype(BF16).astype(F32)
            v_scr[s, first : first + span, :] = nn(ref[s], wv_ref[...]).astype(BF16).astype(F32)
        return carry

    edge_up = remote(after_ref, from_lower, edge_sems, 0, upper)
    edge_down = remote(before_ref, from_upper, edge_sems, 1, lower)

    def halo_gradient(s, carry):
        c = channels
        for first, ref in ((0, before_ref), (halo_blocks + own_blocks, after_ref)):
            parts = [gather_rows(s, b) for b in range(first, first + halo_blocks)]
            dkv = jnp.concatenate(
                [jnp.concatenate([p[i] for p in parts], axis=0).astype(BF16) for i in (0, 1)],
                axis=1,
            )
            weights = jnp.concatenate([wk_ref[...], wv_ref[...]], axis=1)
            from_kv = tn(ref[s], dkv)
            sums_ref[c : 2 * c, :] += from_kv[:, 0:c]
            sums_ref[2 * c : 3 * c, :] += from_kv[:, c:]
            ref[s] = nt(dkv, weights).astype(BF16)
        return carry

    blocks = windows // TOGETHER
    early = blocks - 2

    def step(it, carry):
        @pl.when(it == early)
        def _():
            @pl.when(has_upper)
            def _():
                for copy in halo_down:
                    copy.wait_recv()

            @pl.when(has_lower)
            def _():
                for copy in halo_up:
                    copy.wait_recv()

            code_column(0, code_before[...])
            code_column(span + atoms, code_after[...])
            lax.fori_loop(0, samples, project_halo, 0, unroll=unroll)

        block = jnp.where(
            it < early,
            it + 1,
            jnp.where(it == early, 0, blocks - 1),
        )
        attend(block)
        return carry

    lax.fori_loop(0, blocks, step, 0)
    pair_copy = remote(theirs_ref, got, core_sems, 1, peer)
    pair_copy.start()
    lax.fori_loop(0, samples, halo_gradient, 0, unroll=unroll)

    @pl.when(has_upper)
    def _():
        edge_up.start()

    @pl.when(has_lower)
    def _():
        edge_down.start()

    shape = pw_scr.shape
    at_row = lax.broadcasted_iota(jnp.int32, shape, 0) // pair_channels
    at_col = lax.broadcasted_iota(jnp.int32, shape, 1) % rows
    diagonal = jnp.where(at_row == at_col, pw_scr[...], 0.0)
    by_channel = jnp.sum(diagonal.reshape(rows, pair_channels, stack), axis=0)
    by_channel = jnp.concatenate(
        [by_channel, jnp.zeros((channels - pair_channels, stack), F32)], axis=0
    )
    by_head = jnp.sum(by_channel.T.reshape(heads, rows, channels), axis=1)
    token_row = jnp.sum(tok_scr[...], axis=0, keepdims=True)
    lanes = lax.broadcasted_iota(jnp.int32, (1, stack), 1)
    by_token = jnp.zeros((1, stack), F32)
    for h in range(heads):
        one = jnp.sum(jnp.where(lanes // rows == h, token_row, 0.0), axis=1, keepdims=True)
        by_token = jnp.where(lanes == h, one, by_token)
    base = 5 * channels
    small_rows = 8 * pl.cdiv(heads + 1, 8)
    sums_ref[base : base + heads, :] = by_head
    sums_ref[base + heads : base + heads + 1, :] = by_token

    def weight_gradients(s, carry):
        for b in range(halo_blocks, halo_blocks + own_blocks):
            dk, dv = gather_rows(s, b)
            k_scr[s, b * rows : (b + 1) * rows, :] = dk
            v_scr[s, b * rows : (b + 1) * rows, :] = dv
        c = channels
        own = slice(span, span + atoms)
        grads = jnp.concatenate(
            [
                dqg_scr[s, :, 0:c],
                k_scr[s, own, :].astype(BF16),
                v_scr[s, own, :].astype(BF16),
                dqg_scr[s, :, c:],
            ],
            axis=1,
        )
        sums = tn(act_ref[s], grads)
        for n in range(4):
            sums_ref[n * c : (n + 1) * c, :] += sums[:, n * c : (n + 1) * c]
        sums_ref[4 * c : 5 * c, :] += tn(gated_scr[s], grad_ref[s])
        return carry

    lax.fori_loop(0, samples, weight_gradients, 0, unroll=unroll)
    half_copy = remote(
        sums_ref.at[pl.ds(pl.multiple_of(other * half, 8), half)], got_half, core_sems, 0, peer
    )
    half_copy.start()

    inner = slice(span, atoms - span)

    def own_gradient(s, carry):
        own = slice(span, span + atoms)
        dq = dqg_scr[s, :, 0:channels]
        dg = dqg_scr[s, :, channels:]
        grads = jnp.concatenate(
            [dq, k_scr[s, own, :].astype(BF16), v_scr[s, own, :].astype(BF16), dg], axis=1
        )
        weights = jnp.concatenate([wq_ref[...], wk_ref[...], wv_ref[...], wg_ref[...]], axis=1)
        ga = nt(grads, weights)
        dk_scr[s, 0:span, :] = ga[0:span]
        dk_scr[s, span : 2 * span, :] = ga[atoms - span :]
        q_scr[s, inner, :] = ga[inner].astype(BF16)
        return carry

    lax.fori_loop(0, 2, own_gradient, 0)
    half_copy.wait_recv()
    own_half = pl.ds(pl.multiple_of(core * half, 16), half)
    small = base % half
    got_half[...] += sums_ref[own_half, :]
    rest = got_half[small : small + small_rows, :]
    rest = rest - rest.astype(BF16).astype(F32)
    low_rows = slice(small + small_rows, small + 2 * small_rows)
    got_half[low_rows, :] = jnp.where(core == base // half, rest, got_half[low_rows, :])
    part_b[...] = got_half[...].reshape(part_b.shape).astype(BF16)
    scatter = []
    for d in range(1, ranges):
        target = lax.rem(me + d, ranges)
        copy = remote(part_b.at[target], slots.at[d - 1], scatter_sems, d - 1, everyone[d - 1])
        copy.start()
        scatter.append(copy)
    lax.fori_loop(2, samples, own_gradient, 0, unroll=math.gcd(3, samples - 2))

    lane_out = lax.broadcasted_iota(jnp.int32, (pair_channels, heads * half_rows), 1)
    spread_rows = jnp.zeros((pair_channels, heads * half_rows), F32)
    for h in range(heads):
        spread_rows = jnp.where(lane_out // half_rows == h, wpair_values[:, h : h + 1], spread_rows)
    weight = jnp.concatenate(
        [
            jnp.where(lane_out % half_rows == i, spread_rows, 0.0).astype(BF16)
            for i in range(half_rows)
        ],
        axis=0,
    )
    for copy in scatter:
        copy.wait_recv()
    chunk_total = got_half[pl.ds(pl.multiple_of(me * chunk, 8), chunk), :]
    for d in range(1, ranges):
        chunk_total = chunk_total + slots[d - 1].astype(F32)
    place = pl.ds(pl.multiple_of(core * half + me * chunk, 16), chunk)
    total_ref[place, :] = chunk_total.astype(BF16)
    gather = []
    for d in range(1, ranges):
        copy = remote(
            total_ref.at[place], total_ref.at[place], gather_sems, d - 1, everyone[d - 1]
        )
        copy.start()
        gather.append(copy)

    pair_copy.wait_recv()
    out_rows = half_rows * pair_channels

    def pair_gradient(w, carry):
        both = mine_ref[w] + got[w].astype(F32)
        high = both.astype(BF16)
        low = (both - high.astype(F32)).astype(BF16)
        pair_ref[w, 0:out_rows, :] = (nn(weight, high) + nn(weight, low)).astype(BF16)
        return carry

    lax.fori_loop(0, windows, pair_gradient, 0, unroll=math.gcd(5, windows))
    store_pair = pltpu.make_async_copy(
        pair_ref.at[:, pl.ds(0, out_rows)], pair_out_hbm, store_sems.at[0]
    )
    store_pair.start()

    for copy in gather:
        copy.wait_recv()
    last_copy = remote(
        total_ref.at[own_half], total_ref.at[own_half], core_sems, 2, peer
    )
    last_copy.start()

    @pl.when(has_lower)
    def _():
        edge_down.wait_send()
        edge_up.wait_recv()

    @pl.when(has_upper)
    def _():
        edge_up.wait_send()
        edge_down.wait_recv()

    @pl.when(jnp.logical_not(has_lower))
    def _():
        from_lower[...] = jnp.zeros_like(from_lower)

    @pl.when(jnp.logical_not(has_upper))
    def _():
        from_upper[...] = jnp.zeros_like(from_upper)

    def add_edges(s, carry):
        q_scr[s, 0:span, :] = (dk_scr[s, 0:span, :] + from_lower[s].astype(F32)).astype(BF16)
        q_scr[s, atoms - span : atoms, :] = (
            dk_scr[s, span : 2 * span, :] + from_upper[s].astype(F32)
        ).astype(BF16)
        return carry

    lax.fori_loop(0, samples, add_edges, 0, unroll=unroll)
    store_act = pltpu.make_async_copy(q_scr, ga_hbm, store_sems.at[1])
    store_act.start()

    @pl.when(has_upper)
    def _():
        for copy in halo_up:
            copy.wait_send()

    @pl.when(has_lower)
    def _():
        for copy in halo_down:
            copy.wait_send()

    half_copy.wait_send()
    pair_copy.wait_send()
    for copy in scatter + gather:
        copy.wait_send()
    last_copy.wait()
    store_pair.wait()
    store_act.wait()


def finish_kernel(
    shapes,
    ga_ref,
    gp_ref,
    total_ref,
    ga_out,
    gp_out,
    weights_out,
    pair_weight_out,
    token_weight_out,
    ga_scr,
    gp_scr,
    total_scr,
    weights_scr,
    load_sems,
    store_sems,
    small_sems,
):
    pair_channels, heads, small_rows, pieces = shapes
    load_total = pltpu.make_async_copy(total_ref, total_scr, small_sems.at[0])
    load_total.start()
    moves = []
    for n, (src, held, dst) in enumerate(((ga_ref, ga_scr, ga_out), (gp_ref, gp_scr, gp_out))):
        size = src.shape[0] // pieces
        for p in range(pieces):
            at = pl.ds(p * size, size)
            load = pltpu.make_async_copy(src.at[at], held.at[at], load_sems.at[n, p])
            store = pltpu.make_async_copy(held.at[at], dst.at[at], store_sems.at[n, p])
            moves.append((load, store))
    for load, _ in moves:
        load.start()
    base = weights_out.shape[0]
    channels = weights_out.shape[1]
    load_total.wait()
    weights_scr[...] = total_scr[0:base, :].astype(F32)
    store_weights = pltpu.make_async_copy(weights_scr, weights_out, small_sems.at[1])
    store_weights.start()
    for load, store in moves:
        load.wait()
        store.start()
    tail = total_scr[base : base + 2 * small_rows, :].astype(F32)
    tail = tail[0:small_rows] + tail[small_rows:]
    pair_weight_out[...] = tail[0:heads, 0:pair_channels]
    token_weight_out[...] = tail[heads : heads + 1, 0:heads]
    store_weights.wait()
    for _, store in moves:
        store.wait()


def per_device(
    act,
    grad_out,
    pair,
    w_query,
    w_key,
    w_value,
    w_gate,
    w_out,
    w_pair,
    w_token,
    offsets,
    atom_token,
    padding,
):
    samples, atoms, channels = act.shape
    windows = offsets.shape[0]
    rows = atoms // windows
    pair_channels, heads = w_pair.shape
    span = pair.shape[-1]
    stack = heads * rows
    half = rows // 2
    ranges = lax.axis_size("atoms")
    wide = atoms + 2 * span
    vmem = pl.BlockSpec(memory_space=pltpu.VMEM)
    smem = pl.BlockSpec(memory_space=pltpu.SMEM)
    anywhere = pl.BlockSpec(memory_space=pl.ANY)
    small_rows = 8 * pl.cdiv(heads + 1, 8)
    chunk = 16 * pl.cdiv(5 * channels + 2 * small_rows, 32 * ranges)
    sum_rows = 2 * ranges * chunk

    def kernel(*refs):
        fused_kernel(ranges, *refs)

    edge = pltpu.VMEM((samples, span, channels), BF16)
    slot_rows = windows * (span + PAD) + PAD
    grad_act, grad_pair, total = pl.pallas_call(
        kernel,
        out_shape=(
            jax.ShapeDtypeStruct((samples, atoms, channels), BF16),
            jax.ShapeDtypeStruct((windows, half * pair_channels, span), BF16),
            jax.ShapeDtypeStruct((sum_rows, channels), BF16),
        ),
        in_specs=[smem] * 3 + [anywhere] * 3 + [vmem] * 7,
        out_specs=(anywhere, anywhere, vmem),
        scratch_shapes=[
            pltpu.VMEM((samples, atoms, channels), BF16),
            pltpu.VMEM((samples, atoms, channels), BF16),
            pltpu.VMEM((windows, rows * pair_channels, span), BF16),
            edge,
            edge,
            pltpu.VMEM((atoms // span, 1, span), jnp.int32),
            pltpu.VMEM((1, span), jnp.int32),
            pltpu.VMEM((1, span), jnp.int32),
            pltpu.VMEM((samples, wide, channels), F32),
            pltpu.VMEM((samples, wide, channels), F32),
            pltpu.VMEM((samples, atoms, channels), BF16),
            pltpu.VMEM((samples, atoms, channels), BF16),
            pltpu.VMEM((samples, atoms, channels), F32),
            pltpu.VMEM((samples, atoms, channels), F32),
            pltpu.VMEM((samples, atoms, 2 * channels), BF16),
            pltpu.VMEM((samples, atoms, channels), BF16),
            pltpu.VMEM((samples, slot_rows, channels), F32),
            pltpu.VMEM((samples, slot_rows, channels), F32),
            pltpu.VMEM((rows * pair_channels, stack), F32),
            pltpu.VMEM((span, stack), F32),
            pltpu.VMEM((rows * pair_channels, stack), BF16),
            pltpu.VMEM((wide, stack), F32),
            pltpu.VMEM((windows, 1, stack), F32),
            pltpu.VMEM((windows, heads * half, span), F32),
            pltpu.VMEM((windows, heads * half, span), BF16),
            pltpu.VMEM((windows, heads * half, span), BF16),
            edge,
            edge,
            pltpu.VMEM((sum_rows, channels), F32),
            pltpu.VMEM((ranges * chunk, channels), F32),
            pltpu.VMEM((ranges, chunk, channels), BF16),
            pltpu.VMEM((ranges - 1, chunk, channels), BF16),
            pltpu.SMEM((windows,), jnp.int32),
            pltpu.SemaphoreType.DMA((3,)),
            pltpu.SemaphoreType.DMA((2,)),
            pltpu.SemaphoreType.DMA((2, 4)),
            pltpu.SemaphoreType.DMA((2, 2)),
            pltpu.SemaphoreType.DMA((2, 3)),
            pltpu.SemaphoreType.DMA((2, ranges - 1)),
            pltpu.SemaphoreType.DMA((2, ranges - 1)),
        ],
        compiler_params=pltpu.CompilerParams(
            collective_id=0, has_side_effects=True, vmem_limit_bytes=63 * 1024 * 1024
        ),
        name="fused",
    )(
        offsets,
        w_token,
        padding,
        act,
        grad_out,
        pair.reshape(windows, rows * pair_channels, span),
        atom_token.reshape(atoms // span, span),
        w_query,
        w_key,
        w_value,
        w_gate,
        w_out,
        w_pair.T,
    )

    pieces = 1
    base = 5 * channels

    def last_kernel(*refs):
        finish_kernel((pair_channels, heads, small_rows, pieces), *refs)

    grad_act, grad_pair, weights, pair_weight, token_weight = pl.pallas_call(
        last_kernel,
        out_shape=(
            jax.ShapeDtypeStruct(grad_act.shape, BF16),
            jax.ShapeDtypeStruct(grad_pair.shape, BF16),
            jax.ShapeDtypeStruct((base, channels), F32),
            jax.ShapeDtypeStruct((heads, pair_channels), F32),
            jax.ShapeDtypeStruct((1, heads), F32),
        ),
        in_specs=[anywhere] * 3,
        out_specs=(anywhere, anywhere, anywhere, vmem, vmem),
        scratch_shapes=[
            pltpu.VMEM(grad_act.shape, BF16),
            pltpu.VMEM(grad_pair.shape, BF16),
            pltpu.VMEM(total.shape, BF16),
            pltpu.VMEM((base, channels), F32),
            pltpu.SemaphoreType.DMA((2, pieces)),
            pltpu.SemaphoreType.DMA((2, pieces)),
            pltpu.SemaphoreType.DMA((2,)),
        ],
        name="finish",
    )(grad_act, grad_pair, total)

    grad_weights = weights.reshape(5, channels, channels)
    grad_pair_weight = pair_weight.T
    grad_token_weight = token_weight.reshape(heads)
    grad_pair = grad_pair.reshape(windows, half, pair_channels, span)
    return (grad_act, grad_pair, grad_weights, grad_pair_weight, grad_token_weight)


def solution(mesh):
    in_specs = (
        P("samples", ("groups", "atoms"), None),
        P("samples", ("groups", "atoms"), None),
        P(("groups", "atoms"), None, None, None),
        P(),
        P(),
        P(),
        P(),
        P(),
        P(),
        P(),
        P(("groups", "atoms")),
        P(("groups", "atoms")),
        P(("groups", "atoms")),
    )
    out_specs = (
        P("samples", ("groups", "atoms"), None),
        P(("groups", "atoms"), "samples", None, None),
        P("groups", None, None),
        P("groups", None),
        P("groups"),
    )
    return jax.shard_map(
        per_device, mesh=mesh, in_specs=in_specs, out_specs=out_specs, check_vma=False
    )
```

```python
import math

import jax
import jax.numpy as jnp
from jax import lax
from jax.experimental import pallas as pl
from jax.experimental.pallas import tpu as pltpu
from jax.sharding import PartitionSpec as P

MASKED = -1000000000.0
BF16 = jnp.bfloat16
F32 = jnp.float32
LOG2E = math.log2(math.e)
TOGETHER = 4
PAD = 32


def nn(a, b):
    return lax.dot_general(a, b, (((1,), (0,)), ((), ())), preferred_element_type=F32)


def nt(a, b):
    return lax.dot_general(a, b, (((1,), (1,)), ((), ())), preferred_element_type=F32)


def tn(a, b):
    return lax.dot_general(a, b, (((0,), (0,)), ((), ())), preferred_element_type=F32)


def greet(barrier, devices):
    for device in devices:
        pl.semaphore_signal(
            barrier, inc=1, device_id=device, device_id_type=pl.DeviceIdType.MESH
        )


def remote(src, dst, sems, slot, device):
    return pltpu.make_async_remote_copy(
        src_ref=src,
        dst_ref=dst,
        send_sem=sems.at[0, slot],
        recv_sem=sems.at[1, slot],
        device_id=device,
        device_id_type=pl.DeviceIdType.MESH,
    )


def fused_kernel(
    ranges,
    offsets_ref,
    wtoken_ref,
    padding_ref,
    act_hbm,
    grad_hbm,
    pair_hbm,
    token_ref,
    wq_ref,
    wk_ref,
    wv_ref,
    wg_ref,
    wo_ref,
    wpair_ref,
    ga_hbm,
    pair_out_hbm,
    weights_hbm,
    pair_weight_ref,
    token_weight_ref,
    act_ref,
    grad_ref,
    pair_ref,
    before_ref,
    after_ref,
    code_scr,
    code_before,
    code_after,
    k_scr,
    v_scr,
    q_scr,
    da_scr,
    gate_scr,
    dqg_scr,
    gated_scr,
    dk_scr,
    dv_scr,
    pw_scr,
    tok_scr,
    wpair_scr,
    key_code_scr,
    query_code_scr,
    mine_ref,
    theirs_ref,
    got,
    from_lower,
    from_upper,
    sums_a,
    half_a,
    part_a,
    slots_a,
    total_a,
    sums_b,
    half_b,
    part_b,
    slots_b,
    total_b,
    starts_ref,
    load_sems,
    store_sems,
    halo_sems,
    edge_sems,
    core_sems,
    scatter_sems,
    gather_sems,
    weight_sems,
):
    me = lax.axis_index("atoms")
    core = lax.axis_index("samples")
    other = 1 - core
    samples, atoms, channels = act_ref.shape
    windows = pair_ref.shape[0]
    rows = atoms // windows
    span = before_ref.shape[1]
    wide = atoms + 2 * span
    pair_channels = wpair_ref.shape[1]
    heads = wpair_ref.shape[0]
    head_dim = channels // heads
    scale = 1.0 / math.sqrt(head_dim)
    stack = heads * rows
    half_rows = rows // 2
    unroll = math.gcd(4, samples)
    has_lower, has_upper = me > 0, me < ranges - 1
    lower, upper, peer = {"atoms": me - 1}, {"atoms": me + 1}, {"samples": other}
    everyone = [{"atoms": lax.rem(me + d, ranges)} for d in range(1, ranges)]

    barrier = pltpu.get_barrier_semaphore()
    greet(barrier, [peer] + everyone)
    load_act = pltpu.make_async_copy(act_hbm, act_ref, load_sems.at[0])
    load_grad = pltpu.make_async_copy(grad_hbm, grad_ref, load_sems.at[1])
    load_pair = pltpu.make_async_copy(pair_hbm, pair_ref, load_sems.at[2])
    load_act.start()
    load_grad.start()
    load_pair.start()

    code_rows = atoms // span
    live_end = atoms - padding_ref[0]
    lane_at = lax.broadcasted_iota(jnp.int32, (1, span), 1)
    for r in range(code_rows):
        code_scr[r] = jnp.where(lane_at + r * span < live_end, token_ref[r : r + 1, :] + 1, 0)

    pl.semaphore_wait(barrier, ranges)
    halo_up = [
        remote(act_hbm.at[:, pl.ds(atoms - span, span)], before_ref, halo_sems, 0, upper),
        remote(code_scr.at[code_rows - 1], code_before, halo_sems, 1, upper),
    ]
    halo_down = [
        remote(act_hbm.at[:, pl.ds(0, span)], after_ref, halo_sems, 2, lower),
        remote(code_scr.at[0], code_after, halo_sems, 3, lower),
    ]

    @pl.when(has_upper)
    def _():
        for copy in halo_up:
            copy.start()

    @pl.when(has_lower)
    def _():
        for copy in halo_down:
            copy.start()

    @pl.when(jnp.logical_not(has_lower))
    def _():
        before_ref[...] = jnp.zeros_like(before_ref)
        code_before[...] = jnp.zeros_like(code_before)

    @pl.when(jnp.logical_not(has_upper))
    def _():
        after_ref[...] = jnp.zeros_like(after_ref)
        code_after[...] = jnp.zeros_like(code_after)

    def code_column(first, row):
        column = jnp.broadcast_to(row.astype(F32), (stack, span)).T
        key_code_scr[first : first + span, :] = column

    lane_row = lax.broadcasted_iota(jnp.int32, (pair_channels, stack), 1) % rows
    lane_head = lax.broadcasted_iota(jnp.int32, (pair_channels, stack), 1) // rows
    wpair_values = wpair_ref[...].astype(F32).T
    wpair_rows = jnp.zeros((pair_channels, stack), F32)
    wtoken_row = jnp.zeros((1, stack), F32)
    for h in range(heads):
        wpair_rows = jnp.where(lane_head == h, wpair_values[:, h : h + 1], wpair_rows)
        wtoken_row = jnp.where(lane_head[0:1] == h, wtoken_ref[h], wtoken_row)
    for i in range(rows):
        wpair_scr[i * pair_channels : (i + 1) * pair_channels, :] = jnp.where(
            lane_row == i, wpair_rows, 0.0
        ).astype(BF16)
    for r in range(code_rows):
        code_column(span + r * span, code_scr[r])
        tokens = (token_ref[r : r + 1, :] + 1).astype(F32)
        for u in range(span // rows):
            piece = tokens[:, u * rows : (u + 1) * rows]
            query_code_scr[r * (span // rows) + u] = jnp.concatenate([piece] * heads, axis=1)
    pw_scr[...] = jnp.zeros_like(pw_scr)
    tok_scr[...] = jnp.zeros_like(tok_scr)
    sums_a[...] = jnp.zeros_like(sums_a)
    sums_b[...] = jnp.zeros_like(sums_b)
    anchor = me * atoms
    last_start = ranges * atoms - span
    for w in range(windows):
        starts_ref[w] = (
            jnp.clip(anchor + w * rows + offsets_ref[w], 0, last_start) - anchor + span
        )

    load_act.wait()
    load_grad.wait()
    slot = span + PAD

    def project(s, carry):
        own = act_ref[s]
        q_scr[s] = (nn(own, wq_ref[...]) * (scale * LOG2E)).astype(BF16)
        gate = jax.nn.sigmoid(nn(own, wg_ref[...]))
        gated_gy = nt(grad_ref[s], wo_ref[...]) * gate
        gate_scr[s] = gate
        da_scr[s] = gated_gy.astype(BF16)
        k_scr[s, span : span + atoms, :] = nn(own, wk_ref[...]).astype(BF16).astype(F32)
        v_scr[s, span : span + atoms, :] = nn(own, wv_ref[...]).astype(BF16).astype(F32)
        blank = jnp.zeros((PAD, channels), F32)
        for w in range(windows + 1):
            dk_scr[s, w * slot : w * slot + PAD, :] = blank
            dv_scr[s, w * slot : w * slot + PAD, :] = blank
        return carry

    lax.fori_loop(0, samples, project, 0, unroll=unroll)
    load_pair.wait()

    row_head = lax.broadcasted_iota(jnp.int32, (stack, channels), 0) // rows
    column_head = lax.broadcasted_iota(jnp.int32, (stack, channels), 1) // head_dim
    head_mask = jnp.where(row_head == column_head, 1.0, 0.0).astype(BF16)
    lane = lax.broadcasted_iota(jnp.int32, (rows, channels), 1) // head_dim
    head_is = [lane == h for h in range(heads)]
    first_mine = core == 0

    def spread(x):
        return jnp.concatenate([x] * heads, axis=0) * head_mask

    def collect(x):
        out = x[0:rows]
        for h in range(1, heads):
            out = jnp.where(head_is[h], x[h * rows : (h + 1) * rows], out)
        return out

    def attend(block):
        ws = [block * TOGETHER + u for u in range(TOGETHER)]
        mine_rows = [pl.ds(pl.multiple_of(w * rows, rows), rows) for w in ws]
        key_rows = [pl.ds(starts_ref[w], span) for w in ws]
        slot_rows = [pl.ds(pl.multiple_of(w * slot + PAD, 8), span) for w in ws]
        sames, biases = [], []
        for u, w in enumerate(ws):
            key_code = key_code_scr[key_rows[u], :]
            same = key_code == query_code_scr[w]
            bias = (tn(pair_ref[w], wpair_scr[...]) + jnp.where(same, wtoken_row, 0.0)) * LOG2E
            biases.append(jnp.where(key_code > 0.0, bias, MASKED))
            sames.append(same)
        units = [(u, s) for u in range(TOGETHER) for s in range(samples)]
        keys = [k_scr[s, key_rows[u], :].astype(BF16) for u, s in units]
        values = [v_scr[s, key_rows[u], :].astype(BF16) for u, s in units]
        qm = [spread(q_scr[s, mine_rows[u], :]) for u, s in units]
        dam = [spread(da_scr[s, mine_rows[u], :]) for u, s in units]
        scores = [nt(k, q) + biases[u] for k, q, (u, s) in zip(keys, qm, units)]
        dprobs = [nt(v, d) for v, d in zip(values, dam)]
        tops = [jnp.max(x, axis=0, keepdims=True) for x in scores]
        exps = [jnp.exp2(x - t) for x, t in zip(scores, tops)]
        probs = [e * (1.0 / jnp.sum(e, axis=0, keepdims=True)) for e in exps]
        probs_b = [p.astype(BF16) for p in probs]
        for (u, s), p, d in zip(units, probs_b, dam):
            dv_scr[s, slot_rows[u], :] = nn(p, d)
        ds = [p * (d - jnp.sum(p * d, axis=0, keepdims=True)) for p, d in zip(probs, dprobs)]
        ds_b = [d.astype(BF16) for d in ds]
        for (u, s), d, q in zip(units, ds_b, qm):
            dk_scr[s, slot_rows[u], :] = nn(d, q)
        for (u, s), p, v in zip(units, probs_b, values):
            a = collect(tn(p, v))
            gate = gate_scr[s, mine_rows[u], :]
            gated_gy = da_scr[s, mine_rows[u], :].astype(F32)
            gated_scr[s, mine_rows[u], :] = (gate * a).astype(BF16)
            dqg_scr[s, mine_rows[u], channels:] = (gated_gy * (1.0 - gate) * a).astype(BF16)
        for (u, s), d, k in zip(units, ds_b, keys):
            dqg_scr[s, mine_rows[u], 0:channels] = (collect(tn(d, k)) * scale).astype(BF16)
        for u, w in enumerate(ws):
            of_window = [d for d, unit in zip(ds, units) if unit[0] == u]
            total = of_window[0]
            for d in of_window[1:]:
                total = total + d
            of_token = jnp.where(sames[u], total, 0.0)
            token_sum = of_token if u == 0 else token_sum + of_token
            pw_scr[...] += nn(pair_ref[w], total.astype(BF16))
            turned = total.T
            for h in range(heads):
                low = turned[h * rows : h * rows + half_rows]
                high = turned[h * rows + half_rows : (h + 1) * rows]
                at = slice(h * half_rows, (h + 1) * half_rows)
                mine_ref[w, at, :] = jnp.where(first_mine, low, high)
                theirs_ref[w, at, :] = jnp.where(first_mine, high, low).astype(BF16)
        tok_scr[...] += token_sum

    def gather_rows(s, b):
        dk, dv = None, None
        for w in range(max(0, b - 2 * span // rows), min(b, windows - 1) + 1):
            shift = jnp.clip(b * rows - starts_ref[w], -PAD, span)
            at = pl.ds(w * slot + PAD + shift, rows)
            k, v = dk_scr[s, at, :], dv_scr[s, at, :]
            dk, dv = (k, v) if dk is None else (dk + k, dv + v)
        return dk * (1.0 / LOG2E), dv

    halo_blocks = span // rows
    own_blocks = atoms // rows

    def project_halo(s, carry):
        for ref, first in ((before_ref, 0), (after_ref, span + atoms)):
            k_scr[s, first : first + span, :] = nn(ref[s], wk_ref[...]).astype(BF16).astype(F32)
            v_scr[s, first : first + span, :] = nn(ref[s], wv_ref[...]).astype(BF16).astype(F32)
        return carry

    edge_up = remote(after_ref, from_lower, edge_sems, 0, upper)
    edge_down = remote(before_ref, from_upper, edge_sems, 1, lower)

    def halo_gradient(s, carry):
        c = channels
        for first, ref in ((0, before_ref), (halo_blocks + own_blocks, after_ref)):
            parts = [gather_rows(s, b) for b in range(first, first + halo_blocks)]
            dkv = jnp.concatenate(
                [jnp.concatenate([p[i] for p in parts], axis=0).astype(BF16) for i in (0, 1)],
                axis=1,
            )
            weights = jnp.concatenate([wk_ref[...], wv_ref[...]], axis=1)
            from_kv = tn(ref[s], dkv)
            sums_b[0:c, :] += from_kv[:, 0:c]
            sums_b[c : 2 * c, :] += from_kv[:, c:]
            ref[s] = nt(dkv, weights).astype(BF16)
        return carry

    blocks = windows // TOGETHER
    early = blocks - 2

    def step(it, carry):
        @pl.when(it == early)
        def _():
            @pl.when(has_upper)
            def _():
                for copy in halo_down:
                    copy.wait_recv()

            @pl.when(has_lower)
            def _():
                for copy in halo_up:
                    copy.wait_recv()

            code_column(0, code_before[...])
            code_column(span + atoms, code_after[...])
            lax.fori_loop(0, samples, project_halo, 0, unroll=unroll)

        block = jnp.where(
            it < early,
            it + 1,
            jnp.where(it == early, 0, blocks - 1),
        )
        attend(block)
        return carry

    lax.fori_loop(0, blocks, step, 0)
    pair_copy = remote(theirs_ref, got, core_sems, 1, peer)
    pair_copy.start()
    lax.fori_loop(0, samples, halo_gradient, 0, unroll=unroll)

    @pl.when(has_upper)
    def _():
        edge_up.start()

    @pl.when(has_lower)
    def _():
        edge_down.start()

    shape = pw_scr.shape
    at_row = lax.broadcasted_iota(jnp.int32, shape, 0) // pair_channels
    at_col = lax.broadcasted_iota(jnp.int32, shape, 1) % rows
    diagonal = jnp.where(at_row == at_col, pw_scr[...], 0.0)
    by_channel = jnp.sum(diagonal.reshape(rows, pair_channels, stack), axis=0)
    by_channel = jnp.concatenate(
        [by_channel, jnp.zeros((channels - pair_channels, stack), F32)], axis=0
    )
    by_head = jnp.sum(by_channel.T.reshape(heads, rows, channels), axis=1)
    token_row = jnp.sum(tok_scr[...], axis=0, keepdims=True)
    lanes = lax.broadcasted_iota(jnp.int32, (1, stack), 1)
    by_token = jnp.zeros((1, stack), F32)
    for h in range(heads):
        one = jnp.sum(jnp.where(lanes // rows == h, token_row, 0.0), axis=1, keepdims=True)
        by_token = jnp.where(lanes == h, one, by_token)
    base = 3 * channels
    small_rows = 8 * pl.cdiv(heads + 1, 8)
    sums_a[base : base + heads, :] = by_head
    sums_a[base + heads : base + heads + 1, :] = by_token

    def halves(sums, got_half, slot):
        half = got_half.shape[0]
        theirs = pl.ds(pl.multiple_of(other * half, 8), half)
        return remote(sums.at[theirs], got_half, core_sems, slot, peer)

    def scattered(part, slots, first):
        return [
            remote(
                part.at[lax.rem(me + d, ranges)],
                slots.at[d - 1],
                scatter_sems,
                first + d - 1,
                everyone[d - 1],
            )
            for d in range(1, ranges)
        ]

    def gathered(total, chunk, first):
        place = pl.ds(pl.multiple_of((core * ranges + me) * chunk, 16), chunk)
        copies = [
            remote(total.at[place], total.at[place], gather_sems, first + d - 1, everyone[d - 1])
            for d in range(1, ranges)
        ]
        return place, copies

    def add_half(sums, got_half):
        half = got_half.shape[0]
        got_half[...] += sums[pl.ds(pl.multiple_of(core * half, 8), half), :]

    def add_chunks(got_half, slots):
        chunk = slots.shape[1]
        out = got_half[pl.ds(pl.multiple_of(me * chunk, 8), chunk), :]
        for d in range(1, ranges):
            out = out + slots[d - 1].astype(F32)
        return out.astype(BF16)

    def own_total(total, slot):
        half = total.shape[0] // 2
        at = pl.ds(pl.multiple_of(core * half, 16), half)
        return remote(total.at[at], total.at[at], core_sems, slot, peer)

    half_copy_a = halves(sums_a, half_a, 0)
    half_copy_b = halves(sums_b, half_b, 3)
    scatter_a = scattered(part_a, slots_a, 0)
    scatter_b = scattered(part_b, slots_b, ranges - 1)
    place_a, gather_a = gathered(total_a, slots_a.shape[1], 0)
    place_b, gather_b = gathered(total_b, slots_b.shape[1], ranges - 1)
    last_copy_a = own_total(total_a, 2)
    last_copy_b = own_total(total_b, 4)

    def own_weights(s, carry):
        c = channels
        sums = tn(act_ref[s], dqg_scr[s])
        sums_a[0:c, :] += sums[:, 0:c]
        sums_a[c : 2 * c, :] += sums[:, c:]
        sums_a[2 * c : 3 * c, :] += tn(gated_scr[s], grad_ref[s])
        return carry

    lax.fori_loop(0, samples, own_weights, 0, unroll=unroll)
    half_copy_a.start()

    def weight_gradients(s, carry):
        for b in range(halo_blocks, halo_blocks + own_blocks):
            dk, dv = gather_rows(s, b)
            k_scr[s, b * rows : (b + 1) * rows, :] = dk
            v_scr[s, b * rows : (b + 1) * rows, :] = dv
        c = channels
        own = slice(span, span + atoms)
        grads = jnp.concatenate(
            [k_scr[s, own, :].astype(BF16), v_scr[s, own, :].astype(BF16)], axis=1
        )
        sums = tn(act_ref[s], grads)
        sums_b[0:c, :] += sums[:, 0:c]
        sums_b[c : 2 * c, :] += sums[:, c:]
        return carry

    lax.fori_loop(0, unroll, weight_gradients, 0, unroll=unroll)
    half_copy_a.wait_recv()
    add_half(sums_a, half_a)
    half_size = half_a.shape[0]
    small = base % half_size
    rest = half_a[small : small + small_rows, :]
    rest = rest - rest.astype(BF16).astype(F32)
    low_rows = slice(small + small_rows, small + 2 * small_rows)
    half_a[low_rows, :] = jnp.where(core == base // half_size, rest, half_a[low_rows, :])
    part_a[...] = half_a[...].reshape(part_a.shape).astype(BF16)
    for copy in scatter_a:
        copy.start()
    lax.fori_loop(unroll, samples, weight_gradients, 0, unroll=unroll)
    half_copy_b.start()

    inner = slice(span, atoms - span)

    def own_gradient(s, carry):
        own = slice(span, span + atoms)
        dq = dqg_scr[s, :, 0:channels]
        dg = dqg_scr[s, :, channels:]
        grads = jnp.concatenate(
            [dq, k_scr[s, own, :].astype(BF16), v_scr[s, own, :].astype(BF16), dg], axis=1
        )
        weights = jnp.concatenate([wq_ref[...], wk_ref[...], wv_ref[...], wg_ref[...]], axis=1)
        ga = nt(grads, weights)
        dk_scr[s, 0:span, :] = ga[0:span]
        dk_scr[s, span : 2 * span, :] = ga[atoms - span :]
        q_scr[s, inner, :] = ga[inner].astype(BF16)
        return carry

    lax.fori_loop(0, 2, own_gradient, 0)
    half_copy_b.wait_recv()
    add_half(sums_b, half_b)
    part_b[...] = half_b[...].reshape(part_b.shape).astype(BF16)
    for copy in scatter_b:
        copy.start()
    for copy in scatter_a:
        copy.wait_recv()
    total_a[place_a, :] = add_chunks(half_a, slots_a)
    for copy in gather_a:
        copy.start()
    lax.fori_loop(2, samples, own_gradient, 0, unroll=math.gcd(3, samples - 2))

    lane_out = lax.broadcasted_iota(jnp.int32, (pair_channels, heads * half_rows), 1)
    spread_rows = jnp.zeros((pair_channels, heads * half_rows), F32)
    for h in range(heads):
        spread_rows = jnp.where(lane_out // half_rows == h, wpair_values[:, h : h + 1], spread_rows)
    weight = jnp.concatenate(
        [
            jnp.where(lane_out % half_rows == i, spread_rows, 0.0).astype(BF16)
            for i in range(half_rows)
        ],
        axis=0,
    )
    for copy in scatter_b:
        copy.wait_recv()
    total_b[place_b, :] = add_chunks(half_b, slots_b)
    for copy in gather_b:
        copy.start()
    for copy in gather_a:
        copy.wait_recv()
    last_copy_a.start()

    pair_copy.wait_recv()
    out_rows = half_rows * pair_channels

    def pair_gradient(w, carry):
        both = mine_ref[w] + got[w].astype(F32)
        high = both.astype(BF16)
        low = (both - high.astype(F32)).astype(BF16)
        pair_ref[w, 0:out_rows, :] = (nn(weight, high) + nn(weight, low)).astype(BF16)
        return carry

    lax.fori_loop(0, windows, pair_gradient, 0, unroll=math.gcd(5, windows))
    store_pair = pltpu.make_async_copy(
        pair_ref.at[:, pl.ds(0, out_rows)], pair_out_hbm, store_sems.at[0]
    )
    store_pair.start()

    for copy in gather_b:
        copy.wait_recv()
    last_copy_b.start()

    @pl.when(has_lower)
    def _():
        edge_down.wait_send()
        edge_up.wait_recv()

    @pl.when(has_upper)
    def _():
        edge_up.wait_send()
        edge_down.wait_recv()

    @pl.when(jnp.logical_not(has_lower))
    def _():
        from_lower[...] = jnp.zeros_like(from_lower)

    @pl.when(jnp.logical_not(has_upper))
    def _():
        from_upper[...] = jnp.zeros_like(from_upper)

    def add_edges(s, carry):
        q_scr[s, 0:span, :] = (dk_scr[s, 0:span, :] + from_lower[s].astype(F32)).astype(BF16)
        q_scr[s, atoms - span : atoms, :] = (
            dk_scr[s, span : 2 * span, :] + from_upper[s].astype(F32)
        ).astype(BF16)
        return carry

    lax.fori_loop(0, samples, add_edges, 0, unroll=unroll)
    store_act = pltpu.make_async_copy(q_scr, ga_hbm, store_sems.at[1])
    store_act.start()

    @pl.when(has_upper)
    def _():
        for copy in halo_up:
            copy.wait_send()

    @pl.when(has_lower)
    def _():
        for copy in halo_down:
            copy.wait_send()

    pair_copy.wait_send()
    half_copy_a.wait_send()
    half_copy_b.wait_send()
    last_copy_a.wait()
    last_copy_b.wait()
    c = channels
    sums_a[0:base, :] = total_a[0:base, :].astype(F32)
    sums_b[0 : 2 * c, :] = total_b[0 : 2 * c, :].astype(F32)
    stores = [
        pltpu.make_async_copy(src, weights_hbm.at[pl.ds(to, rows_of)], weight_sems.at[n])
        for n, (src, to, rows_of) in enumerate(
            (
                (sums_a.at[pl.ds(0, c)], 0, c),
                (sums_b.at[pl.ds(0, 2 * c)], c, 2 * c),
                (sums_a.at[pl.ds(c, 2 * c)], 3 * c, 2 * c),
            )
        )
    ]
    for store in stores:
        store.start()
    tail = total_a[base : base + 2 * small_rows, :].astype(F32)
    tail = tail[0:small_rows] + tail[small_rows:]
    pair_weight_ref[...] = tail[0:heads, 0:pair_channels]
    token_weight_ref[...] = tail[heads : heads + 1, 0:heads]
    for copy in scatter_a + scatter_b + gather_a + gather_b:
        copy.wait_send()
    store_pair.wait()
    store_act.wait()
    for store in stores:
        store.wait()


def finish_kernel(*refs):
    ins, outs, held = refs[0:5], refs[5:10], refs[10:13]
    load_sems, store_sems = refs[13:15]
    small = [
        pltpu.make_async_copy(ins[n], outs[n], store_sems.at[n]) for n in range(3, len(ins))
    ]
    loads = [pltpu.make_async_copy(ins[n], held[n], load_sems.at[n]) for n in range(3)]
    stores = [pltpu.make_async_copy(held[n], outs[n], store_sems.at[n]) for n in range(3)]
    for copy in loads + small:
        copy.start()
    for load, store in zip(loads, stores):
        load.wait()
        store.start()
    for copy in stores + small:
        copy.wait()


def per_device(
    act,
    grad_out,
    pair,
    w_query,
    w_key,
    w_value,
    w_gate,
    w_out,
    w_pair,
    w_token,
    offsets,
    atom_token,
    padding,
):
    samples, atoms, channels = act.shape
    windows = offsets.shape[0]
    rows = atoms // windows
    pair_channels, heads = w_pair.shape
    span = pair.shape[-1]
    stack = heads * rows
    half = rows // 2
    ranges = lax.axis_size("atoms")
    wide = atoms + 2 * span
    vmem = pl.BlockSpec(memory_space=pltpu.VMEM)
    smem = pl.BlockSpec(memory_space=pltpu.SMEM)
    anywhere = pl.BlockSpec(memory_space=pl.ANY)
    small_rows = 8 * pl.cdiv(heads + 1, 8)

    def sum_scratch(rows_of):
        chunk = 16 * pl.cdiv(rows_of, 32 * ranges)
        half_size = ranges * chunk
        return [
            pltpu.VMEM((2 * half_size, channels), F32),
            pltpu.VMEM((half_size, channels), F32),
            pltpu.VMEM((ranges, chunk, channels), BF16),
            pltpu.VMEM((ranges - 1, chunk, channels), BF16),
            pltpu.VMEM((2 * half_size, channels), BF16),
        ]

    def kernel(*refs):
        fused_kernel(ranges, *refs)

    edge = pltpu.VMEM((samples, span, channels), BF16)
    slot_rows = windows * (span + PAD) + PAD
    results = pl.pallas_call(
        kernel,
        out_shape=(
            jax.ShapeDtypeStruct((samples, atoms, channels), BF16),
            jax.ShapeDtypeStruct((windows, half * pair_channels, span), BF16),
            jax.ShapeDtypeStruct((5 * channels, channels), F32),
            jax.ShapeDtypeStruct((heads, pair_channels), F32),
            jax.ShapeDtypeStruct((1, heads), F32),
        ),
        in_specs=[smem] * 3 + [anywhere] * 3 + [vmem] * 7,
        out_specs=(anywhere, anywhere, anywhere, vmem, vmem),
        scratch_shapes=[
            pltpu.VMEM((samples, atoms, channels), BF16),
            pltpu.VMEM((samples, atoms, channels), BF16),
            pltpu.VMEM((windows, rows * pair_channels, span), BF16),
            edge,
            edge,
            pltpu.VMEM((atoms // span, 1, span), jnp.int32),
            pltpu.VMEM((1, span), jnp.int32),
            pltpu.VMEM((1, span), jnp.int32),
            pltpu.VMEM((samples, wide, channels), F32),
            pltpu.VMEM((samples, wide, channels), F32),
            pltpu.VMEM((samples, atoms, channels), BF16),
            pltpu.VMEM((samples, atoms, channels), BF16),
            pltpu.VMEM((samples, atoms, channels), F32),
            pltpu.VMEM((samples, atoms, 2 * channels), BF16),
            pltpu.VMEM((samples, atoms, channels), BF16),
            pltpu.VMEM((samples, slot_rows, channels), F32),
            pltpu.VMEM((samples, slot_rows, channels), F32),
            pltpu.VMEM((rows * pair_channels, stack), F32),
            pltpu.VMEM((span, stack), F32),
            pltpu.VMEM((rows * pair_channels, stack), BF16),
            pltpu.VMEM((wide, stack), F32),
            pltpu.VMEM((windows, 1, stack), F32),
            pltpu.VMEM((windows, heads * half, span), F32),
            pltpu.VMEM((windows, heads * half, span), BF16),
            pltpu.VMEM((windows, heads * half, span), BF16),
            edge,
            edge,
            *sum_scratch(3 * channels + 2 * small_rows),
            *sum_scratch(2 * channels),
            pltpu.SMEM((windows,), jnp.int32),
            pltpu.SemaphoreType.DMA((3,)),
            pltpu.SemaphoreType.DMA((2,)),
            pltpu.SemaphoreType.DMA((2, 4)),
            pltpu.SemaphoreType.DMA((2, 2)),
            pltpu.SemaphoreType.DMA((2, 5)),
            pltpu.SemaphoreType.DMA((2, 2 * (ranges - 1))),
            pltpu.SemaphoreType.DMA((2, 2 * (ranges - 1))),
            pltpu.SemaphoreType.DMA((3,)),
        ],
        compiler_params=pltpu.CompilerParams(
            collective_id=0, has_side_effects=True, vmem_limit_bytes=63 * 1024 * 1024
        ),
        name="fused",
    )(
        offsets,
        w_token,
        padding,
        act,
        grad_out,
        pair.reshape(windows, rows * pair_channels, span),
        atom_token.reshape(atoms // span, span),
        w_query,
        w_key,
        w_value,
        w_gate,
        w_out,
        w_pair.T,
    )

    grad_act, grad_pair, weights, pair_weight, token_weight = pl.pallas_call(
        finish_kernel,
        out_shape=tuple(jax.ShapeDtypeStruct(r.shape, r.dtype) for r in results),
        in_specs=[anywhere] * 5,
        out_specs=(anywhere,) * 5,
        scratch_shapes=[pltpu.VMEM(r.shape, r.dtype) for r in results[:3]]
        + [pltpu.SemaphoreType.DMA((3,)), pltpu.SemaphoreType.DMA((5,))],
        name="finish",
    )(*results)

    grad_weights = weights.reshape(5, channels, channels)
    grad_pair_weight = pair_weight.T
    grad_token_weight = token_weight.reshape(heads)
    grad_pair = grad_pair.reshape(windows, half, pair_channels, span)
    return (grad_act, grad_pair, grad_weights, grad_pair_weight, grad_token_weight)


def solution(mesh):
    in_specs = (
        P("samples", ("groups", "atoms"), None),
        P("samples", ("groups", "atoms"), None),
        P(("groups", "atoms"), None, None, None),
        P(),
        P(),
        P(),
        P(),
        P(),
        P(),
        P(),
        P(("groups", "atoms")),
        P(("groups", "atoms")),
        P(("groups", "atoms")),
    )
    out_specs = (
        P("samples", ("groups", "atoms"), None),
        P(("groups", "atoms"), "samples", None, None),
        P("groups", None, None),
        P("groups", None),
        P("groups"),
    )
    return jax.shard_map(
        per_device, mesh=mesh, in_specs=in_specs, out_specs=out_specs, check_vma=False
    )
```

```python
import math

import jax
import jax.numpy as jnp
from jax import lax
from jax.experimental import pallas as pl
from jax.experimental.pallas import tpu as pltpu
from jax.sharding import PartitionSpec as P

MASKED = -1000000000.0
BF16 = jnp.bfloat16
F32 = jnp.float32
LOG2E = math.log2(math.e)
TOGETHER = 4
PAD = 32


def nn(a, b):
    return lax.dot_general(a, b, (((1,), (0,)), ((), ())), preferred_element_type=F32)


def nt(a, b):
    return lax.dot_general(a, b, (((1,), (1,)), ((), ())), preferred_element_type=F32)


def tn(a, b):
    return lax.dot_general(a, b, (((0,), (0,)), ((), ())), preferred_element_type=F32)


def greet(barrier, devices):
    for device in devices:
        pl.semaphore_signal(
            barrier, inc=1, device_id=device, device_id_type=pl.DeviceIdType.MESH
        )


def remote(src, dst, sems, slot, device):
    return pltpu.make_async_remote_copy(
        src_ref=src,
        dst_ref=dst,
        send_sem=sems.at[0, slot],
        recv_sem=sems.at[1, slot],
        device_id=device,
        device_id_type=pl.DeviceIdType.MESH,
    )


def fused_kernel(
    ranges,
    offsets_ref,
    wtoken_ref,
    padding_ref,
    act_hbm,
    grad_hbm,
    pair_hbm,
    token_ref,
    wq_ref,
    wk_ref,
    wv_ref,
    wg_ref,
    wo_ref,
    wpair_ref,
    ga_hbm,
    pair_out_hbm,
    weights_hbm,
    pair_weight_ref,
    token_weight_ref,
    act_ref,
    grad_ref,
    pair_ref,
    before_ref,
    after_ref,
    code_scr,
    code_before,
    code_after,
    k_scr,
    v_scr,
    q_scr,
    da_scr,
    gate_scr,
    dqg_scr,
    gated_scr,
    dk_scr,
    dv_scr,
    pw_scr,
    tok_scr,
    wpair_scr,
    key_code_scr,
    query_code_scr,
    mine_ref,
    theirs_ref,
    got,
    from_lower,
    from_upper,
    sums_a,
    half_a,
    part_a,
    slots_a,
    total_a,
    sums_b,
    half_b,
    part_b,
    slots_b,
    total_b,
    starts_ref,
    load_sems,
    store_sems,
    halo_sems,
    edge_sems,
    core_sems,
    scatter_sems,
    gather_sems,
    weight_sems,
):
    me = lax.axis_index("atoms")
    core = lax.axis_index("samples")
    other = 1 - core
    samples, atoms, channels = act_ref.shape
    windows = pair_ref.shape[0]
    rows = atoms // windows
    span = before_ref.shape[1]
    wide = atoms + 2 * span
    pair_channels = wpair_ref.shape[1]
    heads = wpair_ref.shape[0]
    head_dim = channels // heads
    scale = 1.0 / math.sqrt(head_dim)
    stack = heads * rows
    half_rows = rows // 2
    unroll = math.gcd(4, samples)
    has_lower, has_upper = me > 0, me < ranges - 1
    lower, upper, peer = {"atoms": me - 1}, {"atoms": me + 1}, {"samples": other}
    everyone = [{"atoms": lax.rem(me + d, ranges)} for d in range(1, ranges)]

    barrier = pltpu.get_barrier_semaphore()
    greet(barrier, [peer] + everyone)
    load_act = pltpu.make_async_copy(act_hbm, act_ref, load_sems.at[0])
    load_grad = pltpu.make_async_copy(grad_hbm, grad_ref, load_sems.at[1])
    load_pair = pltpu.make_async_copy(pair_hbm, pair_ref, load_sems.at[2])
    load_act.start()
    load_grad.start()
    load_pair.start()

    code_rows = atoms // span
    live_end = atoms - padding_ref[0]
    lane_at = lax.broadcasted_iota(jnp.int32, (1, span), 1)
    for r in range(code_rows):
        code_scr[r] = jnp.where(lane_at + r * span < live_end, token_ref[r : r + 1, :] + 1, 0)

    pl.semaphore_wait(barrier, ranges)
    halo_up = [
        remote(act_hbm.at[:, pl.ds(atoms - span, span)], before_ref, halo_sems, 0, upper),
        remote(code_scr.at[code_rows - 1], code_before, halo_sems, 1, upper),
    ]
    halo_down = [
        remote(act_hbm.at[:, pl.ds(0, span)], after_ref, halo_sems, 2, lower),
        remote(code_scr.at[0], code_after, halo_sems, 3, lower),
    ]

    @pl.when(has_upper)
    def _():
        for copy in halo_up:
            copy.start()

    @pl.when(has_lower)
    def _():
        for copy in halo_down:
            copy.start()

    @pl.when(jnp.logical_not(has_lower))
    def _():
        before_ref[...] = jnp.zeros_like(before_ref)
        code_before[...] = jnp.zeros_like(code_before)

    @pl.when(jnp.logical_not(has_upper))
    def _():
        after_ref[...] = jnp.zeros_like(after_ref)
        code_after[...] = jnp.zeros_like(code_after)

    def code_column(first, row):
        column = jnp.broadcast_to(row.astype(F32), (stack, span)).T
        key_code_scr[first : first + span, :] = column

    lane_row = lax.broadcasted_iota(jnp.int32, (pair_channels, stack), 1) % rows
    lane_head = lax.broadcasted_iota(jnp.int32, (pair_channels, stack), 1) // rows
    wpair_values = wpair_ref[...].astype(F32).T
    wpair_rows = jnp.zeros((pair_channels, stack), F32)
    wtoken_row = jnp.zeros((1, stack), F32)
    for h in range(heads):
        wpair_rows = jnp.where(lane_head == h, wpair_values[:, h : h + 1], wpair_rows)
        wtoken_row = jnp.where(lane_head[0:1] == h, wtoken_ref[h], wtoken_row)
    for i in range(rows):
        wpair_scr[i * pair_channels : (i + 1) * pair_channels, :] = jnp.where(
            lane_row == i, wpair_rows, 0.0
        ).astype(BF16)
    for r in range(code_rows):
        code_column(span + r * span, code_scr[r])
        tokens = (token_ref[r : r + 1, :] + 1).astype(F32)
        for u in range(span // rows):
            piece = tokens[:, u * rows : (u + 1) * rows]
            query_code_scr[r * (span // rows) + u] = jnp.concatenate([piece] * heads, axis=1)
    pw_scr[...] = jnp.zeros_like(pw_scr)
    tok_scr[...] = jnp.zeros_like(tok_scr)
    sums_a[...] = jnp.zeros_like(sums_a)
    sums_b[...] = jnp.zeros_like(sums_b)
    anchor = me * atoms
    last_start = ranges * atoms - span
    for w in range(windows):
        starts_ref[w] = (
            jnp.clip(anchor + w * rows + offsets_ref[w], 0, last_start) - anchor + span
        )

    load_act.wait()
    load_grad.wait()
    slot = span + PAD

    def project(s, carry):
        own = act_ref[s]
        q_scr[s] = (nn(own, wq_ref[...]) * (scale * LOG2E)).astype(BF16)
        gate = jax.nn.sigmoid(nn(own, wg_ref[...]))
        gated_gy = nt(grad_ref[s], wo_ref[...]) * gate
        gate_scr[s] = gate
        da_scr[s] = gated_gy.astype(BF16)
        k_scr[s, span : span + atoms, :] = nn(own, wk_ref[...]).astype(BF16).astype(F32)
        v_scr[s, span : span + atoms, :] = nn(own, wv_ref[...]).astype(BF16).astype(F32)
        blank = jnp.zeros((PAD, channels), F32)
        for w in range(windows + 1):
            dk_scr[s, w * slot : w * slot + PAD, :] = blank
            dv_scr[s, w * slot : w * slot + PAD, :] = blank
        return carry

    lax.fori_loop(0, samples, project, 0, unroll=unroll)
    load_pair.wait()

    row_head = lax.broadcasted_iota(jnp.int32, (stack, channels), 0) // rows
    column_head = lax.broadcasted_iota(jnp.int32, (stack, channels), 1) // head_dim
    head_mask = jnp.where(row_head == column_head, 1.0, 0.0).astype(BF16)
    lane = lax.broadcasted_iota(jnp.int32, (rows, channels), 1) // head_dim
    head_is = [lane == h for h in range(heads)]
    first_mine = core == 0

    def spread(x):
        return jnp.concatenate([x] * heads, axis=0) * head_mask

    def collect(x):
        out = x[0:rows]
        for h in range(1, heads):
            out = jnp.where(head_is[h], x[h * rows : (h + 1) * rows], out)
        return out

    def attend(block):
        ws = [block * TOGETHER + u for u in range(TOGETHER)]
        mine_rows = [pl.ds(pl.multiple_of(w * rows, rows), rows) for w in ws]
        key_rows = [pl.ds(starts_ref[w], span) for w in ws]
        slot_rows = [pl.ds(pl.multiple_of(w * slot + PAD, 8), span) for w in ws]
        sames, biases = [], []
        for u, w in enumerate(ws):
            key_code = key_code_scr[key_rows[u], :]
            same = key_code == query_code_scr[w]
            bias = (tn(pair_ref[w], wpair_scr[...]) + jnp.where(same, wtoken_row, 0.0)) * LOG2E
            biases.append(jnp.where(key_code > 0.0, bias, MASKED))
            sames.append(same)
        units = [(u, s) for u in range(TOGETHER) for s in range(samples)]
        keys = [k_scr[s, key_rows[u], :].astype(BF16) for u, s in units]
        values = [v_scr[s, key_rows[u], :].astype(BF16) for u, s in units]
        qm = [spread(q_scr[s, mine_rows[u], :]) for u, s in units]
        dam = [spread(da_scr[s, mine_rows[u], :]) for u, s in units]
        scores = [nt(k, q) + biases[u] for k, q, (u, s) in zip(keys, qm, units)]
        dprobs = [nt(v, d) for v, d in zip(values, dam)]
        tops = [jnp.max(x, axis=0, keepdims=True) for x in scores]
        exps = [jnp.exp2(x - t) for x, t in zip(scores, tops)]
        probs = [e * (1.0 / jnp.sum(e, axis=0, keepdims=True)) for e in exps]
        probs_b = [p.astype(BF16) for p in probs]
        for (u, s), p, d in zip(units, probs_b, dam):
            dv_scr[s, slot_rows[u], :] = nn(p, d)
        ds = [p * (d - jnp.sum(p * d, axis=0, keepdims=True)) for p, d in zip(probs, dprobs)]
        ds_b = [d.astype(BF16) for d in ds]
        for (u, s), d, q in zip(units, ds_b, qm):
            dk_scr[s, slot_rows[u], :] = nn(d, q)
        for (u, s), p, v in zip(units, probs_b, values):
            a = collect(tn(p, v))
            gate = gate_scr[s, mine_rows[u], :]
            gated_gy = da_scr[s, mine_rows[u], :].astype(F32)
            gated_scr[s, mine_rows[u], :] = (gate * a).astype(BF16)
            dqg_scr[s, mine_rows[u], channels:] = (gated_gy * (1.0 - gate) * a).astype(BF16)
        for (u, s), d, k in zip(units, ds_b, keys):
            dqg_scr[s, mine_rows[u], 0:channels] = (collect(tn(d, k)) * scale).astype(BF16)
        for u, w in enumerate(ws):
            of_window = [d for d, unit in zip(ds, units) if unit[0] == u]
            total = of_window[0]
            for d in of_window[1:]:
                total = total + d
            of_token = jnp.where(sames[u], total, 0.0)
            token_sum = of_token if u == 0 else token_sum + of_token
            pw_scr[...] += nn(pair_ref[w], total.astype(BF16))
            turned = total.T
            for h in range(heads):
                low = turned[h * rows : h * rows + half_rows]
                high = turned[h * rows + half_rows : (h + 1) * rows]
                at = slice(h * half_rows, (h + 1) * half_rows)
                mine_ref[w, at, :] = jnp.where(first_mine, low, high)
                theirs_ref[w, at, :] = jnp.where(first_mine, high, low).astype(BF16)
        tok_scr[...] += token_sum

    def gather_rows(s, b):
        dk, dv = None, None
        for w in range(max(0, b - 2 * span // rows), min(b, windows - 1) + 1):
            shift = jnp.clip(b * rows - starts_ref[w], -PAD, span)
            at = pl.ds(w * slot + PAD + shift, rows)
            k, v = dk_scr[s, at, :], dv_scr[s, at, :]
            dk, dv = (k, v) if dk is None else (dk + k, dv + v)
        return dk * (1.0 / LOG2E), dv

    halo_blocks = span // rows
    own_blocks = atoms // rows

    def project_halo(s, carry):
        for ref, first in ((before_ref, 0), (after_ref, span + atoms)):
            k_scr[s, first : first + span, :] = nn(ref[s], wk_ref[...]).astype(BF16).astype(F32)
            v_scr[s, first : first + span, :] = nn(ref[s], wv_ref[...]).astype(BF16).astype(F32)
        return carry

    edge_up = remote(after_ref, from_lower, edge_sems, 0, upper)
    edge_down = remote(before_ref, from_upper, edge_sems, 1, lower)

    def halo_gradient(s, carry):
        c = channels
        for first, ref in ((0, before_ref), (halo_blocks + own_blocks, after_ref)):
            parts = [gather_rows(s, b) for b in range(first, first + halo_blocks)]
            dkv = jnp.concatenate(
                [jnp.concatenate([p[i] for p in parts], axis=0).astype(BF16) for i in (0, 1)],
                axis=1,
            )
            weights = jnp.concatenate([wk_ref[...], wv_ref[...]], axis=1)
            from_kv = tn(ref[s], dkv)
            sums_b[0:c, :] += from_kv[:, 0:c]
            sums_b[c : 2 * c, :] += from_kv[:, c:]
            ref[s] = nt(dkv, weights).astype(BF16)
        return carry

    blocks = windows // TOGETHER
    early = (blocks - 1) // 2

    def step(it, carry):
        @pl.when(it == early)
        def _():
            @pl.when(has_upper)
            def _():
                for copy in halo_down:
                    copy.wait_recv()

            @pl.when(has_lower)
            def _():
                for copy in halo_up:
                    copy.wait_recv()

            code_column(0, code_before[...])
            code_column(span + atoms, code_after[...])
            lax.fori_loop(0, samples, project_halo, 0, unroll=unroll)

        @pl.when(it == early + 2)
        def _():
            lax.fori_loop(0, samples, halo_gradient, 0, unroll=unroll)

            @pl.when(has_upper)
            def _():
                edge_up.start()

            @pl.when(has_lower)
            def _():
                edge_down.start()

        block = jnp.where(
            it < early,
            it + 1,
            jnp.where(it == early, 0, jnp.where(it == early + 1, blocks - 1, it - 1)),
        )
        attend(block)
        return carry

    lax.fori_loop(0, blocks, step, 0)
    pair_copy = remote(theirs_ref, got, core_sems, 1, peer)
    pair_copy.start()
    shape = pw_scr.shape
    at_row = lax.broadcasted_iota(jnp.int32, shape, 0) // pair_channels
    at_col = lax.broadcasted_iota(jnp.int32, shape, 1) % rows
    diagonal = jnp.where(at_row == at_col, pw_scr[...], 0.0)
    by_channel = jnp.sum(diagonal.reshape(rows, pair_channels, stack), axis=0)
    by_channel = jnp.concatenate(
        [by_channel, jnp.zeros((channels - pair_channels, stack), F32)], axis=0
    )
    by_head = jnp.sum(by_channel.T.reshape(heads, rows, channels), axis=1)
    token_row = jnp.sum(tok_scr[...], axis=0, keepdims=True)
    lanes = lax.broadcasted_iota(jnp.int32, (1, stack), 1)
    by_token = jnp.zeros((1, stack), F32)
    for h in range(heads):
        one = jnp.sum(jnp.where(lanes // rows == h, token_row, 0.0), axis=1, keepdims=True)
        by_token = jnp.where(lanes == h, one, by_token)
    base = 3 * channels
    small_rows = 8 * pl.cdiv(heads + 1, 8)
    sums_a[base : base + heads, :] = by_head
    sums_a[base + heads : base + heads + 1, :] = by_token

    def halves(sums, got_half, slot):
        half = got_half.shape[0]
        theirs = pl.ds(pl.multiple_of(other * half, 8), half)
        return remote(sums.at[theirs], got_half, core_sems, slot, peer)

    def scattered(part, slots, first):
        return [
            remote(
                part.at[lax.rem(me + d, ranges)],
                slots.at[d - 1],
                scatter_sems,
                first + d - 1,
                everyone[d - 1],
            )
            for d in range(1, ranges)
        ]

    def gathered(total, chunk, first):
        place = pl.ds(pl.multiple_of((core * ranges + me) * chunk, 16), chunk)
        copies = [
            remote(total.at[place], total.at[place], gather_sems, first + d - 1, everyone[d - 1])
            for d in range(1, ranges)
        ]
        return place, copies

    def add_half(sums, got_half):
        half = got_half.shape[0]
        got_half[...] += sums[pl.ds(pl.multiple_of(core * half, 8), half), :]

    def add_chunks(got_half, slots):
        chunk = slots.shape[1]
        out = got_half[pl.ds(pl.multiple_of(me * chunk, 8), chunk), :]
        for d in range(1, ranges):
            out = out + slots[d - 1].astype(F32)
        return out.astype(BF16)

    def own_total(total, slot):
        half = total.shape[0] // 2
        at = pl.ds(pl.multiple_of(core * half, 16), half)
        return remote(total.at[at], total.at[at], core_sems, slot, peer)

    half_copy_a = halves(sums_a, half_a, 0)
    half_copy_b = halves(sums_b, half_b, 3)
    scatter_a = scattered(part_a, slots_a, 0)
    scatter_b = scattered(part_b, slots_b, ranges - 1)
    place_a, gather_a = gathered(total_a, slots_a.shape[1], 0)
    place_b, gather_b = gathered(total_b, slots_b.shape[1], ranges - 1)
    last_copy_a = own_total(total_a, 2)
    last_copy_b = own_total(total_b, 4)

    def own_weights(s, carry):
        c = channels
        sums = tn(act_ref[s], dqg_scr[s])
        sums_a[0:c, :] += sums[:, 0:c]
        sums_a[c : 2 * c, :] += sums[:, c:]
        sums_a[2 * c : 3 * c, :] += tn(gated_scr[s], grad_ref[s])
        return carry

    lax.fori_loop(0, samples, own_weights, 0, unroll=unroll)
    half_copy_a.start()

    def weight_gradients(s, carry):
        for b in range(halo_blocks, halo_blocks + own_blocks):
            dk, dv = gather_rows(s, b)
            k_scr[s, b * rows : (b + 1) * rows, :] = dk
            v_scr[s, b * rows : (b + 1) * rows, :] = dv
        c = channels
        own = slice(span, span + atoms)
        grads = jnp.concatenate(
            [k_scr[s, own, :].astype(BF16), v_scr[s, own, :].astype(BF16)], axis=1
        )
        sums = tn(act_ref[s], grads)
        sums_b[0:c, :] += sums[:, 0:c]
        sums_b[c : 2 * c, :] += sums[:, c:]
        return carry

    lax.fori_loop(0, unroll, weight_gradients, 0, unroll=unroll)
    half_copy_a.wait_recv()
    add_half(sums_a, half_a)
    half_size = half_a.shape[0]
    small = base % half_size
    rest = half_a[small : small + small_rows, :]
    rest = rest - rest.astype(BF16).astype(F32)
    low_rows = slice(small + small_rows, small + 2 * small_rows)
    half_a[low_rows, :] = jnp.where(core == base // half_size, rest, half_a[low_rows, :])
    part_a[...] = half_a[...].reshape(part_a.shape).astype(BF16)
    for copy in scatter_a:
        copy.start()
    lax.fori_loop(unroll, samples, weight_gradients, 0, unroll=unroll)
    half_copy_b.start()

    inner = slice(span, atoms - span)

    def own_gradient(s, carry):
        own = slice(span, span + atoms)
        dq = dqg_scr[s, :, 0:channels]
        dg = dqg_scr[s, :, channels:]
        grads = jnp.concatenate(
            [dq, k_scr[s, own, :].astype(BF16), v_scr[s, own, :].astype(BF16), dg], axis=1
        )
        weights = jnp.concatenate([wq_ref[...], wk_ref[...], wv_ref[...], wg_ref[...]], axis=1)
        ga = nt(grads, weights)
        dk_scr[s, 0:span, :] = ga[0:span]
        dk_scr[s, span : 2 * span, :] = ga[atoms - span :]
        q_scr[s, inner, :] = ga[inner].astype(BF16)
        return carry

    lax.fori_loop(0, 2, own_gradient, 0)
    half_copy_b.wait_recv()
    add_half(sums_b, half_b)
    part_b[...] = half_b[...].reshape(part_b.shape).astype(BF16)
    for copy in scatter_b:
        copy.start()
    lax.fori_loop(2, samples, own_gradient, 0, unroll=math.gcd(3, samples - 2))
    for copy in scatter_a:
        copy.wait_recv()
    total_a[place_a, :] = add_chunks(half_a, slots_a)
    for copy in gather_a:
        copy.start()

    lane_out = lax.broadcasted_iota(jnp.int32, (pair_channels, heads * half_rows), 1)
    spread_rows = jnp.zeros((pair_channels, heads * half_rows), F32)
    for h in range(heads):
        spread_rows = jnp.where(lane_out // half_rows == h, wpair_values[:, h : h + 1], spread_rows)
    weight = jnp.concatenate(
        [
            jnp.where(lane_out % half_rows == i, spread_rows, 0.0).astype(BF16)
            for i in range(half_rows)
        ],
        axis=0,
    )
    for copy in scatter_b:
        copy.wait_recv()
    total_b[place_b, :] = add_chunks(half_b, slots_b)
    for copy in gather_b:
        copy.start()
    for copy in gather_a:
        copy.wait_recv()
    last_copy_a.start()

    pair_copy.wait_recv()
    out_rows = half_rows * pair_channels

    def pair_gradient(w, carry):
        both = mine_ref[w] + got[w].astype(F32)
        high = both.astype(BF16)
        low = (both - high.astype(F32)).astype(BF16)
        pair_ref[w, 0:out_rows, :] = (nn(weight, high) + nn(weight, low)).astype(BF16)
        return carry

    lax.fori_loop(0, windows, pair_gradient, 0, unroll=math.gcd(5, windows))
    store_pair = pltpu.make_async_copy(
        pair_ref.at[:, pl.ds(0, out_rows)], pair_out_hbm, store_sems.at[0]
    )
    store_pair.start()

    for copy in gather_b:
        copy.wait_recv()
    last_copy_b.start()

    @pl.when(has_lower)
    def _():
        edge_down.wait_send()
        edge_up.wait_recv()

    @pl.when(has_upper)
    def _():
        edge_up.wait_send()
        edge_down.wait_recv()

    @pl.when(jnp.logical_not(has_lower))
    def _():
        from_lower[...] = jnp.zeros_like(from_lower)

    @pl.when(jnp.logical_not(has_upper))
    def _():
        from_upper[...] = jnp.zeros_like(from_upper)

    def add_edges(s, carry):
        q_scr[s, 0:span, :] = (dk_scr[s, 0:span, :] + from_lower[s].astype(F32)).astype(BF16)
        q_scr[s, atoms - span : atoms, :] = (
            dk_scr[s, span : 2 * span, :] + from_upper[s].astype(F32)
        ).astype(BF16)
        return carry

    lax.fori_loop(0, samples, add_edges, 0, unroll=unroll)
    store_act = pltpu.make_async_copy(q_scr, ga_hbm, store_sems.at[1])
    store_act.start()

    @pl.when(has_upper)
    def _():
        for copy in halo_up:
            copy.wait_send()

    @pl.when(has_lower)
    def _():
        for copy in halo_down:
            copy.wait_send()

    pair_copy.wait_send()
    half_copy_a.wait_send()
    half_copy_b.wait_send()
    last_copy_a.wait()
    last_copy_b.wait()
    c = channels
    sums_a[0:base, :] = total_a[0:base, :].astype(F32)
    sums_b[0 : 2 * c, :] = total_b[0 : 2 * c, :].astype(F32)
    stores = [
        pltpu.make_async_copy(src, weights_hbm.at[pl.ds(to, rows_of)], weight_sems.at[n])
        for n, (src, to, rows_of) in enumerate(
            (
                (sums_a.at[pl.ds(0, c)], 0, c),
                (sums_b.at[pl.ds(0, 2 * c)], c, 2 * c),
                (sums_a.at[pl.ds(c, 2 * c)], 3 * c, 2 * c),
            )
        )
    ]
    for store in stores:
        store.start()
    tail = total_a[base : base + 2 * small_rows, :].astype(F32)
    tail = tail[0:small_rows] + tail[small_rows:]
    pair_weight_ref[...] = tail[0:heads, 0:pair_channels]
    token_weight_ref[...] = tail[heads : heads + 1, 0:heads]
    for copy in scatter_a + scatter_b + gather_a + gather_b:
        copy.wait_send()
    store_pair.wait()
    store_act.wait()
    for store in stores:
        store.wait()


def finish_kernel(*refs):
    ins, outs, held = refs[0:5], refs[5:10], refs[10:13]
    load_sems, store_sems = refs[13:15]
    small = [
        pltpu.make_async_copy(ins[n], outs[n], store_sems.at[n]) for n in range(3, len(ins))
    ]
    loads = [pltpu.make_async_copy(ins[n], held[n], load_sems.at[n]) for n in range(3)]
    stores = [pltpu.make_async_copy(held[n], outs[n], store_sems.at[n]) for n in range(3)]
    for copy in loads + small:
        copy.start()
    for load, store in zip(loads, stores):
        load.wait()
        store.start()
    for copy in stores + small:
        copy.wait()


def per_device(
    act,
    grad_out,
    pair,
    w_query,
    w_key,
    w_value,
    w_gate,
    w_out,
    w_pair,
    w_token,
    offsets,
    atom_token,
    padding,
):
    samples, atoms, channels = act.shape
    windows = offsets.shape[0]
    rows = atoms // windows
    pair_channels, heads = w_pair.shape
    span = pair.shape[-1]
    stack = heads * rows
    half = rows // 2
    ranges = lax.axis_size("atoms")
    wide = atoms + 2 * span
    vmem = pl.BlockSpec(memory_space=pltpu.VMEM)
    smem = pl.BlockSpec(memory_space=pltpu.SMEM)
    anywhere = pl.BlockSpec(memory_space=pl.ANY)
    small_rows = 8 * pl.cdiv(heads + 1, 8)

    def sum_scratch(rows_of):
        chunk = 16 * pl.cdiv(rows_of, 32 * ranges)
        half_size = ranges * chunk
        return [
            pltpu.VMEM((2 * half_size, channels), F32),
            pltpu.VMEM((half_size, channels), F32),
            pltpu.VMEM((ranges, chunk, channels), BF16),
            pltpu.VMEM((ranges - 1, chunk, channels), BF16),
            pltpu.VMEM((2 * half_size, channels), BF16),
        ]

    def kernel(*refs):
        fused_kernel(ranges, *refs)

    edge = pltpu.VMEM((samples, span, channels), BF16)
    slot_rows = windows * (span + PAD) + PAD
    results = pl.pallas_call(
        kernel,
        out_shape=(
            jax.ShapeDtypeStruct((samples, atoms, channels), BF16),
            jax.ShapeDtypeStruct((windows, half * pair_channels, span), BF16),
            jax.ShapeDtypeStruct((5 * channels, channels), F32),
            jax.ShapeDtypeStruct((heads, pair_channels), F32),
            jax.ShapeDtypeStruct((1, heads), F32),
        ),
        in_specs=[smem] * 3 + [anywhere] * 3 + [vmem] * 7,
        out_specs=(anywhere, anywhere, anywhere, vmem, vmem),
        scratch_shapes=[
            pltpu.VMEM((samples, atoms, channels), BF16),
            pltpu.VMEM((samples, atoms, channels), BF16),
            pltpu.VMEM((windows, rows * pair_channels, span), BF16),
            edge,
            edge,
            pltpu.VMEM((atoms // span, 1, span), jnp.int32),
            pltpu.VMEM((1, span), jnp.int32),
            pltpu.VMEM((1, span), jnp.int32),
            pltpu.VMEM((samples, wide, channels), F32),
            pltpu.VMEM((samples, wide, channels), F32),
            pltpu.VMEM((samples, atoms, channels), BF16),
            pltpu.VMEM((samples, atoms, channels), BF16),
            pltpu.VMEM((samples, atoms, channels), F32),
            pltpu.VMEM((samples, atoms, 2 * channels), BF16),
            pltpu.VMEM((samples, atoms, channels), BF16),
            pltpu.VMEM((samples, slot_rows, channels), F32),
            pltpu.VMEM((samples, slot_rows, channels), F32),
            pltpu.VMEM((rows * pair_channels, stack), F32),
            pltpu.VMEM((span, stack), F32),
            pltpu.VMEM((rows * pair_channels, stack), BF16),
            pltpu.VMEM((wide, stack), F32),
            pltpu.VMEM((windows, 1, stack), F32),
            pltpu.VMEM((windows, heads * half, span), F32),
            pltpu.VMEM((windows, heads * half, span), BF16),
            pltpu.VMEM((windows, heads * half, span), BF16),
            edge,
            edge,
            *sum_scratch(3 * channels + 2 * small_rows),
            *sum_scratch(2 * channels),
            pltpu.SMEM((windows,), jnp.int32),
            pltpu.SemaphoreType.DMA((3,)),
            pltpu.SemaphoreType.DMA((2,)),
            pltpu.SemaphoreType.DMA((2, 4)),
            pltpu.SemaphoreType.DMA((2, 2)),
            pltpu.SemaphoreType.DMA((2, 5)),
            pltpu.SemaphoreType.DMA((2, 2 * (ranges - 1))),
            pltpu.SemaphoreType.DMA((2, 2 * (ranges - 1))),
            pltpu.SemaphoreType.DMA((3,)),
        ],
        compiler_params=pltpu.CompilerParams(
            collective_id=0, has_side_effects=True, vmem_limit_bytes=63 * 1024 * 1024
        ),
        name="fused",
    )(
        offsets,
        w_token,
        padding,
        act,
        grad_out,
        pair.reshape(windows, rows * pair_channels, span),
        atom_token.reshape(atoms // span, span),
        w_query,
        w_key,
        w_value,
        w_gate,
        w_out,
        w_pair.T,
    )

    grad_act, grad_pair, weights, pair_weight, token_weight = pl.pallas_call(
        finish_kernel,
        out_shape=tuple(jax.ShapeDtypeStruct(r.shape, r.dtype) for r in results),
        in_specs=[anywhere] * 5,
        out_specs=(anywhere,) * 5,
        scratch_shapes=[pltpu.VMEM(r.shape, r.dtype) for r in results[:3]]
        + [pltpu.SemaphoreType.DMA((3,)), pltpu.SemaphoreType.DMA((5,))],
        name="finish",
    )(*results)

    grad_weights = weights.reshape(5, channels, channels)
    grad_pair_weight = pair_weight.T
    grad_token_weight = token_weight.reshape(heads)
    grad_pair = grad_pair.reshape(windows, half, pair_channels, span)
    return (grad_act, grad_pair, grad_weights, grad_pair_weight, grad_token_weight)


def solution(mesh):
    in_specs = (
        P("samples", ("groups", "atoms"), None),
        P("samples", ("groups", "atoms"), None),
        P(("groups", "atoms"), None, None, None),
        P(),
        P(),
        P(),
        P(),
        P(),
        P(),
        P(),
        P(("groups", "atoms")),
        P(("groups", "atoms")),
        P(("groups", "atoms")),
    )
    out_specs = (
        P("samples", ("groups", "atoms"), None),
        P(("groups", "atoms"), "samples", None, None),
        P("groups", None, None),
        P("groups", None),
        P("groups"),
    )
    return jax.shard_map(
        per_device, mesh=mesh, in_specs=in_specs, out_specs=out_specs, check_vma=False
    )
```

```python
import math

import jax
import jax.numpy as jnp
from jax import lax
from jax.experimental import pallas as pl
from jax.experimental.pallas import tpu as pltpu
from jax.sharding import PartitionSpec as P

MASKED = -1000000000.0
BF16 = jnp.bfloat16
F32 = jnp.float32
LOG2E = math.log2(math.e)
TOGETHER = 4
PAD = 32


def nn(a, b):
    return lax.dot_general(a, b, (((1,), (0,)), ((), ())), preferred_element_type=F32)


def nt(a, b):
    return lax.dot_general(a, b, (((1,), (1,)), ((), ())), preferred_element_type=F32)


def tn(a, b):
    return lax.dot_general(a, b, (((0,), (0,)), ((), ())), preferred_element_type=F32)


def greet(barrier, devices):
    for device in devices:
        pl.semaphore_signal(
            barrier, inc=1, device_id=device, device_id_type=pl.DeviceIdType.MESH
        )


def remote(src, dst, sems, slot, device):
    return pltpu.make_async_remote_copy(
        src_ref=src,
        dst_ref=dst,
        send_sem=sems.at[0, slot],
        recv_sem=sems.at[1, slot],
        device_id=device,
        device_id_type=pl.DeviceIdType.MESH,
    )


def fused_kernel(
    ranges,
    offsets_ref,
    wtoken_ref,
    padding_ref,
    act_hbm,
    grad_hbm,
    pair_hbm,
    token_ref,
    wq_ref,
    wk_ref,
    wv_ref,
    wg_ref,
    wo_ref,
    wpair_ref,
    ga_hbm,
    pair_out_hbm,
    weights_hbm,
    pair_weight_ref,
    token_weight_ref,
    act_ref,
    grad_ref,
    pair_ref,
    before_ref,
    after_ref,
    code_scr,
    code_before,
    code_after,
    k_scr,
    v_scr,
    q_scr,
    da_scr,
    gate_scr,
    gyg_scr,
    dqg_scr,
    gated_scr,
    dk_scr,
    dv_scr,
    pw_scr,
    tok_scr,
    wpair_scr,
    key_code_scr,
    query_code_scr,
    mine_ref,
    theirs_ref,
    got,
    from_lower,
    from_upper,
    sums_ref,
    got_half,
    part_b,
    slots,
    total_ref,
    starts_ref,
    load_sems,
    store_sems,
    halo_sems,
    edge_sems,
    core_sems,
    scatter_sems,
    gather_sems,
):
    me = lax.axis_index("atoms")
    core = lax.axis_index("samples")
    other = 1 - core
    samples, atoms, channels = act_ref.shape
    windows = pair_ref.shape[0]
    rows = atoms // windows
    span = before_ref.shape[1]
    wide = atoms + 2 * span
    pair_channels = wpair_ref.shape[1]
    heads = wpair_ref.shape[0]
    head_dim = channels // heads
    scale = 1.0 / math.sqrt(head_dim)
    stack = heads * rows
    half_rows = rows // 2
    chunk = part_b.shape[1]
    half = ranges * chunk
    unroll = math.gcd(4, samples)
    has_lower, has_upper = me > 0, me < ranges - 1
    lower, upper, peer = {"atoms": me - 1}, {"atoms": me + 1}, {"samples": other}
    everyone = [{"atoms": lax.rem(me + d, ranges)} for d in range(1, ranges)]

    barrier = pltpu.get_barrier_semaphore()
    greet(barrier, [peer] + everyone)
    load_act = pltpu.make_async_copy(act_hbm, act_ref, load_sems.at[0])
    load_grad = pltpu.make_async_copy(grad_hbm, grad_ref, load_sems.at[1])
    load_pair = pltpu.make_async_copy(pair_hbm, pair_ref, load_sems.at[2])
    load_act.start()
    load_grad.start()
    load_pair.start()

    code_rows = atoms // span
    live_end = atoms - padding_ref[0]
    lane_at = lax.broadcasted_iota(jnp.int32, (1, span), 1)
    for r in range(code_rows):
        code_scr[r] = jnp.where(lane_at + r * span < live_end, token_ref[r : r + 1, :] + 1, 0)

    pl.semaphore_wait(barrier, ranges)
    halo_up = [
        remote(act_hbm.at[:, pl.ds(atoms - span, span)], before_ref, halo_sems, 0, upper),
        remote(code_scr.at[code_rows - 1], code_before, halo_sems, 1, upper),
    ]
    halo_down = [
        remote(act_hbm.at[:, pl.ds(0, span)], after_ref, halo_sems, 2, lower),
        remote(code_scr.at[0], code_after, halo_sems, 3, lower),
    ]

    @pl.when(has_upper)
    def _():
        for copy in halo_up:
            copy.start()

    @pl.when(has_lower)
    def _():
        for copy in halo_down:
            copy.start()

    @pl.when(jnp.logical_not(has_lower))
    def _():
        before_ref[...] = jnp.zeros_like(before_ref)
        code_before[...] = jnp.zeros_like(code_before)

    @pl.when(jnp.logical_not(has_upper))
    def _():
        after_ref[...] = jnp.zeros_like(after_ref)
        code_after[...] = jnp.zeros_like(code_after)

    def code_column(first, row):
        column = jnp.broadcast_to(row.astype(F32), (stack, span)).T
        key_code_scr[first : first + span, :] = column

    lane_row = lax.broadcasted_iota(jnp.int32, (pair_channels, stack), 1) % rows
    lane_head = lax.broadcasted_iota(jnp.int32, (pair_channels, stack), 1) // rows
    wpair_values = wpair_ref[...].astype(F32).T
    wpair_rows = jnp.zeros((pair_channels, stack), F32)
    wtoken_row = jnp.zeros((1, stack), F32)
    for h in range(heads):
        wpair_rows = jnp.where(lane_head == h, wpair_values[:, h : h + 1], wpair_rows)
        wtoken_row = jnp.where(lane_head[0:1] == h, wtoken_ref[h], wtoken_row)
    for i in range(rows):
        wpair_scr[i * pair_channels : (i + 1) * pair_channels, :] = jnp.where(
            lane_row == i, wpair_rows, 0.0
        ).astype(BF16)
    for r in range(code_rows):
        code_column(span + r * span, code_scr[r])
        tokens = (token_ref[r : r + 1, :] + 1).astype(F32)
        for u in range(span // rows):
            piece = tokens[:, u * rows : (u + 1) * rows]
            query_code_scr[r * (span // rows) + u] = jnp.concatenate([piece] * heads, axis=1)
    pw_scr[...] = jnp.zeros_like(pw_scr)
    tok_scr[...] = jnp.zeros_like(tok_scr)
    sums_ref[...] = jnp.zeros_like(sums_ref)
    anchor = me * atoms
    last_start = ranges * atoms - span
    for w in range(windows):
        starts_ref[w] = (
            jnp.clip(anchor + w * rows + offsets_ref[w], 0, last_start) - anchor + span
        )

    load_act.wait()
    load_grad.wait()
    slot = span + PAD

    def project(s, carry):
        own = act_ref[s]
        q_scr[s] = (nn(own, wq_ref[...]) * (scale * LOG2E)).astype(BF16)
        gate = jax.nn.sigmoid(nn(own, wg_ref[...]))
        gated_gy = nt(grad_ref[s], wo_ref[...]) * gate
        gate_scr[s] = gate
        da_scr[s] = gated_gy.astype(BF16)
        gyg_scr[s] = gated_gy * (1.0 - gate)
        k_scr[s, span : span + atoms, :] = nn(own, wk_ref[...]).astype(BF16).astype(F32)
        v_scr[s, span : span + atoms, :] = nn(own, wv_ref[...]).astype(BF16).astype(F32)
        blank = jnp.zeros((PAD, channels), F32)
        for w in range(windows + 1):
            dk_scr[s, w * slot : w * slot + PAD, :] = blank
            dv_scr[s, w * slot : w * slot + PAD, :] = blank
        return carry

    lax.fori_loop(0, samples, project, 0, unroll=unroll)
    load_pair.wait()

    row_head = lax.broadcasted_iota(jnp.int32, (stack, channels), 0) // rows
    column_head = lax.broadcasted_iota(jnp.int32, (stack, channels), 1) // head_dim
    head_mask = jnp.where(row_head == column_head, 1.0, 0.0).astype(BF16)
    lane = lax.broadcasted_iota(jnp.int32, (rows, channels), 1) // head_dim
    head_is = [lane == h for h in range(heads)]
    first_mine = core == 0

    def spread(x):
        return jnp.concatenate([x] * heads, axis=0) * head_mask

    def collect(x):
        out = x[0:rows]
        for h in range(1, heads):
            out = jnp.where(head_is[h], x[h * rows : (h + 1) * rows], out)
        return out

    def attend(block):
        ws = [block * TOGETHER + u for u in range(TOGETHER)]
        mine_rows = [pl.ds(pl.multiple_of(w * rows, rows), rows) for w in ws]
        key_rows = [pl.ds(starts_ref[w], span) for w in ws]
        slot_rows = [pl.ds(pl.multiple_of(w * slot + PAD, 8), span) for w in ws]
        sames, biases = [], []
        for u, w in enumerate(ws):
            key_code = key_code_scr[key_rows[u], :]
            same = key_code == query_code_scr[w]
            bias = (tn(pair_ref[w], wpair_scr[...]) + jnp.where(same, wtoken_row, 0.0)) * LOG2E
            biases.append(jnp.where(key_code > 0.0, bias, MASKED))
            sames.append(same)
        units = [(u, s) for u in range(TOGETHER) for s in range(samples)]
        keys = [k_scr[s, key_rows[u], :].astype(BF16) for u, s in units]
        values = [v_scr[s, key_rows[u], :].astype(BF16) for u, s in units]
        qm = [spread(q_scr[s, mine_rows[u], :]) for u, s in units]
        dam = [spread(da_scr[s, mine_rows[u], :]) for u, s in units]
        scores = [nt(k, q) + biases[u] for k, q, (u, s) in zip(keys, qm, units)]
        dprobs = [nt(v, d) for v, d in zip(values, dam)]
        tops = [jnp.max(x, axis=0, keepdims=True) for x in scores]
        exps = [jnp.exp2(x - t) for x, t in zip(scores, tops)]
        probs = [e * (1.0 / jnp.sum(e, axis=0, keepdims=True)) for e in exps]
        probs_b = [p.astype(BF16) for p in probs]
        for (u, s), p, d in zip(units, probs_b, dam):
            dv_scr[s, slot_rows[u], :] = nn(p, d)
        ds = [p * (d - jnp.sum(p * d, axis=0, keepdims=True)) for p, d in zip(probs, dprobs)]
        ds_b = [d.astype(BF16) for d in ds]
        for (u, s), d, q in zip(units, ds_b, qm):
            dk_scr[s, slot_rows[u], :] = nn(d, q)
        for (u, s), p, v in zip(units, probs_b, values):
            a = collect(tn(p, v))
            gated_scr[s, mine_rows[u], :] = (gate_scr[s, mine_rows[u], :] * a).astype(BF16)
            dqg_scr[s, mine_rows[u], channels:] = (gyg_scr[s, mine_rows[u], :] * a).astype(BF16)
        for (u, s), d, k in zip(units, ds_b, keys):
            dqg_scr[s, mine_rows[u], 0:channels] = (collect(tn(d, k)) * scale).astype(BF16)
        for u, w in enumerate(ws):
            of_window = [d for d, unit in zip(ds, units) if unit[0] == u]
            total = of_window[0]
            for d in of_window[1:]:
                total = total + d
            of_token = jnp.where(sames[u], total, 0.0)
            token_sum = of_token if u == 0 else token_sum + of_token
            pw_scr[...] += nn(pair_ref[w], total.astype(BF16))
            turned = total.T
            for h in range(heads):
                low = turned[h * rows : h * rows + half_rows]
                high = turned[h * rows + half_rows : (h + 1) * rows]
                at = slice(h * half_rows, (h + 1) * half_rows)
                mine_ref[w, at, :] = jnp.where(first_mine, low, high)
                theirs_ref[w, at, :] = jnp.where(first_mine, high, low).astype(BF16)
        tok_scr[...] += token_sum

    def gather_rows(s, b):
        dk, dv = None, None
        for w in range(max(0, b - 2 * span // rows), min(b, windows - 1) + 1):
            shift = jnp.clip(b * rows - starts_ref[w], -PAD, span)
            at = pl.ds(w * slot + PAD + shift, rows)
            k, v = dk_scr[s, at, :], dv_scr[s, at, :]
            dk, dv = (k, v) if dk is None else (dk + k, dv + v)
        return dk * (1.0 / LOG2E), dv

    halo_blocks = span // rows
    own_blocks = atoms // rows

    def project_halo(s, carry):
        for ref, first in ((before_ref, 0), (after_ref, span + atoms)):
            k_scr[s, first : first + span, :] = nn(ref[s], wk_ref[...]).astype(BF16).astype(F32)
            v_scr[s, first : first + span, :] = nn(ref[s], wv_ref[...]).astype(BF16).astype(F32)
        return carry

    edge_up = remote(after_ref, from_lower, edge_sems, 0, upper)
    edge_down = remote(before_ref, from_upper, edge_sems, 1, lower)

    def halo_gradient(s, carry):
        c = channels
        for first, ref in ((0, before_ref), (halo_blocks + own_blocks, after_ref)):
            parts = [gather_rows(s, b) for b in range(first, first + halo_blocks)]
            dkv = jnp.concatenate(
                [jnp.concatenate([p[i] for p in parts], axis=0).astype(BF16) for i in (0, 1)],
                axis=1,
            )
            weights = jnp.concatenate([wk_ref[...], wv_ref[...]], axis=1)
            from_kv = tn(ref[s], dkv)
            sums_ref[c : 2 * c, :] += from_kv[:, 0:c]
            sums_ref[2 * c : 3 * c, :] += from_kv[:, c:]
            ref[s] = nt(dkv, weights).astype(BF16)
        return carry

    blocks = windows // TOGETHER
    early = blocks - 2

    def step(it, carry):
        @pl.when(it == early)
        def _():
            @pl.when(has_upper)
            def _():
                for copy in halo_down:
                    copy.wait_recv()

            @pl.when(has_lower)
            def _():
                for copy in halo_up:
                    copy.wait_recv()

            code_column(0, code_before[...])
            code_column(span + atoms, code_after[...])
            lax.fori_loop(0, samples, project_halo, 0, unroll=unroll)

        block = jnp.where(
            it < early,
            it + 1,
            jnp.where(it == early, 0, blocks - 1),
        )
        attend(block)
        return carry

    lax.fori_loop(0, blocks, step, 0)
    pair_copy = remote(theirs_ref, got, core_sems, 1, peer)
    pair_copy.start()
    lax.fori_loop(0, samples, halo_gradient, 0, unroll=unroll)

    @pl.when(has_upper)
    def _():
        edge_up.start()

    @pl.when(has_lower)
    def _():
        edge_down.start()

    shape = pw_scr.shape
    at_row = lax.broadcasted_iota(jnp.int32, shape, 0) // pair_channels
    at_col = lax.broadcasted_iota(jnp.int32, shape, 1) % rows
    diagonal = jnp.where(at_row == at_col, pw_scr[...], 0.0)
    by_channel = jnp.sum(diagonal.reshape(rows, pair_channels, stack), axis=0)
    by_channel = jnp.concatenate(
        [by_channel, jnp.zeros((channels - pair_channels, stack), F32)], axis=0
    )
    by_head = jnp.sum(by_channel.T.reshape(heads, rows, channels), axis=1)
    token_row = jnp.sum(tok_scr[...], axis=0, keepdims=True)
    lanes = lax.broadcasted_iota(jnp.int32, (1, stack), 1)
    by_token = jnp.zeros((1, stack), F32)
    for h in range(heads):
        one = jnp.sum(jnp.where(lanes // rows == h, token_row, 0.0), axis=1, keepdims=True)
        by_token = jnp.where(lanes == h, one, by_token)
    base = 5 * channels
    small_rows = 8 * pl.cdiv(heads + 1, 8)
    sums_ref[base : base + heads, :] = by_head
    sums_ref[base + heads : base + heads + 1, :] = by_token

    def weight_gradients(s, carry):
        for b in range(halo_blocks, halo_blocks + own_blocks):
            dk, dv = gather_rows(s, b)
            k_scr[s, b * rows : (b + 1) * rows, :] = dk
            v_scr[s, b * rows : (b + 1) * rows, :] = dv
        c = channels
        own = slice(span, span + atoms)
        grads = jnp.concatenate(
            [
                dqg_scr[s, :, 0:c],
                k_scr[s, own, :].astype(BF16),
                v_scr[s, own, :].astype(BF16),
                dqg_scr[s, :, c:],
            ],
            axis=1,
        )
        sums = tn(act_ref[s], grads)
        for n in range(4):
            sums_ref[n * c : (n + 1) * c, :] += sums[:, n * c : (n + 1) * c]
        sums_ref[4 * c : 5 * c, :] += tn(gated_scr[s], grad_ref[s])
        return carry

    lax.fori_loop(0, samples, weight_gradients, 0, unroll=unroll)
    half_copy = remote(
        sums_ref.at[pl.ds(pl.multiple_of(other * half, 8), half)], got_half, core_sems, 0, peer
    )
    half_copy.start()

    inner = slice(span, atoms - span)

    def own_gradient(s, carry):
        own = slice(span, span + atoms)
        dq = dqg_scr[s, :, 0:channels]
        dg = dqg_scr[s, :, channels:]
        grads = jnp.concatenate(
            [dq, k_scr[s, own, :].astype(BF16), v_scr[s, own, :].astype(BF16), dg], axis=1
        )
        weights = jnp.concatenate([wq_ref[...], wk_ref[...], wv_ref[...], wg_ref[...]], axis=1)
        ga = nt(grads, weights)
        dk_scr[s, 0:span, :] = ga[0:span]
        dk_scr[s, span : 2 * span, :] = ga[atoms - span :]
        q_scr[s, inner, :] = ga[inner].astype(BF16)
        return carry

    lax.fori_loop(0, 2, own_gradient, 0)
    half_copy.wait_recv()
    own_half = pl.ds(pl.multiple_of(core * half, 16), half)
    small = base % half
    got_half[...] += sums_ref[own_half, :]
    rest = got_half[small : small + small_rows, :]
    rest = rest - rest.astype(BF16).astype(F32)
    low_rows = slice(small + small_rows, small + 2 * small_rows)
    got_half[low_rows, :] = jnp.where(core == base // half, rest, got_half[low_rows, :])
    part_b[...] = got_half[...].reshape(part_b.shape).astype(BF16)
    scatter = []
    for d in range(1, ranges):
        target = lax.rem(me + d, ranges)
        copy = remote(part_b.at[target], slots.at[d - 1], scatter_sems, d - 1, everyone[d - 1])
        copy.start()
        scatter.append(copy)
    lax.fori_loop(2, samples, own_gradient, 0, unroll=math.gcd(3, samples - 2))

    lane_out = lax.broadcasted_iota(jnp.int32, (pair_channels, heads * half_rows), 1)
    spread_rows = jnp.zeros((pair_channels, heads * half_rows), F32)
    for h in range(heads):
        spread_rows = jnp.where(lane_out // half_rows == h, wpair_values[:, h : h + 1], spread_rows)
    weight = jnp.concatenate(
        [
            jnp.where(lane_out % half_rows == i, spread_rows, 0.0).astype(BF16)
            for i in range(half_rows)
        ],
        axis=0,
    )
    for copy in scatter:
        copy.wait_recv()
    chunk_total = got_half[pl.ds(pl.multiple_of(me * chunk, 8), chunk), :]
    for d in range(1, ranges):
        chunk_total = chunk_total + slots[d - 1].astype(F32)
    place = pl.ds(pl.multiple_of(core * half + me * chunk, 16), chunk)
    total_ref[place, :] = chunk_total.astype(BF16)
    gather = []
    for d in range(1, ranges):
        copy = remote(
            total_ref.at[place], total_ref.at[place], gather_sems, d - 1, everyone[d - 1]
        )
        copy.start()
        gather.append(copy)

    pair_copy.wait_recv()
    out_rows = half_rows * pair_channels

    def pair_gradient(w, carry):
        both = mine_ref[w] + got[w].astype(F32)
        high = both.astype(BF16)
        low = (both - high.astype(F32)).astype(BF16)
        pair_ref[w, 0:out_rows, :] = (nn(weight, high) + nn(weight, low)).astype(BF16)
        return carry

    lax.fori_loop(0, windows, pair_gradient, 0, unroll=math.gcd(5, windows))
    store_pair = pltpu.make_async_copy(
        pair_ref.at[:, pl.ds(0, out_rows)], pair_out_hbm, store_sems.at[0]
    )
    store_pair.start()

    for copy in gather:
        copy.wait_recv()
    last_copy = remote(
        total_ref.at[own_half], total_ref.at[own_half], core_sems, 2, peer
    )
    last_copy.start()

    @pl.when(has_lower)
    def _():
        edge_down.wait_send()
        edge_up.wait_recv()

    @pl.when(has_upper)
    def _():
        edge_up.wait_send()
        edge_down.wait_recv()

    @pl.when(jnp.logical_not(has_lower))
    def _():
        from_lower[...] = jnp.zeros_like(from_lower)

    @pl.when(jnp.logical_not(has_upper))
    def _():
        from_upper[...] = jnp.zeros_like(from_upper)

    def add_edges(s, carry):
        q_scr[s, 0:span, :] = (dk_scr[s, 0:span, :] + from_lower[s].astype(F32)).astype(BF16)
        q_scr[s, atoms - span : atoms, :] = (
            dk_scr[s, span : 2 * span, :] + from_upper[s].astype(F32)
        ).astype(BF16)
        return carry

    lax.fori_loop(0, samples, add_edges, 0, unroll=unroll)
    store_act = pltpu.make_async_copy(q_scr, ga_hbm, store_sems.at[1])
    store_act.start()

    @pl.when(has_upper)
    def _():
        for copy in halo_up:
            copy.wait_send()

    @pl.when(has_lower)
    def _():
        for copy in halo_down:
            copy.wait_send()

    half_copy.wait_send()
    pair_copy.wait_send()
    for copy in scatter + gather:
        copy.wait_send()
    last_copy.wait()
    sums_ref[0:base, :] = total_ref[0:base, :].astype(F32)
    store_weights = pltpu.make_async_copy(
        sums_ref.at[pl.ds(0, base)], weights_hbm, store_sems.at[2]
    )
    store_weights.start()
    tail = total_ref[base : base + 2 * small_rows, :].astype(F32)
    tail = tail[0:small_rows] + tail[small_rows:]
    pair_weight_ref[...] = tail[0:heads, 0:pair_channels]
    token_weight_ref[...] = tail[heads : heads + 1, 0:heads]
    store_weights.wait()
    store_pair.wait()
    store_act.wait()


def finish_kernel(*refs):
    ins, outs, held = refs[0:5], refs[5:10], refs[10:13]
    load_sems, store_sems = refs[13:15]
    small = [
        pltpu.make_async_copy(ins[n], outs[n], store_sems.at[n]) for n in range(3, len(ins))
    ]
    loads = [pltpu.make_async_copy(ins[n], held[n], load_sems.at[n]) for n in range(3)]
    stores = [pltpu.make_async_copy(held[n], outs[n], store_sems.at[n]) for n in range(3)]
    for copy in loads + small:
        copy.start()
    for load, store in zip(loads, stores):
        load.wait()
        store.start()
    for copy in stores + small:
        copy.wait()


def per_device(
    act,
    grad_out,
    pair,
    w_query,
    w_key,
    w_value,
    w_gate,
    w_out,
    w_pair,
    w_token,
    offsets,
    atom_token,
    padding,
):
    samples, atoms, channels = act.shape
    windows = offsets.shape[0]
    rows = atoms // windows
    pair_channels, heads = w_pair.shape
    span = pair.shape[-1]
    stack = heads * rows
    half = rows // 2
    ranges = lax.axis_size("atoms")
    wide = atoms + 2 * span
    vmem = pl.BlockSpec(memory_space=pltpu.VMEM)
    smem = pl.BlockSpec(memory_space=pltpu.SMEM)
    anywhere = pl.BlockSpec(memory_space=pl.ANY)
    small_rows = 8 * pl.cdiv(heads + 1, 8)
    chunk = 16 * pl.cdiv(5 * channels + 2 * small_rows, 32 * ranges)
    sum_rows = 2 * ranges * chunk

    def kernel(*refs):
        fused_kernel(ranges, *refs)

    edge = pltpu.VMEM((samples, span, channels), BF16)
    slot_rows = windows * (span + PAD) + PAD
    results = pl.pallas_call(
        kernel,
        out_shape=(
            jax.ShapeDtypeStruct((samples, atoms, channels), BF16),
            jax.ShapeDtypeStruct((windows, half * pair_channels, span), BF16),
            jax.ShapeDtypeStruct((5 * channels, channels), F32),
            jax.ShapeDtypeStruct((heads, pair_channels), F32),
            jax.ShapeDtypeStruct((1, heads), F32),
        ),
        in_specs=[smem] * 3 + [anywhere] * 3 + [vmem] * 7,
        out_specs=(anywhere, anywhere, anywhere, vmem, vmem),
        scratch_shapes=[
            pltpu.VMEM((samples, atoms, channels), BF16),
            pltpu.VMEM((samples, atoms, channels), BF16),
            pltpu.VMEM((windows, rows * pair_channels, span), BF16),
            edge,
            edge,
            pltpu.VMEM((atoms // span, 1, span), jnp.int32),
            pltpu.VMEM((1, span), jnp.int32),
            pltpu.VMEM((1, span), jnp.int32),
            pltpu.VMEM((samples, wide, channels), F32),
            pltpu.VMEM((samples, wide, channels), F32),
            pltpu.VMEM((samples, atoms, channels), BF16),
            pltpu.VMEM((samples, atoms, channels), BF16),
            pltpu.VMEM((samples, atoms, channels), F32),
            pltpu.VMEM((samples, atoms, channels), F32),
            pltpu.VMEM((samples, atoms, 2 * channels), BF16),
            pltpu.VMEM((samples, atoms, channels), BF16),
            pltpu.VMEM((samples, slot_rows, channels), F32),
            pltpu.VMEM((samples, slot_rows, channels), F32),
            pltpu.VMEM((rows * pair_channels, stack), F32),
            pltpu.VMEM((span, stack), F32),
            pltpu.VMEM((rows * pair_channels, stack), BF16),
            pltpu.VMEM((wide, stack), F32),
            pltpu.VMEM((windows, 1, stack), F32),
            pltpu.VMEM((windows, heads * half, span), F32),
            pltpu.VMEM((windows, heads * half, span), BF16),
            pltpu.VMEM((windows, heads * half, span), BF16),
            edge,
            edge,
            pltpu.VMEM((sum_rows, channels), F32),
            pltpu.VMEM((ranges * chunk, channels), F32),
            pltpu.VMEM((ranges, chunk, channels), BF16),
            pltpu.VMEM((ranges - 1, chunk, channels), BF16),
            pltpu.VMEM((sum_rows, channels), BF16),
            pltpu.SMEM((windows,), jnp.int32),
            pltpu.SemaphoreType.DMA((3,)),
            pltpu.SemaphoreType.DMA((3,)),
            pltpu.SemaphoreType.DMA((2, 4)),
            pltpu.SemaphoreType.DMA((2, 2)),
            pltpu.SemaphoreType.DMA((2, 3)),
            pltpu.SemaphoreType.DMA((2, ranges - 1)),
            pltpu.SemaphoreType.DMA((2, ranges - 1)),
        ],
        compiler_params=pltpu.CompilerParams(
            collective_id=0, has_side_effects=True, vmem_limit_bytes=63 * 1024 * 1024
        ),
        name="fused",
    )(
        offsets,
        w_token,
        padding,
        act,
        grad_out,
        pair.reshape(windows, rows * pair_channels, span),
        atom_token.reshape(atoms // span, span),
        w_query,
        w_key,
        w_value,
        w_gate,
        w_out,
        w_pair.T,
    )

    grad_act, grad_pair, weights, pair_weight, token_weight = pl.pallas_call(
        finish_kernel,
        out_shape=tuple(jax.ShapeDtypeStruct(r.shape, r.dtype) for r in results),
        in_specs=[anywhere] * 5,
        out_specs=(anywhere,) * 5,
        scratch_shapes=[pltpu.VMEM(r.shape, r.dtype) for r in results[:3]]
        + [pltpu.SemaphoreType.DMA((3,)), pltpu.SemaphoreType.DMA((5,))],
        name="finish",
    )(*results)

    grad_weights = weights.reshape(5, channels, channels)
    grad_pair_weight = pair_weight.T
    grad_token_weight = token_weight.reshape(heads)
    grad_pair = grad_pair.reshape(windows, half, pair_channels, span)
    return (grad_act, grad_pair, grad_weights, grad_pair_weight, grad_token_weight)


def solution(mesh):
    in_specs = (
        P("samples", ("groups", "atoms"), None),
        P("samples", ("groups", "atoms"), None),
        P(("groups", "atoms"), None, None, None),
        P(),
        P(),
        P(),
        P(),
        P(),
        P(),
        P(),
        P(("groups", "atoms")),
        P(("groups", "atoms")),
        P(("groups", "atoms")),
    )
    out_specs = (
        P("samples", ("groups", "atoms"), None),
        P(("groups", "atoms"), "samples", None, None),
        P("groups", None, None),
        P("groups", None),
        P("groups"),
    )
    return jax.shard_map(
        per_device, mesh=mesh, in_specs=in_specs, out_specs=out_specs, check_vma=False
    )
```

```python
import math

import jax
import jax.numpy as jnp
from jax import lax
from jax.experimental import pallas as pl
from jax.experimental.pallas import tpu as pltpu
from jax.sharding import PartitionSpec as P

MASKED = -1000000000.0
BF16 = jnp.bfloat16
F32 = jnp.float32
LOG2E = math.log2(math.e)
TOGETHER = 4
PAD = 32


def nn(a, b):
    return lax.dot_general(a, b, (((1,), (0,)), ((), ())), preferred_element_type=F32)


def nt(a, b):
    return lax.dot_general(a, b, (((1,), (1,)), ((), ())), preferred_element_type=F32)


def tn(a, b):
    return lax.dot_general(a, b, (((0,), (0,)), ((), ())), preferred_element_type=F32)


def greet(barrier, devices):
    for device in devices:
        pl.semaphore_signal(
            barrier, inc=1, device_id=device, device_id_type=pl.DeviceIdType.MESH
        )


def remote(src, dst, sems, slot, device):
    return pltpu.make_async_remote_copy(
        src_ref=src,
        dst_ref=dst,
        send_sem=sems.at[0, slot],
        recv_sem=sems.at[1, slot],
        device_id=device,
        device_id_type=pl.DeviceIdType.MESH,
    )


def fused_kernel(
    ranges,
    offsets_ref,
    wtoken_ref,
    padding_ref,
    act_hbm,
    grad_hbm,
    pair_hbm,
    token_ref,
    wq_ref,
    wk_ref,
    wv_ref,
    wg_ref,
    wo_ref,
    wpair_ref,
    ga_hbm,
    pair_out_hbm,
    weights_hbm,
    pair_weight_ref,
    token_weight_ref,
    act_ref,
    grad_ref,
    pair_ref,
    before_ref,
    after_ref,
    code_scr,
    code_before,
    code_after,
    k_scr,
    v_scr,
    q_scr,
    da_scr,
    gate_scr,
    gyg_scr,
    dqg_scr,
    gated_scr,
    dk_scr,
    dv_scr,
    pw_scr,
    tok_scr,
    wpair_scr,
    key_code_scr,
    query_code_scr,
    mine_ref,
    theirs_ref,
    got,
    from_lower,
    from_upper,
    sums_ref,
    got_half,
    part_b,
    slots,
    total_ref,
    starts_ref,
    load_sems,
    store_sems,
    halo_sems,
    edge_sems,
    core_sems,
    scatter_sems,
    gather_sems,
):
    me = lax.axis_index("atoms")
    core = lax.axis_index("samples")
    other = 1 - core
    samples, atoms, channels = act_ref.shape
    windows = pair_ref.shape[0]
    rows = atoms // windows
    span = before_ref.shape[1]
    wide = atoms + 2 * span
    pair_channels = wpair_ref.shape[1]
    heads = wpair_ref.shape[0]
    head_dim = channels // heads
    scale = 1.0 / math.sqrt(head_dim)
    stack = heads * rows
    half_rows = rows // 2
    chunk = part_b.shape[1]
    half = ranges * chunk
    unroll = math.gcd(4, samples)
    has_lower, has_upper = me > 0, me < ranges - 1
    lower, upper, peer = {"atoms": me - 1}, {"atoms": me + 1}, {"samples": other}
    everyone = [{"atoms": lax.rem(me + d, ranges)} for d in range(1, ranges)]

    barrier = pltpu.get_barrier_semaphore()
    greet(barrier, [peer] + everyone)
    load_act = pltpu.make_async_copy(act_hbm, act_ref, load_sems.at[0])
    load_grad = pltpu.make_async_copy(grad_hbm, grad_ref, load_sems.at[1])
    load_pair = pltpu.make_async_copy(pair_hbm, pair_ref, load_sems.at[2])
    load_act.start()
    load_grad.start()
    load_pair.start()

    code_rows = atoms // span
    live_end = atoms - padding_ref[0]
    lane_at = lax.broadcasted_iota(jnp.int32, (1, span), 1)
    for r in range(code_rows):
        code_scr[r] = jnp.where(lane_at + r * span < live_end, token_ref[r : r + 1, :] + 1, 0)

    pl.semaphore_wait(barrier, ranges)
    halo_up = [
        remote(act_hbm.at[:, pl.ds(atoms - span, span)], before_ref, halo_sems, 0, upper),
        remote(code_scr.at[code_rows - 1], code_before, halo_sems, 1, upper),
    ]
    halo_down = [
        remote(act_hbm.at[:, pl.ds(0, span)], after_ref, halo_sems, 2, lower),
        remote(code_scr.at[0], code_after, halo_sems, 3, lower),
    ]

    @pl.when(has_upper)
    def _():
        for copy in halo_up:
            copy.start()

    @pl.when(has_lower)
    def _():
        for copy in halo_down:
            copy.start()

    @pl.when(jnp.logical_not(has_lower))
    def _():
        before_ref[...] = jnp.zeros_like(before_ref)
        code_before[...] = jnp.zeros_like(code_before)

    @pl.when(jnp.logical_not(has_upper))
    def _():
        after_ref[...] = jnp.zeros_like(after_ref)
        code_after[...] = jnp.zeros_like(code_after)

    def code_column(first, row):
        column = jnp.broadcast_to(row.astype(F32), (stack, span)).T
        key_code_scr[first : first + span, :] = column

    lane_row = lax.broadcasted_iota(jnp.int32, (pair_channels, stack), 1) % rows
    lane_head = lax.broadcasted_iota(jnp.int32, (pair_channels, stack), 1) // rows
    wpair_values = wpair_ref[...].astype(F32).T
    wpair_rows = jnp.zeros((pair_channels, stack), F32)
    wtoken_row = jnp.zeros((1, stack), F32)
    for h in range(heads):
        wpair_rows = jnp.where(lane_head == h, wpair_values[:, h : h + 1], wpair_rows)
        wtoken_row = jnp.where(lane_head[0:1] == h, wtoken_ref[h], wtoken_row)
    for i in range(rows):
        wpair_scr[i * pair_channels : (i + 1) * pair_channels, :] = jnp.where(
            lane_row == i, wpair_rows, 0.0
        ).astype(BF16)
    for r in range(code_rows):
        code_column(span + r * span, code_scr[r])
        tokens = (token_ref[r : r + 1, :] + 1).astype(F32)
        for u in range(span // rows):
            piece = tokens[:, u * rows : (u + 1) * rows]
            query_code_scr[r * (span // rows) + u] = jnp.concatenate([piece] * heads, axis=1)
    pw_scr[...] = jnp.zeros_like(pw_scr)
    tok_scr[...] = jnp.zeros_like(tok_scr)
    sums_ref[...] = jnp.zeros_like(sums_ref)
    anchor = me * atoms
    last_start = ranges * atoms - span
    for w in range(windows):
        starts_ref[w] = (
            jnp.clip(anchor + w * rows + offsets_ref[w], 0, last_start) - anchor + span
        )

    load_act.wait()
    load_grad.wait()
    slot = span + PAD

    def project(s, carry):
        own = act_ref[s]
        q_scr[s] = (nn(own, wq_ref[...]) * (scale * LOG2E)).astype(BF16)
        gate = jax.nn.sigmoid(nn(own, wg_ref[...]))
        gated_gy = nt(grad_ref[s], wo_ref[...]) * gate
        gate_scr[s] = gate
        da_scr[s] = gated_gy.astype(BF16)
        gyg_scr[s] = gated_gy * (1.0 - gate)
        k_scr[s, span : span + atoms, :] = nn(own, wk_ref[...]).astype(BF16).astype(F32)
        v_scr[s, span : span + atoms, :] = nn(own, wv_ref[...]).astype(BF16).astype(F32)
        blank = jnp.zeros((PAD, channels), F32)
        for w in range(windows + 1):
            dk_scr[s, w * slot : w * slot + PAD, :] = blank
            dv_scr[s, w * slot : w * slot + PAD, :] = blank
        return carry

    lax.fori_loop(0, samples, project, 0, unroll=unroll)
    load_pair.wait()

    row_head = lax.broadcasted_iota(jnp.int32, (stack, channels), 0) // rows
    column_head = lax.broadcasted_iota(jnp.int32, (stack, channels), 1) // head_dim
    head_mask = jnp.where(row_head == column_head, 1.0, 0.0).astype(BF16)
    lane = lax.broadcasted_iota(jnp.int32, (rows, channels), 1) // head_dim
    head_is = [lane == h for h in range(heads)]
    first_mine = core == 0

    def spread(x):
        return jnp.concatenate([x] * heads, axis=0) * head_mask

    def collect(x):
        out = x[0:rows]
        for h in range(1, heads):
            out = jnp.where(head_is[h], x[h * rows : (h + 1) * rows], out)
        return out

    def attend(block):
        ws = [block * TOGETHER + u for u in range(TOGETHER)]
        mine_rows = [pl.ds(pl.multiple_of(w * rows, rows), rows) for w in ws]
        key_rows = [pl.ds(starts_ref[w], span) for w in ws]
        slot_rows = [pl.ds(pl.multiple_of(w * slot + PAD, 8), span) for w in ws]
        sames, biases = [], []
        for u, w in enumerate(ws):
            key_code = key_code_scr[key_rows[u], :]
            same = key_code == query_code_scr[w]
            bias = (tn(pair_ref[w], wpair_scr[...]) + jnp.where(same, wtoken_row, 0.0)) * LOG2E
            biases.append(jnp.where(key_code > 0.0, bias, MASKED))
            sames.append(same)
        units = [(u, s) for u in range(TOGETHER) for s in range(samples)]
        keys = [k_scr[s, key_rows[u], :].astype(BF16) for u, s in units]
        values = [v_scr[s, key_rows[u], :].astype(BF16) for u, s in units]
        qm = [spread(q_scr[s, mine_rows[u], :]) for u, s in units]
        dam = [spread(da_scr[s, mine_rows[u], :]) for u, s in units]
        scores = [nt(k, q) + biases[u] for k, q, (u, s) in zip(keys, qm, units)]
        dprobs = [nt(v, d) for v, d in zip(values, dam)]
        tops = [jnp.max(x, axis=0, keepdims=True) for x in scores]
        exps = [jnp.exp2(x - t) for x, t in zip(scores, tops)]
        probs = [e * (1.0 / jnp.sum(e, axis=0, keepdims=True)) for e in exps]
        probs_b = [p.astype(BF16) for p in probs]
        for (u, s), p, d in zip(units, probs_b, dam):
            dv_scr[s, slot_rows[u], :] = nn(p, d)
        ds = [p * (d - jnp.sum(p * d, axis=0, keepdims=True)) for p, d in zip(probs, dprobs)]
        ds_b = [d.astype(BF16) for d in ds]
        for (u, s), d, q in zip(units, ds_b, qm):
            dk_scr[s, slot_rows[u], :] = nn(d, q)
        for (u, s), p, v in zip(units, probs_b, values):
            a = collect(tn(p, v))
            gated_scr[s, mine_rows[u], :] = (gate_scr[s, mine_rows[u], :] * a).astype(BF16)
            dqg_scr[s, mine_rows[u], channels:] = (gyg_scr[s, mine_rows[u], :] * a).astype(BF16)
        for (u, s), d, k in zip(units, ds_b, keys):
            dqg_scr[s, mine_rows[u], 0:channels] = (collect(tn(d, k)) * scale).astype(BF16)
        for u, w in enumerate(ws):
            of_window = [d for d, unit in zip(ds, units) if unit[0] == u]
            total = of_window[0]
            for d in of_window[1:]:
                total = total + d
            of_token = jnp.where(sames[u], total, 0.0)
            token_sum = of_token if u == 0 else token_sum + of_token
            pw_scr[...] += nn(pair_ref[w], total.astype(BF16))
            turned = total.T
            for h in range(heads):
                low = turned[h * rows : h * rows + half_rows]
                high = turned[h * rows + half_rows : (h + 1) * rows]
                at = slice(h * half_rows, (h + 1) * half_rows)
                mine_ref[w, at, :] = jnp.where(first_mine, low, high)
                theirs_ref[w, at, :] = jnp.where(first_mine, high, low).astype(BF16)
        tok_scr[...] += token_sum

    def gather_rows(s, b):
        dk, dv = None, None
        for w in range(max(0, b - 2 * span // rows), min(b, windows - 1) + 1):
            shift = jnp.clip(b * rows - starts_ref[w], -PAD, span)
            at = pl.ds(w * slot + PAD + shift, rows)
            k, v = dk_scr[s, at, :], dv_scr[s, at, :]
            dk, dv = (k, v) if dk is None else (dk + k, dv + v)
        return dk * (1.0 / LOG2E), dv

    halo_blocks = span // rows
    own_blocks = atoms // rows

    def project_halo(s, carry):
        for ref, first in ((before_ref, 0), (after_ref, span + atoms)):
            k_scr[s, first : first + span, :] = nn(ref[s], wk_ref[...]).astype(BF16).astype(F32)
            v_scr[s, first : first + span, :] = nn(ref[s], wv_ref[...]).astype(BF16).astype(F32)
        return carry

    edge_up = remote(after_ref, from_lower, edge_sems, 0, upper)
    edge_down = remote(before_ref, from_upper, edge_sems, 1, lower)

    def halo_gradient(s, first, ref):
        c = channels
        parts = [gather_rows(s, b) for b in range(first, first + halo_blocks)]
        dkv = jnp.concatenate(
            [jnp.concatenate([p[i] for p in parts], axis=0).astype(BF16) for i in (0, 1)],
            axis=1,
        )
        weights = jnp.concatenate([wk_ref[...], wv_ref[...]], axis=1)
        from_kv = tn(ref[s], dkv)
        sums_ref[c : 2 * c, :] += from_kv[:, 0:c]
        sums_ref[2 * c : 3 * c, :] += from_kv[:, c:]
        ref[s] = nt(dkv, weights).astype(BF16)

    def lower_gradient(s, carry):
        halo_gradient(s, 0, before_ref)
        return carry

    def upper_gradient(s, carry):
        halo_gradient(s, halo_blocks + own_blocks, after_ref)
        return carry

    blocks = windows // TOGETHER
    early = blocks - 2

    def step(it, carry):
        @pl.when(it == early)
        def _():
            @pl.when(has_upper)
            def _():
                for copy in halo_down:
                    copy.wait_recv()

            @pl.when(has_lower)
            def _():
                for copy in halo_up:
                    copy.wait_recv()

            code_column(0, code_before[...])
            code_column(span + atoms, code_after[...])
            lax.fori_loop(0, samples, project_halo, 0, unroll=unroll)

        @pl.when(it == early + 1)
        def _():
            lax.fori_loop(0, samples, lower_gradient, 0, unroll=unroll)

            @pl.when(has_lower)
            def _():
                edge_down.start()

        block = jnp.where(
            it < early,
            it + 1,
            jnp.where(it == early, 0, blocks - 1),
        )
        attend(block)
        return carry

    lax.fori_loop(0, blocks, step, 0)
    pair_copy = remote(theirs_ref, got, core_sems, 1, peer)
    pair_copy.start()
    lax.fori_loop(0, samples, upper_gradient, 0, unroll=unroll)

    @pl.when(has_upper)
    def _():
        edge_up.start()

    shape = pw_scr.shape
    at_row = lax.broadcasted_iota(jnp.int32, shape, 0) // pair_channels
    at_col = lax.broadcasted_iota(jnp.int32, shape, 1) % rows
    diagonal = jnp.where(at_row == at_col, pw_scr[...], 0.0)
    by_channel = jnp.sum(diagonal.reshape(rows, pair_channels, stack), axis=0)
    by_channel = jnp.concatenate(
        [by_channel, jnp.zeros((channels - pair_channels, stack), F32)], axis=0
    )
    by_head = jnp.sum(by_channel.T.reshape(heads, rows, channels), axis=1)
    token_row = jnp.sum(tok_scr[...], axis=0, keepdims=True)
    lanes = lax.broadcasted_iota(jnp.int32, (1, stack), 1)
    by_token = jnp.zeros((1, stack), F32)
    for h in range(heads):
        one = jnp.sum(jnp.where(lanes // rows == h, token_row, 0.0), axis=1, keepdims=True)
        by_token = jnp.where(lanes == h, one, by_token)
    base = 5 * channels
    small_rows = 8 * pl.cdiv(heads + 1, 8)
    sums_ref[base : base + heads, :] = by_head
    sums_ref[base + heads : base + heads + 1, :] = by_token

    def weight_gradients(s, carry):
        for b in range(halo_blocks, halo_blocks + own_blocks):
            dk, dv = gather_rows(s, b)
            k_scr[s, b * rows : (b + 1) * rows, :] = dk
            v_scr[s, b * rows : (b + 1) * rows, :] = dv
        c = channels
        own = slice(span, span + atoms)
        grads = jnp.concatenate(
            [
                dqg_scr[s, :, 0:c],
                k_scr[s, own, :].astype(BF16),
                v_scr[s, own, :].astype(BF16),
                dqg_scr[s, :, c:],
            ],
            axis=1,
        )
        sums = tn(act_ref[s], grads)
        for n in range(4):
            sums_ref[n * c : (n + 1) * c, :] += sums[:, n * c : (n + 1) * c]
        sums_ref[4 * c : 5 * c, :] += tn(gated_scr[s], grad_ref[s])
        return carry

    lax.fori_loop(0, samples, weight_gradients, 0, unroll=unroll)
    half_copy = remote(
        sums_ref.at[pl.ds(pl.multiple_of(other * half, 8), half)], got_half, core_sems, 0, peer
    )
    half_copy.start()

    inner = slice(span, atoms - span)

    def own_gradient(s, carry):
        own = slice(span, span + atoms)
        dq = dqg_scr[s, :, 0:channels]
        dg = dqg_scr[s, :, channels:]
        grads = jnp.concatenate(
            [dq, k_scr[s, own, :].astype(BF16), v_scr[s, own, :].astype(BF16), dg], axis=1
        )
        weights = jnp.concatenate([wq_ref[...], wk_ref[...], wv_ref[...], wg_ref[...]], axis=1)
        ga = nt(grads, weights)
        dk_scr[s, 0:span, :] = ga[0:span]
        dk_scr[s, span : 2 * span, :] = ga[atoms - span :]
        q_scr[s, inner, :] = ga[inner].astype(BF16)
        return carry

    lax.fori_loop(0, 2, own_gradient, 0)
    half_copy.wait_recv()
    own_half = pl.ds(pl.multiple_of(core * half, 16), half)
    small = base % half
    got_half[...] += sums_ref[own_half, :]
    rest = got_half[small : small + small_rows, :]
    rest = rest - rest.astype(BF16).astype(F32)
    low_rows = slice(small + small_rows, small + 2 * small_rows)
    got_half[low_rows, :] = jnp.where(core == base // half, rest, got_half[low_rows, :])
    part_b[...] = got_half[...].reshape(part_b.shape).astype(BF16)
    scatter = []
    for d in range(1, ranges):
        target = lax.rem(me + d, ranges)
        copy = remote(part_b.at[target], slots.at[d - 1], scatter_sems, d - 1, everyone[d - 1])
        copy.start()
        scatter.append(copy)
    lax.fori_loop(2, samples, own_gradient, 0, unroll=math.gcd(3, samples - 2))

    lane_out = lax.broadcasted_iota(jnp.int32, (pair_channels, heads * half_rows), 1)
    spread_rows = jnp.zeros((pair_channels, heads * half_rows), F32)
    for h in range(heads):
        spread_rows = jnp.where(lane_out // half_rows == h, wpair_values[:, h : h + 1], spread_rows)
    weight = jnp.concatenate(
        [
            jnp.where(lane_out % half_rows == i, spread_rows, 0.0).astype(BF16)
            for i in range(half_rows)
        ],
        axis=0,
    )
    for copy in scatter:
        copy.wait_recv()
    chunk_total = got_half[pl.ds(pl.multiple_of(me * chunk, 8), chunk), :]
    for d in range(1, ranges):
        chunk_total = chunk_total + slots[d - 1].astype(F32)
    place = pl.ds(pl.multiple_of(core * half + me * chunk, 16), chunk)
    total_ref[place, :] = chunk_total.astype(BF16)
    gather = []
    for d in range(1, ranges):
        copy = remote(
            total_ref.at[place], total_ref.at[place], gather_sems, d - 1, everyone[d - 1]
        )
        copy.start()
        gather.append(copy)

    pair_copy.wait_recv()
    out_rows = half_rows * pair_channels

    def pair_gradient(w, carry):
        both = mine_ref[w] + got[w].astype(F32)
        high = both.astype(BF16)
        low = (both - high.astype(F32)).astype(BF16)
        pair_ref[w, 0:out_rows, :] = (nn(weight, high) + nn(weight, low)).astype(BF16)
        return carry

    lax.fori_loop(0, windows, pair_gradient, 0, unroll=math.gcd(5, windows))
    store_pair = pltpu.make_async_copy(
        pair_ref.at[:, pl.ds(0, out_rows)], pair_out_hbm, store_sems.at[0]
    )
    store_pair.start()

    for copy in gather:
        copy.wait_recv()
    last_copy = remote(
        total_ref.at[own_half], total_ref.at[own_half], core_sems, 2, peer
    )
    last_copy.start()

    @pl.when(has_lower)
    def _():
        edge_down.wait_send()
        edge_up.wait_recv()

    @pl.when(has_upper)
    def _():
        edge_up.wait_send()
        edge_down.wait_recv()

    @pl.when(jnp.logical_not(has_lower))
    def _():
        from_lower[...] = jnp.zeros_like(from_lower)

    @pl.when(jnp.logical_not(has_upper))
    def _():
        from_upper[...] = jnp.zeros_like(from_upper)

    def add_edges(s, carry):
        q_scr[s, 0:span, :] = (dk_scr[s, 0:span, :] + from_lower[s].astype(F32)).astype(BF16)
        q_scr[s, atoms - span : atoms, :] = (
            dk_scr[s, span : 2 * span, :] + from_upper[s].astype(F32)
        ).astype(BF16)
        return carry

    lax.fori_loop(0, samples, add_edges, 0, unroll=unroll)
    store_act = pltpu.make_async_copy(q_scr, ga_hbm, store_sems.at[1])
    store_act.start()

    @pl.when(has_upper)
    def _():
        for copy in halo_up:
            copy.wait_send()

    @pl.when(has_lower)
    def _():
        for copy in halo_down:
            copy.wait_send()

    half_copy.wait_send()
    pair_copy.wait_send()
    for copy in scatter + gather:
        copy.wait_send()
    last_copy.wait()
    sums_ref[0:base, :] = total_ref[0:base, :].astype(F32)
    store_weights = pltpu.make_async_copy(
        sums_ref.at[pl.ds(0, base)], weights_hbm, store_sems.at[2]
    )
    store_weights.start()
    tail = total_ref[base : base + 2 * small_rows, :].astype(F32)
    tail = tail[0:small_rows] + tail[small_rows:]
    pair_weight_ref[...] = tail[0:heads, 0:pair_channels]
    token_weight_ref[...] = tail[heads : heads + 1, 0:heads]
    store_weights.wait()
    store_pair.wait()
    store_act.wait()


def finish_kernel(*refs):
    ins, outs, held = refs[0:5], refs[5:10], refs[10:13]
    load_sems, store_sems = refs[13:15]
    small = [
        pltpu.make_async_copy(ins[n], outs[n], store_sems.at[n]) for n in range(3, len(ins))
    ]
    loads = [pltpu.make_async_copy(ins[n], held[n], load_sems.at[n]) for n in range(3)]
    stores = [pltpu.make_async_copy(held[n], outs[n], store_sems.at[n]) for n in range(3)]
    for copy in loads + small:
        copy.start()
    for load, store in zip(loads, stores):
        load.wait()
        store.start()
    for copy in stores + small:
        copy.wait()


def per_device(
    act,
    grad_out,
    pair,
    w_query,
    w_key,
    w_value,
    w_gate,
    w_out,
    w_pair,
    w_token,
    offsets,
    atom_token,
    padding,
):
    samples, atoms, channels = act.shape
    windows = offsets.shape[0]
    rows = atoms // windows
    pair_channels, heads = w_pair.shape
    span = pair.shape[-1]
    stack = heads * rows
    half = rows // 2
    ranges = lax.axis_size("atoms")
    wide = atoms + 2 * span
    vmem = pl.BlockSpec(memory_space=pltpu.VMEM)
    smem = pl.BlockSpec(memory_space=pltpu.SMEM)
    anywhere = pl.BlockSpec(memory_space=pl.ANY)
    small_rows = 8 * pl.cdiv(heads + 1, 8)
    chunk = 16 * pl.cdiv(5 * channels + 2 * small_rows, 32 * ranges)
    sum_rows = 2 * ranges * chunk

    def kernel(*refs):
        fused_kernel(ranges, *refs)

    edge = pltpu.VMEM((samples, span, channels), BF16)
    slot_rows = windows * (span + PAD) + PAD
    results = pl.pallas_call(
        kernel,
        out_shape=(
            jax.ShapeDtypeStruct((samples, atoms, channels), BF16),
            jax.ShapeDtypeStruct((windows, half * pair_channels, span), BF16),
            jax.ShapeDtypeStruct((5 * channels, channels), F32),
            jax.ShapeDtypeStruct((heads, pair_channels), F32),
            jax.ShapeDtypeStruct((1, heads), F32),
        ),
        in_specs=[smem] * 3 + [anywhere] * 3 + [vmem] * 7,
        out_specs=(anywhere, anywhere, anywhere, vmem, vmem),
        scratch_shapes=[
            pltpu.VMEM((samples, atoms, channels), BF16),
            pltpu.VMEM((samples, atoms, channels), BF16),
            pltpu.VMEM((windows, rows * pair_channels, span), BF16),
            edge,
            edge,
            pltpu.VMEM((atoms // span, 1, span), jnp.int32),
            pltpu.VMEM((1, span), jnp.int32),
            pltpu.VMEM((1, span), jnp.int32),
            pltpu.VMEM((samples, wide, channels), F32),
            pltpu.VMEM((samples, wide, channels), F32),
            pltpu.VMEM((samples, atoms, channels), BF16),
            pltpu.VMEM((samples, atoms, channels), BF16),
            pltpu.VMEM((samples, atoms, channels), F32),
            pltpu.VMEM((samples, atoms, channels), F32),
            pltpu.VMEM((samples, atoms, 2 * channels), BF16),
            pltpu.VMEM((samples, atoms, channels), BF16),
            pltpu.VMEM((samples, slot_rows, channels), F32),
            pltpu.VMEM((samples, slot_rows, channels), F32),
            pltpu.VMEM((rows * pair_channels, stack), F32),
            pltpu.VMEM((span, stack), F32),
            pltpu.VMEM((rows * pair_channels, stack), BF16),
            pltpu.VMEM((wide, stack), F32),
            pltpu.VMEM((windows, 1, stack), F32),
            pltpu.VMEM((windows, heads * half, span), F32),
            pltpu.VMEM((windows, heads * half, span), BF16),
            pltpu.VMEM((windows, heads * half, span), BF16),
            edge,
            edge,
            pltpu.VMEM((sum_rows, channels), F32),
            pltpu.VMEM((ranges * chunk, channels), F32),
            pltpu.VMEM((ranges, chunk, channels), BF16),
            pltpu.VMEM((ranges - 1, chunk, channels), BF16),
            pltpu.VMEM((sum_rows, channels), BF16),
            pltpu.SMEM((windows,), jnp.int32),
            pltpu.SemaphoreType.DMA((3,)),
            pltpu.SemaphoreType.DMA((3,)),
            pltpu.SemaphoreType.DMA((2, 4)),
            pltpu.SemaphoreType.DMA((2, 2)),
            pltpu.SemaphoreType.DMA((2, 3)),
            pltpu.SemaphoreType.DMA((2, ranges - 1)),
            pltpu.SemaphoreType.DMA((2, ranges - 1)),
        ],
        compiler_params=pltpu.CompilerParams(
            collective_id=0, has_side_effects=True, vmem_limit_bytes=63 * 1024 * 1024
        ),
        name="fused",
    )(
        offsets,
        w_token,
        padding,
        act,
        grad_out,
        pair.reshape(windows, rows * pair_channels, span),
        atom_token.reshape(atoms // span, span),
        w_query,
        w_key,
        w_value,
        w_gate,
        w_out,
        w_pair.T,
    )

    grad_act, grad_pair, weights, pair_weight, token_weight = pl.pallas_call(
        finish_kernel,
        out_shape=tuple(jax.ShapeDtypeStruct(r.shape, r.dtype) for r in results),
        in_specs=[anywhere] * 5,
        out_specs=(anywhere,) * 5,
        scratch_shapes=[pltpu.VMEM(r.shape, r.dtype) for r in results[:3]]
        + [pltpu.SemaphoreType.DMA((3,)), pltpu.SemaphoreType.DMA((5,))],
        name="finish",
    )(*results)

    grad_weights = weights.reshape(5, channels, channels)
    grad_pair_weight = pair_weight.T
    grad_token_weight = token_weight.reshape(heads)
    grad_pair = grad_pair.reshape(windows, half, pair_channels, span)
    return (grad_act, grad_pair, grad_weights, grad_pair_weight, grad_token_weight)


def solution(mesh):
    in_specs = (
        P("samples", ("groups", "atoms"), None),
        P("samples", ("groups", "atoms"), None),
        P(("groups", "atoms"), None, None, None),
        P(),
        P(),
        P(),
        P(),
        P(),
        P(),
        P(),
        P(("groups", "atoms")),
        P(("groups", "atoms")),
        P(("groups", "atoms")),
    )
    out_specs = (
        P("samples", ("groups", "atoms"), None),
        P(("groups", "atoms"), "samples", None, None),
        P("groups", None, None),
        P("groups", None),
        P("groups"),
    )
    return jax.shard_map(
        per_device, mesh=mesh, in_specs=in_specs, out_specs=out_specs, check_vma=False
    )
```
